128 devices in a mesh: clip: 4 (over y_hi, core), frame: 32 (over z, x, y_lo).
Axes of the slice: x: 4, y: 4 (y_hi: 2, y_lo: 2; y = y_hi * 2 + y_lo), z: 4, core: 2. Of those that a mesh axis runs over, the one named last changes fastest.
Arguments:
- clips_in: bfloat16 [4, 64, 32, 32, 320], P('clip', 'frame'), may hold values from -6 to 6
- cotangent: bfloat16 [4, 64, 32, 32, 320], P('clip', 'frame'), may hold values from -0.0234375 to 0.0234375
- spatial_weight: bfloat16 [3, 3, 320, 320], replicated, may hold values from -0.109375 to 0.109375
- temporal_weight: bfloat16 [2, 3, 320, 320], replicated, may hold values from -0.1875 to 0.1875
Outputs:
- block_out: bfloat16 [4, 64, 32, 32, 320], P('clip', 'frame')
- grad_spatial: float32 [320, 3, 3, 320], P('frame', None, None, 'clip')
- grad_temporal: float32 [320, 2, 3, 320], P('frame', None, None, 'clip')
The draws below stay inside these ranges and needn't reach their ends.
All inputs are finite; a program needn't handle non-finite values.
Results may differ from the reference program's by a relative error of at most 0.0064.
Values may be sent and summed in bfloat16 or wider, within the bound.
No kernel may reach another device: no remote copies, remote signals or barrier semaphores. Data moves between devices by JAX's collectives and lax.ppermute only.
A program may use at most 128 MiB of HBM per device.

```python
import jax
import jax.numpy as jnp
from jax import lax

C = 320
H = 32
W = 32
LAYERS = 2
F = 64
CLIPS = 4


def with_spikes(values, key, source, target, shards_of, factor):
    owner, partner = [(jnp.arange(values.shape[axis_at]) // (values.shape[axis_at] // shards_of)).reshape([-1 if axis == axis_at else 1 for axis in range(values.ndim)]) for axis_at in (source, target)]
    chosen = jax.random.permutation(key, shards_of)[partner]
    strong = (owner == chosen) | (owner == (partner + shards_of // 2) % shards_of)
    return jnp.where(strong, factor * values, values)


def block_scale(own_key, shape, shards, smallest, high):
    level = 1.0
    for axis_at, parts in shards:
        steps = jax.random.uniform(jax.random.fold_in(jax.random.fold_in(own_key, 6), axis_at), (parts,), jnp.float32, smallest / len(shards), high / len(shards))
        level = level * jnp.repeat(jnp.exp(steps), shape[axis_at] // parts).reshape((-1,) + (1,) * (len(shape) - 1 - axis_at))
    return level


def normal_values(stream_key, shape, deviation, bound, split=(), held_as=jnp.bfloat16):
    level = block_scale(stream_key, shape, split, -0.22, 0.18) if split else 1.0
    entries = jax.random.normal(stream_key, shape, jnp.float32) * deviation * level
    return jnp.minimum(jnp.maximum(entries, -bound), bound).astype(held_as)


def gaussian_with(own_key, shape, spread, limit, cuts, heavy, kind=jnp.bfloat16):
    array = spread * jax.random.normal(own_key, shape, jnp.float32)
    if cuts:
        array = array * block_scale(own_key, shape, cuts, -0.22, 0.18)
    return jnp.clip(with_spikes(array, jax.random.fold_in(own_key, 3), *heavy), -limit, limit).astype(kind)


def setup_inputs(seed: int = 0) -> dict:
    key_of = jax.random.split(jax.random.key(seed), 5)
    clips_in = normal_values(key_of[0], (CLIPS, F, H, W, C), 1.0, 6.0, ((0, 4), (1, 32)))
    cotangent = gaussian_with(key_of[1], (CLIPS, F, H, W, C), (1.0 / (CLIPS * F * H * W) ** 0.5), 0.0234375, ((0, 4), (1, 32)), (1, 4, 32, 2.75))
    spatial_weight = normal_values(key_of[2], (3, 3, C, C), (9 * C) ** -0.5, 0.109375)
    temporal_weight = normal_values(key_of[3], (LAYERS, 3, C, C), (3 * C) ** -0.5, 0.1875)
    return {"clips_in": clips_in, "cotangent": cotangent, "spatial_weight": spatial_weight, "temporal_weight": temporal_weight}


def spatial_conv(latent, kernel):
    width = latent.shape[4]
    rows = latent.shape[2]
    cols = latent.shape[3]
    padded = jnp.pad(latent, ((0, 0), (0, 0), (1, 1), (1, 1), (0, 0)))
    total = jnp.zeros((latent.size // width, kernel.shape[3]), jnp.float32)
    for row_off in range(3):
        for col_off in range(3):
            window = padded[:, :, row_off:row_off + rows, col_off:col_off + cols, :].reshape(-1, width)
            total = total + jnp.dot(window, kernel[row_off, col_off], preferred_element_type=jnp.float32)
    return total.reshape(latent.shape)

def spatial_grad(latent, upstream):
    width = latent.shape[4]
    rows = latent.shape[2]
    cols = latent.shape[3]
    padded = jnp.pad(latent, ((0, 0), (0, 0), (1, 1), (1, 1), (0, 0)))
    flat_up = upstream.reshape(-1, width)
    result = []
    for row_off in range(3):
        line = []
        for col_off in range(3):
            window = padded[:, :, row_off:row_off + rows, col_off:col_off + cols, :].reshape(-1, width)
            line.append(jnp.dot(window.T, flat_up, preferred_element_type=jnp.float32))
        result.append(jnp.stack(line))
    return jnp.stack(result)

def time_pad(tensor):
    return jnp.pad(tensor, ((0, 0), (1, 1), (0, 0), (0, 0), (0, 0)))

def one_clip(latent, upstream, spatial_weight, temporal_weight):
    width = latent.shape[4]
    summed = spatial_conv(latent, spatial_weight)
    state = (latent.astype(jnp.float32) + summed).astype(jnp.bfloat16)
    frames = state.shape[1]
    states = []
    acts = []
    for layer in range(LAYERS):
        states.append(state)
        active = jax.nn.silu(state.astype(jnp.float32)).astype(jnp.bfloat16)
        active_pad = time_pad(active)
        acts.append(active_pad)
        term = jnp.zeros((state.size // width, width), jnp.float32)
        for offset in range(3):
            term = term + jnp.dot(active_pad[:, offset:offset + frames].reshape(-1, width), temporal_weight[layer, offset], preferred_element_type=jnp.float32)
        state = (state.astype(jnp.float32) + term.reshape(state.shape)).astype(jnp.bfloat16)
    output = state
    grad = upstream
    grads = [None] * LAYERS
    for layer in reversed(range(LAYERS)):
        active_pad = acts[layer]
        flat_grad = grad.reshape(-1, width)
        grads[layer] = jnp.stack([jnp.dot(active_pad[:, offset:offset + frames].reshape(-1, width).T, flat_grad, preferred_element_type=jnp.float32) for offset in range(3)])
        grad_pad = time_pad(grad)
        carried = jnp.zeros((grad.size // width, width), jnp.float32)
        for offset in range(3):
            carried = carried + jnp.dot(grad_pad[:, 2 - offset:2 - offset + frames].reshape(-1, width), temporal_weight[layer, offset].T, preferred_element_type=jnp.float32)
        before = states[layer].astype(jnp.float32)
        logistic = jax.nn.sigmoid(before)
        slope = logistic * (1.0 + before * (1.0 - logistic))
        grad = (grad.astype(jnp.float32) + carried.reshape(grad.shape) * slope).astype(jnp.bfloat16)
    return (output, spatial_grad(latent, grad), jnp.stack(grads))

def reference(clips_in, cotangent, spatial_weight, temporal_weight):

    def runner(pair):
        return one_clip(pair[0][None], pair[1][None], spatial_weight, temporal_weight)
    outputs, spatial_parts, temporal_parts = lax.map(runner, (clips_in, cotangent))
    block_out = outputs[:, 0]
    grad_spatial = jnp.transpose(lax.optimization_barrier(jnp.sum(spatial_parts, axis=0)), (3, 0, 1, 2))
    grad_temporal = jnp.transpose(lax.optimization_barrier(jnp.sum(temporal_parts, axis=0)), (3, 0, 1, 2))
    return (block_out, grad_spatial, grad_temporal)
```

```python
import jax
import jax.numpy as jnp
from jax import lax
from jax.sharding import PartitionSpec as P


def spatial_conv(latent, kernel):
    width = latent.shape[4]
    rows = latent.shape[2]
    cols = latent.shape[3]
    padded = jnp.pad(latent, ((0, 0), (0, 0), (1, 1), (1, 1), (0, 0)))
    total = jnp.zeros((latent.size // width, kernel.shape[3]), jnp.float32)
    for row_off in range(3):
        for col_off in range(3):
            window = padded[:, :, row_off : row_off + rows, col_off : col_off + cols, :].reshape(
                -1, width
            )
            total = total + jnp.dot(
                window, kernel[row_off, col_off], preferred_element_type=jnp.float32
            )
    return total.reshape(latent.shape)


def spatial_grad(latent, upstream):
    width = latent.shape[4]
    rows = latent.shape[2]
    cols = latent.shape[3]
    padded = jnp.pad(latent, ((0, 0), (0, 0), (1, 1), (1, 1), (0, 0)))
    flat_up = upstream.reshape(-1, width)
    pieces = []
    for row_off in range(3):
        for col_off in range(3):
            window = padded[:, :, row_off : row_off + rows, col_off : col_off + cols, :].reshape(
                -1, width
            )
            pieces.append(jnp.dot(flat_up.T, window, preferred_element_type=jnp.float32))
    stacked = jnp.stack(pieces, axis=1)
    return stacked.reshape(stacked.shape[0], 3, 3, stacked.shape[2])


def time_pad(tensor):
    return jnp.pad(tensor, ((0, 0), (1, 1), (0, 0), (0, 0), (0, 0)))


def temporal_forward(state, temporal_weight):
    width = state.shape[4]
    frames = state.shape[1]
    states = []
    acts = []
    for layer in range(temporal_weight.shape[0]):
        states.append(state)
        active = jax.nn.silu(state.astype(jnp.float32)).astype(jnp.bfloat16)
        active_pad = time_pad(active)
        acts.append(active_pad)
        term = jnp.zeros((state.size // width, width), jnp.float32)
        for offset in range(3):
            term = term + jnp.dot(
                active_pad[:, offset : offset + frames].reshape(-1, width),
                temporal_weight[layer, offset],
                preferred_element_type=jnp.float32,
            )
        state = (state.astype(jnp.float32) + term.reshape(state.shape)).astype(jnp.bfloat16)
    return (state, states, acts)


def temporal_backward(upstream, states, acts, temporal_weight):
    width = upstream.shape[4]
    frames = upstream.shape[1]
    grad = upstream
    count = temporal_weight.shape[0]
    grads = [None] * count
    for layer in reversed(range(count)):
        active_pad = acts[layer]
        flat_grad = grad.reshape(-1, width)
        grads[layer] = jnp.stack(
            [
                jnp.dot(
                    flat_grad.T,
                    active_pad[:, offset : offset + frames].reshape(-1, width),
                    preferred_element_type=jnp.float32,
                )
                for offset in range(3)
            ],
            axis=1,
        )
        grad_pad = time_pad(grad)
        carried = jnp.zeros((grad.size // width, width), jnp.float32)
        for offset in range(3):
            carried = carried + jnp.dot(
                grad_pad[:, 2 - offset : 2 - offset + frames].reshape(-1, width),
                temporal_weight[layer, offset].T,
                preferred_element_type=jnp.float32,
            )
        before = states[layer].astype(jnp.float32)
        logistic = jax.nn.sigmoid(before)
        slope = logistic * (1.0 + before * (1.0 - logistic))
        grad = (grad.astype(jnp.float32) + carried.reshape(grad.shape) * slope).astype(jnp.bfloat16)
    return (grad, jnp.stack(grads, axis=1))


def reduce_scatter(partial):
    out, first, second, inner = partial.shape
    owners, clips = lax.axis_size("frame"), lax.axis_size("clip")
    rows, cols = out // owners, inner // clips
    block = rows * first * second * cols
    sent = partial.astype(jnp.bfloat16).reshape(owners, rows, first, second, clips, cols)
    sent = sent.transpose(0, 4, 1, 2, 3, 5).reshape(owners * clips, 16, block // 16)
    got = lax.all_to_all(sent, ("frame", "clip"), split_axis=0, concat_axis=0, tiled=True)
    summed = jnp.sum(got.astype(jnp.float32), axis=0)
    return summed.reshape(rows, first, second, cols)


def on_device(clips_in, cotangent, spatial_weight, temporal_weight):
    summed = spatial_conv(clips_in, spatial_weight)
    first = (clips_in.astype(jnp.float32) + summed).astype(jnp.bfloat16)
    hidden, upstream = (
        lax.all_to_all(first, "frame", split_axis=2, concat_axis=1, tiled=True),
        lax.all_to_all(cotangent, "frame", split_axis=2, concat_axis=1, tiled=True),
    )
    output, states, acts = temporal_forward(hidden, temporal_weight)
    grad_first, grad_temporal = temporal_backward(upstream, states, acts, temporal_weight)
    output, grad_first = (
        lax.all_to_all(output, "frame", split_axis=1, concat_axis=2, tiled=True),
        lax.all_to_all(grad_first, "frame", split_axis=1, concat_axis=2, tiled=True),
    )
    grad_spatial = spatial_grad(clips_in, grad_first)
    grad_temporal = reduce_scatter(grad_temporal)
    grad_spatial = reduce_scatter(grad_spatial)
    return (output, grad_spatial, grad_temporal)


def solution(mesh):
    placed = (P("clip", "frame", None, None, None), P("clip", "frame", None, None, None), P(), P())
    return jax.shard_map(
        on_device,
        mesh=mesh,
        in_specs=placed,
        out_specs=(
            P("clip", "frame", None, None, None),
            P("frame", None, None, "clip"),
            P("frame", None, None, "clip"),
        ),
        check_vma=False,
    )
```

```python
import functools

import jax
import jax.numpy as jnp
from jax import lax
from jax.experimental import pallas as pl
from jax.experimental.pallas import tpu as pltpu
from jax.sharding import PartitionSpec as P


BF = jnp.bfloat16
F32 = jnp.float32
C = 320
COLS = 32
ROWS = 16
PX = ROWS * COLS
TALL = PX + COLS
FULL = 2 * PX
VM = pl.BlockSpec(memory_space=pltpu.VMEM)
SM = pl.BlockSpec(memory_space=pltpu.SMEM)


def dot(a, b):
    return jnp.dot(a, b, preferred_element_type=F32)


def run(kernel, outs, args, scratch=(), flops=0):
    nbytes = sum(a.size * a.dtype.itemsize for a in args) + sum(
        functools.reduce(lambda m, n: m * n, s, 1) * jnp.dtype(d).itemsize for s, d in outs
    )
    return pl.pallas_call(
        kernel,
        out_shape=[jax.ShapeDtypeStruct(s, d) for s, d in outs],
        in_specs=[SM] + [VM] * (len(args) - 1),
        out_specs=[VM] * len(outs),
        scratch_shapes=list(scratch),
        cost_estimate=pl.CostEstimate(flops=flops, bytes_accessed=nbytes, transcendentals=0),
        name=kernel.__name__,
    )(*args)


def column_of(rows):
    return lax.broadcasted_iota(jnp.int32, (rows, 1), 0) % COLS


def right_by_one(v):
    return jnp.where(column_of(v.shape[0]) == 0, 0.0, pltpu.roll(v, 1, 0))


def left_by_one(v):
    return jnp.where(column_of(v.shape[0]) == COLS - 1, 0.0, pltpu.roll(v, v.shape[0] - 1, 0))


def sigmoid(v):
    return 1.0 / (1.0 + jnp.exp(-v))


def pad_rows(pad, rows, odd):
    pad[pl.ds(0, COLS), :] = jnp.zeros((COLS, C), BF)
    pad[pl.ds(TALL, COLS), :] = jnp.zeros((COLS, C), BF)
    pad[pl.ds(pl.multiple_of(COLS * (1 - odd), COLS), TALL), :] = rows


def convolve(pad, w):
    parts = []
    for j in range(3):
        acc = dot(pad[pl.ds(0, PX), :], w[j])
        acc = acc + dot(pad[pl.ds(COLS, PX), :], w[3 + j])
        acc = acc + dot(pad[pl.ds(2 * COLS, PX), :], w[6 + j])
        parts.append(acc)
    centre = pad[pl.ds(COLS, PX), :].astype(F32)
    total = right_by_one(parts[0]) + parts[1] + left_by_one(parts[2])
    return (centre + total).astype(BF)


def conv_own(at, x, w, out0, out1, pad):
    odd = at[0]
    start = pl.multiple_of((TALL - 2 * COLS) * odd, COLS)
    for q, out in enumerate((out0, out1)):
        frame = odd + q * (1 - 2 * odd)
        pad_rows(pad, x[frame, pl.ds(start, TALL), :], odd)
        out[...] = convolve(pad, w)


def conv_other(at, x, w, out, pad):
    pad_rows(pad, x[...], at[0])
    out[...] = convolve(pad, w)


def activate(refs, acts):
    for n, ref in enumerate(refs):
        v = ref[...].astype(F32)
        acts[n] = (v * sigmoid(v)).astype(BF)


def tap(k, odd):
    return k + odd * (2 - 2 * k)


def layer_one(at, left, s0, s1, s2, s3, right, w, acts, nxt, first, last):
    odd = at[0]
    activate((left, s0, s1, s2, s3, right), acts)
    for q, ref in enumerate((s0, s1, s2, s3)):
        term = dot(acts[q], w[tap(0, odd)]) + dot(acts[q + 1], w[tap(1, odd)])
        term = term + dot(acts[q + 2], w[tap(2, odd)])
        value = (ref[...].astype(F32) + term).astype(BF)
        nxt[q] = value
        if q == 0:
            first[...] = value
        if q == 3:
            last[...] = value


def layer_two(at, left, state, right, w, acts, own, sent):
    odd = at[0]
    activate((left, state.at[0], state.at[1], state.at[2], state.at[3], right), acts)
    for q in range(4):
        term = dot(acts[q], w[tap(0, odd)]) + dot(acts[q + 1], w[tap(1, odd)])
        term = term + dot(acts[q + 2], w[tap(2, odd)])
        value = (state[q].astype(F32) + term).astype(BF)
        if q < 2:
            own[q] = value
        else:
            sent[3 - q] = value


def carry(six, q, wt, odd):
    term = dot(six[q + 2][...], wt[tap(0, odd)]) + dot(six[q + 1][...], wt[tap(1, odd)])
    return term + dot(six[q][...], wt[tap(2, odd)])


def descend(back, carried, before):
    v = before.astype(F32)
    s = sigmoid(v)
    return (back.astype(F32) + carried * (s * (1.0 + v * (1.0 - s)))).astype(BF)


def cotangent_views(cot, other_inner, other_outer, odd):
    start = pl.multiple_of(PX * odd, PX)
    own = [cot.at[odd + q * (1 - 2 * odd), pl.ds(start, PX), :] for q in range(2)]
    return own + [other_inner, other_outer]


def back_one(at, left, cot, c2, c3, right, state, wt, back, first, last):
    odd = at[0]
    six = [left] + cotangent_views(cot, c2, c3, odd) + [right]
    for q in range(4):
        value = descend(six[q + 1][...], carry(six, q, wt, odd), state[q])
        back[q] = value
        if q == 0:
            first[...] = value
        if q == 3:
            last[...] = value


def temporal_grads(at, cot, c2, c3, acts2, back, acts1, kept, sent, flip):
    odd, core = at[0], at[1]
    views = cotangent_views(cot, c2, c3, odd)
    for layer, acts in ((0, acts1), (1, acts2)):
        for q in range(4):
            rows = back[q] if layer == 0 else views[q][...]
            flip[:, pl.ds(q * PX, PX)] = rows.T
        for k in range(3):
            total = jnp.zeros((C, C), F32)
            for q in range(4):
                total = total + dot(flip[:, pl.ds(q * PX, PX)], acts[q + k])
            value = total.astype(BF)

            @pl.when(core == layer)
            def _():
                kept[tap(k, odd)] = value

            @pl.when(core != layer)
            def _():
                sent[tap(k, odd)] = value


def back_zero(at, left, back, right, s0, s1, s2, s3, wt, x, x2, x3, kept, sent, pad, flip, terms):
    odd, core = at[0], at[1]
    six = [left] + [back.at[q] for q in range(4)] + [right]
    start = pl.multiple_of((TALL - 2 * COLS) * odd, COLS)
    for q, before in enumerate((s0, s1, s2, s3)):
        if q < 2:
            rows = x[odd + q * (1 - 2 * odd), pl.ds(start, TALL), :]
        else:
            rows = (x2 if q == 2 else x3)[...]
        pad_rows(pad.at[q], rows, odd)
        value = descend(back[q], carry(six, q, wt, odd), before[...])
        wide = value.astype(F32)
        flip[pl.ds(0, C), pl.ds(q * PX, PX)] = left_by_one(wide).astype(BF).T
        flip[pl.ds(C, C), pl.ds(q * PX, PX)] = value.T
        flip[pl.ds(2 * C, C), pl.ds(q * PX, PX)] = right_by_one(wide).astype(BF).T
    for i in range(3):
        total = jnp.zeros((3 * C, C), F32)
        for q in range(4):
            total = total + dot(flip[:, pl.ds(q * PX, PX)], pad[q, pl.ds(i * COLS, PX), :])
        for j in range(3):
            terms[3 * i + j] = total[j * C : (j + 1) * C].astype(BF)
    for n in range(5):
        kept[n] = terms[4 * core + n]
        sent[n] = terms[4 * (1 - core) + n]


def pack(at, kept, got, out, wide, rows, taps):
    owners = out.shape[0]
    for t in range(taps):
        rows[...] = kept[t].astype(F32) + got[t].astype(F32)
        for owner in range(owners):
            wide[owner, pl.ds(10 * t, 10), :] = rows[pl.ds(10 * owner, 10), :]
    for owner in range(owners):
        out[owner] = wide[owner].astype(BF)


def place(at, own, got, out):
    odd = at[0]
    for q in range(2):
        frame = odd + q * (1 - 2 * odd)
        out[frame, pl.ds(pl.multiple_of(PX * odd, PX), PX), :] = own[q]
        out[frame, pl.ds(pl.multiple_of(PX * (1 - odd), PX), PX), :] = got[q]


def after(value, *others):
    return lax.optimization_barrier((value, *others))[0]


def on_device(clips_in, cotangent, spatial_weight, temporal_weight):
    owners = lax.axis_size("frame")
    index = lax.axis_index("frame")
    odd = index % 2
    core = lax.axis_index("clip") % 2
    at = jnp.stack([odd, core]).astype(jnp.int32)
    swap = [(n, n ^ 1) for n in range(owners)]
    outer = [(n, n - 2 if n % 2 == 0 else n + 2) for n in range(owners)]
    outer = [(a, b) for a, b in outer if 0 <= b < owners]
    inner = [(n, n + 2 if n % 2 == 0 else n - 2) for n in range(owners)]
    inner = [(a, b) for a, b in inner if 0 <= b < owners]
    cores = [(0, 1), (1, 0), (2, 3), (3, 2)]
    send = functools.partial(lax.ppermute, axis_name="frame")

    x = clips_in.reshape(2, FULL, C)
    cot = cotangent.reshape(2, FULL, C)
    ws = spatial_weight.reshape(9, C, C)
    wt = jnp.swapaxes(temporal_weight, 2, 3)

    def cut(a, frame, start, size):
        return lax.dynamic_slice(a, (frame, start, 0), (1, size, C))[0]

    tall_start = (TALL - 2 * COLS) * (1 - odd)
    flops = 2 * PX * C * C

    x3 = send(cut(x, odd, tall_start, TALL), perm=swap)
    pads = [pltpu.VMEM((PX + 2 * COLS, C), BF)]
    one = ((PX, C), BF)
    four = ((4, PX, C), BF)
    six = ((6, PX, C), BF)
    s0, s1 = run(conv_own, [one, one], (at, x, ws), pads, 18 * flops)
    x2 = send(after(cut(x, 1 - odd, tall_start, TALL), s0), perm=swap)
    right = send(s0, perm=outer)
    cot_right = send(cut(cot, odd, PX * odd, PX), perm=outer)

    (s3,) = run(conv_other, [one], (at, x3, ws), pads, 9 * flops)
    left = send(s3, perm=inner)
    c3 = send(after(cut(cot, odd, PX * (1 - odd), PX), x3), perm=swap)
    (s2,) = run(conv_other, [one], (at, x2, ws), pads, 9 * flops)
    c2 = send(after(cut(cot, 1 - odd, PX * (1 - odd), PX), x2), perm=swap)
    cot_left = send(c3, perm=inner)

    acts1, state1, first, last = run(
        layer_one, [six, four, one, one], (at, left, s0, s1, s2, s3, right, temporal_weight[0]), (), 12 * flops
    )
    left1 = send(last, perm=inner)
    right1 = send(first, perm=outer)
    back1, first, last = run(
        back_one, [four, one, one], (at, cot_left, cot, c2, c3, cot_right, state1, wt[1]), (), 12 * flops
    )
    back_left = send(last, perm=inner)
    back_right = send(first, perm=outer)
    two = ((2, PX, C), BF)
    acts2, own, sent = run(
        layer_two, [six, two, two], (at, left1, state1, right1, temporal_weight[1]), (), 12 * flops
    )
    returned = send(sent, perm=swap)
    kept, sent = run(
        temporal_grads,
        [((3, C, C), BF)] * 2,
        (at, cot, c2, c3, acts2, back1, acts1),
        [pltpu.VMEM((C, 4 * PX), BF)],
        24 * flops,
    )
    temporal_terms = (kept, lax.ppermute(sent, "clip", cores))
    kept, sent = run(
        back_zero,
        [((5, C, C), BF)] * 2,
        (at, back_left, back1, back_right, s0, s1, s2, s3, wt[0], x, x2, x3),
        [
            pltpu.VMEM((4, PX + 2 * COLS, C), BF),
            pltpu.VMEM((3 * C, 4 * PX), BF),
            pltpu.VMEM((9, C, C), BF),
        ],
        48 * flops,
    )
    spatial_terms = (kept, lax.ppermute(sent, "clip", cores))

    def reduce_scatter(terms):
        kept, got = terms
        taps = kept.shape[0]
        rows = C // owners
        (packed,) = run(
            functools.wraps(pack)(functools.partial(pack, taps=taps)),
            [((owners, rows * taps, C), BF)],
            (at, kept, got),
            [pltpu.VMEM((owners, rows * taps, C), F32), pltpu.VMEM((C, C), F32)],
            1000,
        )
        parts = lax.all_to_all(packed, "frame", split_axis=0, concat_axis=0, tiled=True)
        summed = jnp.sum(parts.astype(F32), axis=0)
        clips = lax.axis_size("clip")
        split = summed.reshape(rows * taps, clips, C // clips).transpose(1, 0, 2)
        split = lax.all_to_all(split, "clip", split_axis=0, concat_axis=0, tiled=True)
        total = split[:2] + split[2:]
        return total.reshape(2, taps, rows, C // clips).transpose(0, 2, 1, 3)

    total = reduce_scatter(temporal_terms)
    grad_temporal = total.transpose(1, 0, 2, 3)
    total = reduce_scatter(spatial_terms)
    grad_spatial = jnp.concatenate([total[0], total[1, :, 1:]], axis=1)
    grad_spatial = grad_spatial.reshape(C // owners, 3, 3, grad_spatial.shape[-1])
    (out,) = run(place, [((2, FULL, C), BF)], (at, own, returned), (), 1000)
    return (out.reshape(clips_in.shape), grad_spatial, grad_temporal)


def solution(mesh):
    placed = (P("clip", "frame", None, None, None), P("clip", "frame", None, None, None), P(), P())
    return jax.shard_map(
        on_device,
        mesh=mesh,
        in_specs=placed,
        out_specs=(
            P("clip", "frame", None, None, None),
            P("frame", None, None, "clip"),
            P("frame", None, None, "clip"),
        ),
        check_vma=False,
    )
```

```python
import functools

import jax
import jax.numpy as jnp
from jax import lax
from jax.experimental import pallas as pl
from jax.experimental.pallas import tpu as pltpu
from jax.sharding import PartitionSpec as P


BF = jnp.bfloat16
F32 = jnp.float32
C = 320
COLS = 32
ROWS = 16
PX = ROWS * COLS
TALL = PX + COLS
FULL = 2 * PX
HEAD = 256
TAIL = C - HEAD
LIMIT = 24 * 1024 * 1024
VM = pl.BlockSpec(memory_space=pltpu.VMEM)
SM = pl.BlockSpec(memory_space=pltpu.SMEM)


def dot(a, b):
    return jnp.dot(a, b, preferred_element_type=F32)


def side(*parts):
    return jnp.concatenate(parts, axis=1)


def run(kernel, outs, args, scratch=(), flops=0):
    nbytes = sum(a.size * a.dtype.itemsize for a in args) + sum(
        functools.reduce(lambda m, n: m * n, s, 1) * jnp.dtype(d).itemsize for s, d in outs
    )
    return pl.pallas_call(
        kernel,
        out_shape=[jax.ShapeDtypeStruct(s, d) for s, d in outs],
        in_specs=[SM] + [VM] * (len(args) - 1),
        out_specs=[VM] * len(outs),
        scratch_shapes=list(scratch),
        cost_estimate=pl.CostEstimate(flops=flops, bytes_accessed=nbytes, transcendentals=0),
        compiler_params=pltpu.CompilerParams(vmem_limit_bytes=LIMIT),
    )(*args)


def column_of(rows):
    return lax.broadcasted_iota(jnp.int32, (rows, 1), 0) % COLS


def right_by_one(v):
    return jnp.where(column_of(v.shape[0]) == 0, 0.0, pltpu.roll(v, 1, 0))


def left_by_one(v):
    return jnp.where(column_of(v.shape[0]) == COLS - 1, 0.0, pltpu.roll(v, v.shape[0] - 1, 0))


def sigmoid(v):
    return 1.0 / (1.0 + jnp.exp(-v))


def pad_rows(pad, rows, odd):
    pad[pl.ds(0, COLS), :] = jnp.zeros((COLS, C), BF)
    pad[pl.ds(TALL, COLS), :] = jnp.zeros((COLS, C), BF)
    pad[pl.ds(pl.multiple_of(COLS * (1 - odd), COLS), TALL), :] = rows


def convolve(pad, tails, w, wn, wk, wr, out):
    tails[...] = side(*[pad[pl.ds(COLS * i, PX), pl.ds(HEAD, TAIL)] for i in range(3)])

    def heads(i):
        return pad[pl.ds(COLS * i, PX), pl.ds(0, HEAD)]

    parts = []
    for j in range(3):
        acc = dot(heads(0), w[j, pl.ds(0, HEAD), pl.ds(0, HEAD)])
        acc = acc + dot(heads(1), w[3 + j, pl.ds(0, HEAD), pl.ds(0, HEAD)])
        acc = acc + dot(heads(2), w[6 + j, pl.ds(0, HEAD), pl.ds(0, HEAD)])
        parts.append(acc + dot(tails[...], wk[j]))
    centre = pad[pl.ds(COLS, PX), pl.ds(0, HEAD)].astype(F32)
    total = right_by_one(parts[0]) + parts[1] + left_by_one(parts[2])
    out[:, pl.ds(0, HEAD)] = (centre + total).astype(BF)
    acc = dot(heads(0), wn[0]) + dot(heads(1), wn[1]) + dot(heads(2), wn[2])
    acc = acc + dot(tails[...], wr[...])
    total = right_by_one(acc[:, :TAIL]) + acc[:, TAIL : 2 * TAIL] + left_by_one(acc[:, 2 * TAIL :])
    centre = pad[pl.ds(COLS, PX), pl.ds(HEAD, TAIL)].astype(F32)
    out[:, pl.ds(HEAD, TAIL)] = (centre + total).astype(BF)


def conv_own(at, x, w, out0, out1, pad0, pad1, tails0, tails1, wn, wk, wr):
    odd = at[0]
    for i in range(3):
        wn[i] = side(*[w[3 * i + j, pl.ds(0, HEAD), pl.ds(HEAD, TAIL)] for j in range(3)])
        for j in range(3):
            wk[j, pl.ds(TAIL * i, TAIL), :] = w[3 * i + j, pl.ds(HEAD, TAIL), pl.ds(0, HEAD)]
        wr[pl.ds(TAIL * i, TAIL), :] = side(
            *[w[3 * i + j, pl.ds(HEAD, TAIL), pl.ds(HEAD, TAIL)] for j in range(3)]
        )
    start = pl.multiple_of((TALL - 2 * COLS) * odd, COLS)
    for q, (out, pad, tails) in enumerate(((out0, pad0, tails0), (out1, pad1, tails1))):
        frame = odd + q * (1 - 2 * odd)
        pad_rows(pad, x[frame, pl.ds(start, TALL), :], odd)
        convolve(pad, tails, w, wn, wk, wr, out)


def conv_other(at, x, w, wn, wk, wr, out, pad, tails):
    pad_rows(pad, x[...], at[0])
    convolve(pad, tails, w, wn, wk, wr, out)


def tap(k, odd):
    return k + odd * (2 - 2 * k)


def tail_rows(w, layer, odd, wk):
    for k in range(3):
        wk[pl.ds(TAIL * k, TAIL), :] = w[layer, tap(k, odd), pl.ds(HEAD, TAIL), :]


def three_taps(first, second, third, tails, w, layer, odd, wk):
    total = dot(first[:, pl.ds(0, HEAD)], w[layer, tap(0, odd), pl.ds(0, HEAD), :])
    total = total + dot(second[:, pl.ds(0, HEAD)], w[layer, tap(1, odd), pl.ds(0, HEAD), :])
    total = total + dot(third[:, pl.ds(0, HEAD)], w[layer, tap(2, odd), pl.ds(0, HEAD), :])
    return total + dot(tails, wk[...])


def ends(*refs):
    return side(*[ref[:, pl.ds(HEAD, TAIL)] for ref in refs])


def temporal(states, w, layer, odd, acts, tails, wk):
    tail_rows(w, layer, odd, wk)
    for n, ref in enumerate(states):
        v = ref[...].astype(F32)
        acts[n] = (v * sigmoid(v)).astype(BF)
    for q in range(4):
        three = [acts.at[q + k] for k in range(3)]
        last = ends(*three)
        tails[q] = last
        term = three_taps(*three, last, w, layer, odd, wk)
        yield (states[q + 1][...].astype(F32) + term).astype(BF)


def layer_one(at, left, s0, s1, s2, s3, right, w, acts, tails, nxt, first, last, wk):
    states = (left, s0, s1, s2, s3, right)
    for q, value in enumerate(temporal(states, w, 0, at[0], acts, tails, wk)):
        nxt[q] = value
        if q == 0:
            first[...] = value
        if q == 3:
            last[...] = value


def layer_two(at, left, state, right, w, acts, tails, own, sent, wk):
    states = (left, state.at[0], state.at[1], state.at[2], state.at[3], right)
    for q, value in enumerate(temporal(states, w, 1, at[0], acts, tails, wk)):
        if q < 2:
            own[q] = value
        else:
            sent[3 - q] = value


def descend(six, q, before, w, layer, odd, wk):
    three = (six[q + 2], six[q + 1], six[q])
    carried = three_taps(*three, ends(*three), w, layer, odd, wk)
    v = before.astype(F32)
    s = sigmoid(v)
    return (six[q + 1][...].astype(F32) + carried * (s * (1.0 + v * (1.0 - s)))).astype(BF)


def cotangent_views(cot, c2, c3, odd):
    start = pl.multiple_of(PX * odd, PX)
    own = [cot.at[odd + q * (1 - 2 * odd), pl.ds(start, PX), :] for q in range(2)]
    return own + [c2, c3]


def back_one(at, left, cot, c2, c3, right, state, w, back, first, last, wk):
    odd = at[0]
    tail_rows(w, 1, odd, wk)
    six = [left] + cotangent_views(cot, c2, c3, odd) + [right]
    for q in range(4):
        value = descend(six, q, state[q], w, 1, odd, wk)
        back[q] = value
        if q == 0:
            first[...] = value
        if q == 3:
            last[...] = value


def split_columns(value, blocks, index):
    width = blocks.shape[-1]
    for b in range(4):
        blocks[b, index] = value[:, b * width : (b + 1) * width]


def share(blocks, kept, sent, core):
    for half in range(2):
        kept[half] = blocks[2 * half + core]
        sent[half] = blocks[2 * half + 1 - core]


def temporal_grads(at, cot, c2, c3, acts2, tails2, back, acts1, tails1, kept, sent, flip, blocks):
    odd, core = at[0], at[1]
    views = cotangent_views(cot, c2, c3, odd)
    for layer, acts, tails in ((0, acts1, tails1), (1, acts2, tails2)):
        for q in range(4):
            rows = back[q] if layer == 0 else views[q][...]
            flip[:, pl.ds(q * PX, PX)] = rows.T
        rest = jnp.zeros((C, 3 * TAIL), F32)
        for q in range(4):
            rest = rest + dot(flip[:, pl.ds(q * PX, PX)], tails[q])
        for k in range(3):
            total = jnp.zeros((C, HEAD), F32)
            for q in range(4):
                total = total + dot(flip[:, pl.ds(q * PX, PX)], acts[q + k, :, pl.ds(0, HEAD)])
            value = side(total, rest[:, k * TAIL : (k + 1) * TAIL]).astype(BF)
            split_columns(value, blocks, 3 * layer + tap(k, odd))
    share(blocks, kept, sent, core)


def back_zero(at, left, back, right, s0, s1, s2, s3, w, flip, wk):
    odd = at[0]
    tail_rows(w, 0, odd, wk)
    six = [left] + [back.at[q] for q in range(4)] + [right]
    for q, before in enumerate((s0, s1, s2, s3)):
        value = descend(six, q, before[...], w, 0, odd, wk)
        wide = value.astype(F32)
        flip[pl.ds(0, C), pl.ds(q * PX, PX)] = left_by_one(wide).astype(BF).T
        flip[pl.ds(C, C), pl.ds(q * PX, PX)] = value.T
        flip[pl.ds(2 * C, C), pl.ds(q * PX, PX)] = right_by_one(wide).astype(BF).T


def spatial_grads(at, flip, p0, p1, p2, p3, t0, t1, t2, t3, kept, sent, blocks):
    rest = jnp.zeros((3 * C, 3 * TAIL), F32)
    for q, tails in enumerate((t0, t1, t2, t3)):
        rest = rest + dot(flip[:, pl.ds(q * PX, PX)], tails[...])
    for i in range(3):
        total = jnp.zeros((3 * C, HEAD), F32)
        for q, pad in enumerate((p0, p1, p2, p3)):
            total = total + dot(flip[:, pl.ds(q * PX, PX)], pad[pl.ds(i * COLS, PX), pl.ds(0, HEAD)])
        value = side(total, rest[:, i * TAIL : (i + 1) * TAIL]).astype(BF)
        for j in range(3):
            split_columns(value[j * C : (j + 1) * C], blocks, 3 * i + j)
    share(blocks, kept, sent, at[1])


def pack(at, kept, got, out, wide, rows):
    halves, taps, channels, _ = kept.shape
    owners = out.shape[0] // halves
    count = channels // owners
    for half in range(halves):
        for t in range(taps):
            rows[...] = kept[half, t].astype(F32) + got[half, t].astype(F32)
            for owner in range(owners):
                place = pl.ds(count * t, count)
                wide[halves * owner + half, place, :] = rows[pl.ds(count * owner, count), :]
    for n in range(halves * owners):
        out[n] = wide[n].astype(BF)


def place(at, own, got, out):
    odd = at[0]
    for q in range(2):
        frame = odd + q * (1 - 2 * odd)
        out[frame, pl.ds(pl.multiple_of(PX * odd, PX), PX), :] = own[q]
        out[frame, pl.ds(pl.multiple_of(PX * (1 - odd), PX), PX), :] = got[q]


def after(value, *others):
    return lax.optimization_barrier((value, *others))[0]


def step(clips_in, cotangent, spatial_weight, temporal_weight):
    owners, clips = lax.axis_size("frame"), lax.axis_size("clip")
    odd = lax.axis_index("frame") % 2
    core = lax.axis_index("clip") % 2
    at = jnp.stack([odd, core]).astype(jnp.int32)
    swap = [(n, n ^ 1) for n in range(owners)]
    outer = [(n, n - 2 if n % 2 == 0 else n + 2) for n in range(owners)]
    outer = [(a, b) for a, b in outer if 0 <= b < owners]
    inner = [(n, n + 2 if n % 2 == 0 else n - 2) for n in range(owners)]
    inner = [(a, b) for a, b in inner if 0 <= b < owners]
    cores = [(n, n ^ 1) for n in range(clips)]

    def send(value, perm, axis="frame"):
        return lax.ppermute(value, axis, perm)

    x = clips_in.reshape(2, FULL, C)
    cot = cotangent.reshape(2, FULL, C)
    ws = spatial_weight.reshape(9, C, C)
    flops = 2 * PX * C * C

    def cut(a, frame, start, size):
        return lax.dynamic_slice(a, (frame, start, 0), (1, size, C))[0]

    tall_start = (TALL - 2 * COLS) * (1 - odd)
    one = ((PX, C), BF)
    four = ((4, PX, C), BF)
    six = ((6, PX, C), BF)
    padded = ((PX + 2 * COLS, C), BF)
    tail = ((PX, 3 * TAIL), BF)
    tails = ((4, PX, 3 * TAIL), BF)
    wk = [pltpu.VMEM((3 * TAIL, C), BF)]
    packed = [((3, HEAD, 3 * TAIL), BF), ((3, 3 * TAIL, HEAD), BF), ((3 * TAIL, 3 * TAIL), BF)]

    x3 = send(cut(x, odd, tall_start, TALL), swap)
    s0, s1, p0, p1, t0, t1, *wp = run(
        conv_own, [one, one, padded, padded, tail, tail, *packed], (at, x, ws), (), 8 * flops
    )
    wt = jnp.swapaxes(temporal_weight, 2, 3)
    x2 = send(cut(after(x, s0), 1 - odd, tall_start, TALL), swap)
    right = send(s0, outer)
    cot_right = send(cut(after(cot, s0), odd, PX * odd, PX), outer)

    s3, p3, t3 = run(conv_other, [one, padded, tail], (at, x3, ws, *wp), (), 4 * flops)
    left = send(s3, inner)
    late = after(cot, x3)
    c3 = send(after(cut(late, odd, PX * (1 - odd), PX), x2), swap)
    s2, p2, t2 = run(conv_other, [one, padded, tail], (at, x2, ws, *wp), (), 4 * flops)
    cot_left = send(c3, inner)
    c2 = send(after(cut(late, 1 - odd, PX * (1 - odd), PX), c3), swap)

    acts1, tails1, state1, first, last = run(
        layer_one, [six, tails, four, one, one], (at, left, s0, s1, s2, s3, right, temporal_weight), wk, 8 * flops
    )
    left1 = send(last, inner)
    right1 = send(first, outer)
    back1, first, last = run(
        back_one, [four, one, one], (at, cot_left, cot, c2, c3, cot_right, state1, wt), wk, 8 * flops
    )
    back_left = send(last, inner)
    back_right = send(first, outer)
    two = ((2, PX, C), BF)
    acts2, tails2, own, sent = run(
        layer_two, [six, tails, two, two], (at, left1, state1, right1, temporal_weight), wk, 8 * flops
    )
    returned = send(sent, swap)

    width = C // clips
    kept, sent = run(
        temporal_grads,
        [((2, 6, C, width), BF)] * 2,
        (at, cot, c2, c3, acts2, tails2, back1, acts1, tails1),
        [pltpu.VMEM((C, 4 * PX), BF), pltpu.VMEM((4, 6, C, width), BF)],
        16 * flops,
    )
    temporal_terms = (kept, send(sent, cores, "clip"))
    (flip,) = run(
        back_zero,
        [((3 * C, 4 * PX), BF)],
        (at, back_left, back1, back_right, s0, s1, s2, s3, wt),
        wk,
        8 * flops,
    )

    groups = [[n + half * 2 + c for n in range(0, owners * clips, clips) for half in range(2)] for c in range(2)]

    def exchange(terms):
        kept, got = terms
        _, taps, _, _ = kept.shape
        block = (2 * owners, taps * (C // owners), width)
        scratch = [pltpu.VMEM(block, F32), pltpu.VMEM((C, width), F32)]
        (sent,) = run(pack, [(block, BF)], (at, kept, got), scratch, 1000)
        return lax.all_to_all(
            sent, ("frame", "clip"), split_axis=0, concat_axis=0, axis_index_groups=groups, tiled=True
        )

    def total(parts):
        summed = jnp.sum(parts.astype(F32), axis=0)
        return summed.reshape(-1, C // owners, width).transpose(1, 0, 2)

    temporal_parts = exchange(temporal_terms)
    kept, sent = run(
        spatial_grads,
        [((2, 9, C, width), BF)] * 2,
        (at, flip, p0, p1, p2, p3, t0, t1, t2, t3),
        [pltpu.VMEM((4, 9, C, width), BF)],
        24 * flops,
    )
    spatial_terms = (kept, send(sent, cores, "clip"))
    spatial_parts = exchange(spatial_terms)
    (out,) = run(place, [((2, FULL, C), BF)], (at, own, returned), (), 1000)
    grad_temporal = total(temporal_parts).reshape(C // owners, 2, 3, width)
    grad_spatial = total(spatial_parts).reshape(C // owners, 3, 3, width)
    return (out.reshape(clips_in.shape), grad_spatial, grad_temporal)


def solution(mesh):
    placed = (P("clip", "frame", None, None, None), P("clip", "frame", None, None, None), P(), P())
    return jax.shard_map(
        step,
        mesh=mesh,
        in_specs=placed,
        out_specs=(
            P("clip", "frame", None, None, None),
            P("frame", None, None, "clip"),
            P("frame", None, None, "clip"),
        ),
        check_vma=False,
    )
```

```python
import functools

import jax
import jax.numpy as jnp
from jax import lax
from jax.experimental import pallas as pl
from jax.experimental.pallas import tpu as pltpu
from jax.sharding import PartitionSpec as P


BF = jnp.bfloat16
F32 = jnp.float32
C = 320
COLS = 32
ROWS = 16
PX = ROWS * COLS
TALL = PX + COLS
FULL = 2 * PX
HEAD = 256
TAIL = C - HEAD
CLIPS = 4
VMEM_BYTES = 67_043_328
WIDTH = C // CLIPS
HBM = pl.BlockSpec(memory_space=pltpu.HBM)
SM = pl.BlockSpec(memory_space=pltpu.SMEM)


ONE = (PX, C)
TALL_ONE = (TALL, C)
THREE_TAILS = 3 * TAIL
SIDES = (CLIPS, PX, 3 * WIDTH)
KERNELS = (3, C, C)


def dot(a, b):
    return jnp.dot(a, b, preferred_element_type=F32)


def side(*parts):
    return jnp.concatenate(parts, axis=1)


class Mover:
    def __init__(self, sems):
        self.sems, self.count, self.leaving = sems, 0, []

    def copy(self, src, dst):
        c = pltpu.make_async_copy(src, dst, self.sems.at[self.count])
        self.count += 1
        c.start()
        return c

    def fetch(self, src, dst):
        return Arrival(self.copy(src, dst), dst)

    def put(self, src, dst):
        self.leaving.append(self.copy(src, dst))

    def finish(self):
        for c in self.leaving:
            c.wait()


class Arrival:
    def __init__(self, copy, ref):
        self.copy, self.ref = copy, ref

    def get(self):
        if self.copy is not None:
            self.copy.wait()
            self.copy = None
        return self.ref


def nth(ref, n):
    return ref.at[pl.ds(n * PX, PX), :]


def run(kernel, outs, args, scratch, copies, flops=0):
    nbytes = sum(a.size * a.dtype.itemsize for a in args) + sum(
        functools.reduce(lambda m, n: m * n, s, 2) for s in outs
    )
    return pl.pallas_call(
        kernel,
        out_shape=[jax.ShapeDtypeStruct(s, BF) for s in outs],
        in_specs=[SM] + [HBM] * (len(args) - 1),
        out_specs=[HBM] * len(outs),
        scratch_shapes=[s if not isinstance(s, tuple) else pltpu.VMEM(s, BF) for s in scratch]
        + [pltpu.SemaphoreType.DMA((copies,))],
        cost_estimate=pl.CostEstimate(flops=flops, bytes_accessed=nbytes, transcendentals=0),
        compiler_params=pltpu.CompilerParams(vmem_limit_bytes=VMEM_BYTES),
    )(*args)


def column_of(rows):
    return lax.broadcasted_iota(jnp.int32, (rows, 1), 0) % COLS


def right_by_one(v):
    return jnp.where(column_of(v.shape[0]) == 0, 0.0, pltpu.roll(v, 1, 0))


def left_by_one(v):
    return jnp.where(column_of(v.shape[0]) == COLS - 1, 0.0, pltpu.roll(v, v.shape[0] - 1, 0))


def sigmoid(v):
    return 1.0 / (1.0 + jnp.exp(-v))


def padded(pad, odd):
    pad[pl.ds(0, COLS), :] = jnp.zeros((COLS, C), BF)
    pad[pl.ds(TALL, COLS), :] = jnp.zeros((COLS, C), BF)
    return pad.at[pl.ds(pl.multiple_of(COLS * (1 - odd), COLS), TALL), :]


def convolve(pad, w, wn, wk, wr, out, sides):
    tails = side(*[pad[pl.ds(COLS * i, PX), pl.ds(HEAD, TAIL)] for i in range(3)])

    def heads(i):
        return pad[pl.ds(COLS * i, PX), pl.ds(0, HEAD)]

    parts = []
    for j in range(3):
        acc = dot(heads(0), w[j, pl.ds(0, HEAD), pl.ds(0, HEAD)])
        acc = acc + dot(heads(1), w[3 + j, pl.ds(0, HEAD), pl.ds(0, HEAD)])
        acc = acc + dot(heads(2), w[6 + j, pl.ds(0, HEAD), pl.ds(0, HEAD)])
        parts.append(acc + dot(tails, wk[j]))
    centre = pad[pl.ds(COLS, PX), pl.ds(0, HEAD)].astype(F32)
    total = right_by_one(parts[0]) + parts[1] + left_by_one(parts[2])
    out[:, pl.ds(0, HEAD)] = (centre + total).astype(BF)
    acc = dot(heads(0), wn[0]) + dot(heads(1), wn[1]) + dot(heads(2), wn[2])
    acc = acc + dot(tails, wr[...])
    total = right_by_one(acc[:, :TAIL]) + acc[:, TAIL : 2 * TAIL] + left_by_one(acc[:, 2 * TAIL :])
    centre = pad[pl.ds(COLS, PX), pl.ds(HEAD, TAIL)].astype(F32)
    out[:, pl.ds(HEAD, TAIL)] = (centre + total).astype(BF)
    for b in range(CLIPS):
        columns = slice(b * WIDTH, (b + 1) * WIDTH)
        sides[b] = side(*[pad[pl.ds(COLS * i, PX), columns] for i in range(3)])


def conv_own(at, x, cot, w, pair, out1, sides, x2, c3, c2, wn, wk, wr, *rest):
    vw, vwn, vwk, vwr, pads, states, vsides, vx2, vcot, sems = rest
    odd = at[0]
    move = Mover(sems)
    start = pl.multiple_of((TALL - 2 * COLS) * odd, COLS)
    frames = [odd, 1 - odd]
    rows = [
        move.fetch(x.at[frames[q], pl.ds(start, TALL), :], padded(pads.at[q], odd)) for q in range(2)
    ]
    weights = [move.fetch(w.at[n], vw.at[n]) for n in range(9)]
    away = pl.multiple_of((TALL - 2 * COLS) * (1 - odd), COLS)
    parts = [(move.fetch(x.at[1 - odd, pl.ds(away, TALL), :], vx2), x2)]
    here, there = pl.multiple_of(PX * odd, PX), pl.multiple_of(PX * (1 - odd), PX)
    parts += [
        (move.fetch(cot.at[odd, pl.ds(here, PX), :], vcot.at[0]), nth(pair, 1)),
        (move.fetch(cot.at[odd, pl.ds(there, PX), :], vcot.at[1]), c3),
        (move.fetch(cot.at[1 - odd, pl.ds(there, PX), :], vcot.at[2]), c2),
    ]
    for arrival in weights:
        arrival.get()
    for i in range(3):
        vwn[i] = side(*[vw[3 * i + j, pl.ds(0, HEAD), pl.ds(HEAD, TAIL)] for j in range(3)])
        for j in range(3):
            vwk[j, pl.ds(TAIL * i, TAIL), :] = vw[3 * i + j, pl.ds(HEAD, TAIL), pl.ds(0, HEAD)]
        vwr[pl.ds(TAIL * i, TAIL), :] = side(
            *[vw[3 * i + j, pl.ds(HEAD, TAIL), pl.ds(HEAD, TAIL)] for j in range(3)]
        )
    move.put(vwn, wn)
    move.put(vwk, wk)
    move.put(vwr, wr)
    for arrival, out in parts:
        move.put(arrival.get(), out)
    for q, out in enumerate((nth(pair, 0), out1)):
        rows[q].get()
        convolve(pads.at[q], vw, vwn, vwk, vwr, states.at[q], vsides.at[q])
        move.put(states.at[q], out)
        move.put(vsides.at[q], sides.at[q])
    move.finish()


def conv_other(at, x, w, wn, wk, wr, out, sides, *rest):
    vw, vwn, vwk, vwr, pad, state, vsides, sems = rest
    move = Mover(sems)
    needed = [move.fetch(x, padded(pad, at[0]))]
    needed += [move.fetch(w, vw), move.fetch(wn, vwn), move.fetch(wk, vwk), move.fetch(wr, vwr)]
    for arrival in needed:
        arrival.get()
    convolve(pad, vw, vwn, vwk, vwr, state, vsides)
    move.put(state, out)
    move.put(vsides, sides)
    move.finish()


def tap(k, odd):
    return k + odd * (2 - 2 * k)


def taps_of(move, w, layer, odd, vw):
    return [move.fetch(w.at[layer, tap(k, odd)], vw.at[k]) for k in range(3)]


def tail_rows(arrivals, wk):
    for k, arrival in enumerate(arrivals):
        wk[pl.ds(TAIL * k, TAIL), :] = arrival.get()[pl.ds(HEAD, TAIL), :]


def three_taps(three, vw, wk):
    tails = side(*[ref[:, pl.ds(HEAD, TAIL)] for ref in three])
    totals = []
    for columns in (pl.ds(0, HEAD), pl.ds(HEAD, TAIL)):
        total = dot(three[0][:, pl.ds(0, HEAD)], vw[0, pl.ds(0, HEAD), columns])
        total = total + dot(three[1][:, pl.ds(0, HEAD)], vw[1, pl.ds(0, HEAD), columns])
        total = total + dot(three[2][:, pl.ds(0, HEAD)], vw[2, pl.ds(0, HEAD), columns])
        totals.append(total + dot(tails, wk[:, columns]))
    return side(*totals)


def temporal(move, states, w, layer, odd, acts, vw, wk, vacts):
    weights = taps_of(move, w, layer, odd, vw)
    states = [move.fetch(src, dst) for src, dst in states]
    tail_rows(weights, wk)
    done = 0
    for q in range(4):
        while done < q + 3:
            v = states[done].get()[...].astype(F32)
            vacts[done] = (v * sigmoid(v)).astype(BF)
            move.put(vacts.at[done], acts.at[done])
            done += 1
        term = three_taps([vacts.at[q + k] for k in range(3)], vw, wk)
        yield (states[q + 1].get()[...].astype(F32) + term).astype(BF)


def layer_one(at, left, pair, s1, s2, s3, right, c3, w, acts, state, last, first, *rest):
    vs, vc3, vw, wk, vacts, nxt, sems = rest
    move = Mover(sems)
    sources = (left, nth(pair, 0), s1, s2, s3, nth(right, 0))
    states = [(ref, vs.at[n]) for n, ref in enumerate(sources)]
    for q, value in enumerate(temporal(move, states, w, 0, at[0], acts, vw, wk, vacts)):
        nxt[q] = value
        move.put(nxt.at[q], state.at[q])
        if q == 0:
            move.put(nxt.at[0], first)
            passing = move.fetch(c3, vc3)
    move.put(nxt.at[3], nth(last, 0))
    move.put(passing.get(), nth(last, 1))
    move.finish()


def layer_two(at, left, state, right, w, acts, own, sent, *rest):
    vs, vw, wk, vacts, nxt, sems = rest
    move = Mover(sems)
    sources = (nth(left, 0), state.at[0], state.at[1], state.at[2], state.at[3], right)
    states = [(ref, vs.at[n]) for n, ref in enumerate(sources)]
    for q, value in enumerate(temporal(move, states, w, 1, at[0], acts, vw, wk, vacts)):
        nxt[q] = value
        move.put(nxt.at[q], own.at[q] if q < 2 else nth(sent, 3 - q))
    move.finish()


def descend(six, q, before, vw, wk):
    three = [six[q + 2 - k].get() for k in range(3)]
    carried = three_taps(three, vw, wk)
    v = before.get()[...].astype(F32)
    s = sigmoid(v)
    return (three[1][...].astype(F32) + carried * (s * (1.0 + v * (1.0 - s)))).astype(BF)


def cotangent_views(cot, c2, c3, odd):
    start = pl.multiple_of(PX * odd, PX)
    return [cot.at[odd, pl.ds(start, PX), :], cot.at[1 - odd, pl.ds(start, PX), :], c2, c3]


def back_one(at, left, cot, c2, c3, right, state, w, back, first, last, *rest):
    vs, vstate, vw, wk, nxt, sems = rest
    odd = at[0]
    move = Mover(sems)
    weights = taps_of(move, w, 1, odd, vw)
    sources = [nth(left, 1)] + cotangent_views(cot, c2, c3, odd) + [nth(right, 1)]
    six = [move.fetch(ref, vs.at[n]) for n, ref in enumerate(sources)]
    before = [move.fetch(state.at[q], vstate.at[q]) for q in range(4)]
    tail_rows(weights, wk)
    for q in range(4):
        nxt[q] = descend(six, q, before[q], vw, wk)
        move.put(nxt.at[q], back.at[q])
        if q == 0:
            move.put(nxt.at[0], first)
    move.put(nxt.at[3], last)
    move.finish()


def temporal_grads(at, cot, c2, c3, acts2, back, acts1, blocks, *rest):
    vback, vacts, flip, vblocks, sems = rest
    odd = at[0]
    move = Mover(sems)
    views = cotangent_views(cot, c2, c3, odd)
    arrivals = []
    for layer, acts in ((0, acts1), (1, acts2)):
        ups = [back.at[q] for q in range(4)] if layer == 0 else views
        arrivals.append(
            (
                [move.fetch(ref, vback.at[layer, q]) for q, ref in enumerate(ups)],
                [move.fetch(acts.at[n], vacts.at[layer, n]) for n in range(6)],
            )
        )
    for layer, (ups, acts) in enumerate(arrivals):
        for q in range(4):
            flip[:, pl.ds(q * PX, PX)] = ups[q].get()[...].T
        for arrival in acts:
            arrival.get()
        tails = jnp.zeros((C, THREE_TAILS), F32)
        for q in range(4):
            ends = side(*[vacts[layer, q + tap(k, odd), :, pl.ds(HEAD, TAIL)] for k in range(3)])
            tails = tails + dot(flip[:, pl.ds(q * PX, PX)], ends)
        values = []
        for k in range(3):
            total = jnp.zeros((C, HEAD), F32)
            for q in range(4):
                heads = vacts[layer, q + tap(k, odd), :, pl.ds(0, HEAD)]
                total = total + dot(flip[:, pl.ds(q * PX, PX)], heads)
            values.append(side(total, tails[:, k * TAIL : (k + 1) * TAIL]).astype(BF))
        for b in range(CLIPS):
            vblocks[layer, b] = side(*[v[:, b * WIDTH : (b + 1) * WIDTH] for v in values])
            move.put(vblocks.at[layer, b], blocks.at[b, layer])
    move.finish()


def back_zero(at, left, back, right, pair, s1, s2, s3, w, flip, *rest):
    vs, vstate, vw, wk, vflip, sems = rest
    odd = at[0]
    move = Mover(sems)
    weights = taps_of(move, w, 0, odd, vw)
    sources = [left] + [back.at[q] for q in range(4)] + [right]
    six = [move.fetch(ref, vs.at[n]) for n, ref in enumerate(sources)]
    before = [move.fetch(ref, vstate.at[q]) for q, ref in enumerate((nth(pair, 0), s1, s2, s3))]
    tail_rows(weights, wk)
    for q in range(4):
        value = descend(six, q, before[q], vw, wk)
        turned = value.T
        wide = turned.astype(F32)
        column = lax.broadcasted_iota(jnp.int32, (1, PX), 1) % COLS
        ahead = jnp.where(column == COLS - 1, 0.0, pltpu.roll(wide, PX - 1, 1))
        behind = jnp.where(column == 0, 0.0, pltpu.roll(wide, 1, 1))
        vflip[q, pl.ds(0, C), :] = ahead.astype(BF)
        vflip[q, pl.ds(C, C), :] = turned
        vflip[q, pl.ds(2 * C, C), :] = behind.astype(BF)
        move.put(vflip.at[q], flip.at[q])
    move.finish()


def spatial_grads(at, flip, own_sides, sides2, sides3, temporal_blocks, kept, sent, *rest):
    vflip, vsides, blocks, sems = rest
    core = at[1]
    move = Mover(sems)
    sources = (own_sides.at[0], own_sides.at[1], sides2, sides3)
    arrivals = []
    for q in range(4):
        arrivals.append(move.fetch(flip.at[q], vflip.at[q]))
        arrivals.append(move.fetch(sources[q], vsides.at[q]))
    passing = [move.fetch(temporal_blocks.at[b], blocks.at[b, pl.ds(3, 2)]) for b in range(CLIPS)]
    for arrival in arrivals:
        arrival.get()
    for n in range(CLIPS):
        half = n % 2
        b = 2 * half + ((1 - core) if n < 2 else core)
        total = jnp.zeros((3 * C, 3 * WIDTH), F32)
        for q in range(4):
            total = total + dot(vflip[q], vsides[q, b])
        for j in range(3):
            blocks[b, j] = total[j * C : (j + 1) * C].astype(BF)
        if n == 0:
            for arrival in passing:
                arrival.get()
        move.put(blocks.at[b], (sent if n < 2 else kept).at[half])
    move.finish()


def pack(at, kept, got, out, *rest):
    vkept, vgot, wide, rows, vout, sems = rest
    halves, taps, channels, _ = kept.shape
    owners = out.shape[0] // halves
    count = channels // owners
    move = Mover(sems)
    arrivals = [
        (move.fetch(kept.at[h, t], vkept.at[h, t]), move.fetch(got.at[h, t], vgot.at[h, t]))
        for h in range(halves)
        for t in range(taps)
    ]
    for h in range(halves):
        for t in range(taps):
            mine, theirs = arrivals[h * taps + t]
            rows[...] = mine.get()[...].astype(F32) + theirs.get()[...].astype(F32)
            for owner in range(owners):
                wide[owner, pl.ds(count * t, count), :] = rows[pl.ds(count * owner, count), :]
        for owner in range(owners):
            vout[owners * h + owner] = wide[owner].astype(BF)
        move.put(vout.at[pl.ds(owners * h, owners)], out.at[pl.ds(owners * h, owners)])
    move.finish()


def place(at, own, got, out, *rest):
    vown, vgot, sems = rest
    odd = at[0]
    move = Mover(sems)
    here, there = pl.multiple_of(PX * odd, PX), pl.multiple_of(PX * (1 - odd), PX)
    frames = (odd, 1 - odd)
    arrivals = []
    for q in range(2):
        arrivals.append((move.fetch(own.at[q], vown.at[q]), out.at[frames[q], pl.ds(here, PX), :]))
        arrivals.append((move.fetch(nth(got, q), vgot.at[q]), out.at[frames[q], pl.ds(there, PX), :]))
    for arrival, target in arrivals:
        move.put(arrival.get(), target)
    move.finish()


def after(value, *others):
    return lax.optimization_barrier((value, *others))[0]


def step(clips_in, cotangent, spatial_weight, temporal_weight):
    owners, clips = lax.axis_size("frame"), lax.axis_size("clip")
    odd = lax.axis_index("frame") % 2
    core = lax.axis_index("clip") % 2
    at = jnp.stack([odd, core]).astype(jnp.int32)
    swap = [(n, n ^ 1) for n in range(owners)]
    outer = [(n, n - 2 if n % 2 == 0 else n + 2) for n in range(owners)]
    outer = [(a, b) for a, b in outer if 0 <= b < owners]
    inner = [(n, n + 2 if n % 2 == 0 else n - 2) for n in range(owners)]
    inner = [(a, b) for a, b in inner if 0 <= b < owners]
    cores = [(n, n ^ 1) for n in range(clips)]

    def send(value, perm, axis="frame"):
        shape = value.shape
        if axis == "frame":
            value = value.reshape(-1, COLS, C)
        return lax.ppermute(value, axis, perm).reshape(shape)

    x = clips_in.reshape(2, FULL, C)
    cot = cotangent.reshape(2, FULL, C)
    ws = spatial_weight.reshape(9, C, C)
    flops = 2 * PX * C * C

    flat, two, four, six = (2 * PX, C), (2, PX, C), (4, PX, C), (6, PX, C)
    packed = [(3, HEAD, THREE_TAILS), (3, THREE_TAILS, HEAD), (THREE_TAILS, THREE_TAILS)]
    whole = [(9, C, C), *packed]
    pad = (PX + 2 * COLS, C)
    kernels = [KERNELS, (THREE_TAILS, C)]

    tall_start = (TALL - 2 * COLS) * (1 - odd)
    x3 = send(lax.dynamic_slice(x, (odd, tall_start, 0), (1, TALL, C))[0], swap)
    pair, s1, own_sides, x2, c3, c2, *wp = run(
        conv_own,
        [flat, ONE, (2, *SIDES), TALL_ONE, ONE, ONE, *packed],
        (at, x, cot, ws),
        [*whole, (2, *pad), two, (2, *SIDES), TALL_ONE, (3, PX, C)],
        32,
        8 * flops,
    )
    wt = jnp.swapaxes(temporal_weight, 2, 3)
    right = send(pair, outer)
    x2 = send(x2, swap)

    other = [*whole, pad, ONE, SIDES]
    s3, sides3 = run(conv_other, [ONE, SIDES], (at, x3, ws, *wp), other, 8, 4 * flops)
    left = send(s3, inner)
    c3 = send(after(c3, x2), swap)
    s2, sides2 = run(conv_other, [ONE, SIDES], (at, x2, ws, *wp), other, 8, 4 * flops)
    c2 = send(after(c2, c3), swap)

    acts1, state1, last, first = run(
        layer_one,
        [six, four, flat, ONE],
        (at, left, pair, s1, s2, s3, right, c3, temporal_weight),
        [six, ONE, *kernels, six, four],
        32,
        8 * flops,
    )
    left1 = send(last, inner)
    right1 = send(first, outer)
    back1, first, last = run(
        back_one,
        [four, ONE, ONE],
        (at, left1, cot, c2, c3, right, state1, wt),
        [six, four, *kernels, four],
        32,
        8 * flops,
    )
    back_left = send(last, inner)
    back_right = send(first, outer)
    acts2, own, sent = run(
        layer_two,
        [six, two, flat],
        (at, left1, state1, right1, temporal_weight),
        [six, *kernels, six, four],
        32,
        8 * flops,
    )
    returned = send(sent, swap)

    (temporal_blocks,) = run(
        temporal_grads,
        [(CLIPS, 2, C, 3 * WIDTH)],
        (at, cot, c2, c3, acts2, back1, acts1),
        [(2, *four), (2, *six), (C, 4 * PX), (2, CLIPS, C, 3 * WIDTH)],
        32,
        16 * flops,
    )
    (flip,) = run(
        back_zero,
        [(4, 3 * C, PX)],
        (at, back_left, back1, back_right, pair, s1, s2, s3, wt),
        [six, four, *kernels, (4, 3 * C, PX)],
        32,
        8 * flops,
    )
    shares = (2, 5, C, 3 * WIDTH)
    kept, sent = run(
        spatial_grads,
        [shares] * 2,
        (at, flip, own_sides, sides2, sides3, temporal_blocks),
        [(4, 3 * C, PX), (4, *SIDES), (CLIPS, 5, C, 3 * WIDTH)],
        32,
        24 * flops,
    )
    got = send(sent, cores, "clip")

    rows = C // owners
    block = (2 * owners, 5 * rows, 3 * WIDTH)
    (packs,) = run(
        pack,
        [block],
        (at, kept, got),
        [
            shares,
            shares,
            pltpu.VMEM((owners, 5 * rows, 3 * WIDTH), F32),
            pltpu.VMEM((C, 3 * WIDTH), F32),
            block,
        ],
        32,
        1000,
    )
    groups = [[n + half * 2 + c for half in range(2) for n in range(0, owners * clips, clips)] for c in range(2)]
    parts = lax.all_to_all(
        packs, ("frame", "clip"), split_axis=0, concat_axis=0, axis_index_groups=groups, tiled=True
    )
    (out,) = run(place, [(2, FULL, C)], (at, own, returned), [two, two], 16, 1000)
    total = jnp.sum(parts.astype(F32), axis=0).reshape(5, rows, 3, WIDTH)
    grad_spatial = total[:3].transpose(1, 2, 0, 3)
    grad_temporal = total[3:].transpose(1, 0, 2, 3)
    return (out.reshape(clips_in.shape), grad_spatial, grad_temporal)


def solution(mesh):
    placed = (P("clip", "frame", None, None, None), P("clip", "frame", None, None, None), P(), P())
    return jax.shard_map(
        step,
        mesh=mesh,
        in_specs=placed,
        out_specs=(
            P("clip", "frame", None, None, None),
            P("frame", None, None, "clip"),
            P("frame", None, None, "clip"),
        ),
        check_vma=False,
    )
```

```python
import functools

import jax
import jax.numpy as jnp
from jax import lax
from jax.experimental import pallas as pl
from jax.experimental.pallas import tpu as pltpu
from jax.sharding import PartitionSpec as P


BF = jnp.bfloat16
F32 = jnp.float32
C = 320
COLS = 32
ROWS = 16
PX = ROWS * COLS
TALL = PX + COLS
FULL = 2 * PX
HEAD = 256
TAIL = C - HEAD
CLIPS = 4
VMEM_BYTES = 24 * 1024 * 1024
WIDTH = C // CLIPS
HBM = pl.BlockSpec(memory_space=pltpu.HBM)
VM = pl.BlockSpec(memory_space=pltpu.VMEM)
SM = pl.BlockSpec(memory_space=pltpu.SMEM)


ONE = (PX, C)
TALL_ONE = (TALL, C)
THREE_TAILS = 3 * TAIL
SIDES = (CLIPS, PX, 3 * WIDTH)
KERNELS = (3, C, C)


def dot(a, b):
    return jnp.dot(a, b, preferred_element_type=F32)


def side(*parts):
    return jnp.concatenate(parts, axis=1)


class Mover:
    def __init__(self, sems):
        self.sems, self.count, self.leaving = sems, 0, []

    def copy(self, src, dst):
        c = pltpu.make_async_copy(src, dst, self.sems.at[self.count])
        self.count += 1
        c.start()
        return c

    def fetch(self, src, dst):
        return Arrival(self.copy(src, dst), dst)

    def put(self, src, dst):
        self.leaving.append(self.copy(src, dst))

    def finish(self):
        for c in self.leaving:
            c.wait()


class Arrival:
    def __init__(self, copy, ref):
        self.copy, self.ref = copy, ref

    def get(self):
        if self.copy is not None:
            self.copy.wait()
            self.copy = None
        return self.ref


def nth(ref, n):
    return ref.at[pl.ds(n * PX, PX), :]


def run(kernel, outs, args, scratch=(), copies=0, flops=0, far=(), far_outs=False, limit=VMEM_BYTES):
    nbytes = sum(a.size * a.dtype.itemsize for a in args) + sum(
        functools.reduce(lambda m, n: m * n, s, 2) for s in outs
    )
    return pl.pallas_call(
        kernel,
        out_shape=[jax.ShapeDtypeStruct(s, BF) for s in outs],
        in_specs=[SM] + [HBM if n in far else VM for n in range(1, len(args))],
        out_specs=[HBM if far_outs else VM] * len(outs),
        scratch_shapes=[s if not isinstance(s, tuple) else pltpu.VMEM(s, BF) for s in scratch]
        + ([pltpu.SemaphoreType.DMA((copies,))] if copies else []),
        cost_estimate=pl.CostEstimate(flops=flops, bytes_accessed=nbytes, transcendentals=0),
        compiler_params=pltpu.CompilerParams(vmem_limit_bytes=limit),
    )(*args)


def column_of(rows):
    return lax.broadcasted_iota(jnp.int32, (rows, 1), 0) % COLS


def right_by_one(v):
    return jnp.where(column_of(v.shape[0]) == 0, 0.0, pltpu.roll(v, 1, 0))


def left_by_one(v):
    return jnp.where(column_of(v.shape[0]) == COLS - 1, 0.0, pltpu.roll(v, v.shape[0] - 1, 0))


def sigmoid(v):
    return 1.0 / (1.0 + jnp.exp(-v))


def padded(pad, odd):
    pad[pl.ds(0, COLS), :] = jnp.zeros((COLS, C), BF)
    pad[pl.ds(TALL, COLS), :] = jnp.zeros((COLS, C), BF)
    return pad.at[pl.ds(pl.multiple_of(COLS * (1 - odd), COLS), TALL), :]


def convolve(pad, w, wn, wk, wr, out, sides):
    tails = side(*[pad[pl.ds(COLS * i, PX), pl.ds(HEAD, TAIL)] for i in range(3)])

    def heads(i):
        return pad[pl.ds(COLS * i, PX), pl.ds(0, HEAD)]

    parts = []
    for j in range(3):
        acc = dot(heads(0), w[j, pl.ds(0, HEAD), pl.ds(0, HEAD)])
        acc = acc + dot(heads(1), w[3 + j, pl.ds(0, HEAD), pl.ds(0, HEAD)])
        acc = acc + dot(heads(2), w[6 + j, pl.ds(0, HEAD), pl.ds(0, HEAD)])
        parts.append(acc + dot(tails, wk[j]))
    centre = pad[pl.ds(COLS, PX), pl.ds(0, HEAD)].astype(F32)
    total = right_by_one(parts[0]) + parts[1] + left_by_one(parts[2])
    out[:, pl.ds(0, HEAD)] = (centre + total).astype(BF)
    acc = dot(heads(0), wn[0]) + dot(heads(1), wn[1]) + dot(heads(2), wn[2])
    acc = acc + dot(tails, wr[...])
    total = right_by_one(acc[:, :TAIL]) + acc[:, TAIL : 2 * TAIL] + left_by_one(acc[:, 2 * TAIL :])
    centre = pad[pl.ds(COLS, PX), pl.ds(HEAD, TAIL)].astype(F32)
    out[:, pl.ds(HEAD, TAIL)] = (centre + total).astype(BF)
    for b in range(CLIPS):
        columns = slice(b * WIDTH, (b + 1) * WIDTH)
        sides[b] = side(*[pad[pl.ds(COLS * i, PX), columns] for i in range(3)])


def conv_own(at, x, cot, w, tw, out0, out1, sides, x2, c3, c2, cot0, cot1, vw, wn, wk, wr, vt, vtk, vb, vbk, pads, sems):
    odd = at[0]
    move = Mover(sems)
    start = pl.multiple_of((TALL - 2 * COLS) * odd, COLS)
    frames = [odd, 1 - odd]
    rows = [
        move.fetch(x.at[frames[q], pl.ds(start, TALL), :], padded(pads.at[q], odd)) for q in range(2)
    ]
    weights = [move.fetch(w.at[n], vw.at[n]) for n in range(9)]
    away = pl.multiple_of((TALL - 2 * COLS) * (1 - odd), COLS)
    here, there = pl.multiple_of(PX * odd, PX), pl.multiple_of(PX * (1 - odd), PX)
    later = [
        move.fetch(x.at[1 - odd, pl.ds(away, TALL), :], x2),
        move.fetch(cot.at[odd, pl.ds(here, PX), :], cot0),
        move.fetch(cot.at[1 - odd, pl.ds(here, PX), :], cot1),
        move.fetch(cot.at[odd, pl.ds(there, PX), :], c3),
        move.fetch(cot.at[1 - odd, pl.ds(there, PX), :], c2),
    ]
    taps = [(l, k, move.fetch(tw.at[l, tap(k, odd)], vt.at[l, k])) for l in range(2) for k in range(3)]
    for arrival in weights:
        arrival.get()
    for i in range(3):
        wn[i] = side(*[vw[3 * i + j, pl.ds(0, HEAD), pl.ds(HEAD, TAIL)] for j in range(3)])
        for j in range(3):
            wk[j, pl.ds(TAIL * i, TAIL), :] = vw[3 * i + j, pl.ds(HEAD, TAIL), pl.ds(0, HEAD)]
        wr[pl.ds(TAIL * i, TAIL), :] = side(
            *[vw[3 * i + j, pl.ds(HEAD, TAIL), pl.ds(HEAD, TAIL)] for j in range(3)]
        )
    for arrival in rows:
        arrival.get()
    for l, k, arrival in taps:
        arrival.get()
        turned = vt[l, k].T
        vb[l, k] = turned
        vtk[l, pl.ds(TAIL * k, TAIL), :] = vt[l, k, pl.ds(HEAD, TAIL), :]
        vbk[l, pl.ds(TAIL * k, TAIL), :] = turned[HEAD:, :]
    for q, out in enumerate((out0, out1)):
        convolve(pads.at[q], vw, wn, wk, wr, out, sides.at[q])
    for arrival in later:
        arrival.get()


def conv_other(at, x, w, wn, wk, wr, out, sides, pad):
    padded(pad, at[0])[...] = x[...]
    convolve(pad, w, wn, wk, wr, out, sides)


def tap(k, odd):
    return k + odd * (2 - 2 * k)


def three_taps(three, vw, layer, wk):
    tails = side(*[ref[:, pl.ds(HEAD, TAIL)] for ref in three])
    totals = []
    for columns in (pl.ds(0, HEAD), pl.ds(HEAD, TAIL)):
        total = dot(three[0][:, pl.ds(0, HEAD)], vw[layer, 0, pl.ds(0, HEAD), columns])
        total = total + dot(three[1][:, pl.ds(0, HEAD)], vw[layer, 1, pl.ds(0, HEAD), columns])
        total = total + dot(three[2][:, pl.ds(0, HEAD)], vw[layer, 2, pl.ds(0, HEAD), columns])
        totals.append(total + dot(tails, wk[layer, :, columns]))
    return side(*totals)


def temporal(states, vw, layer, wk, acts):
    done = 0
    for q in range(4):
        while done < q + 3:
            v = states[done][...].astype(F32)
            acts[done] = (v * sigmoid(v)).astype(BF)
            done += 1
        term = three_taps([acts.at[q + k] for k in range(3)], vw, layer, wk)
        yield (states[q + 1][...].astype(F32) + term).astype(BF)


def layer_one(at, left, s0, s1, s2, s3, right, vw, wk, acts, state, last, first):
    states = (left, s0, s1, s2, s3, right)
    for q, value in enumerate(temporal(states, vw, 0, wk, acts)):
        state[q] = value
        if q == 0:
            first[...] = value
        if q == 3:
            last[...] = value


def layer_two(at, left, state, right, vw, wk, acts, own, sent):
    states = (left, state.at[0], state.at[1], state.at[2], state.at[3], right)
    for q, value in enumerate(temporal(states, vw, 1, wk, acts)):
        if q < 2:
            own[q] = value
        else:
            sent[pl.ds((3 - q) * PX, PX), :] = value


def descend(six, q, before, vw, layer, wk):
    three = [six[q + 2 - k] for k in range(3)]
    carried = three_taps(three, vw, layer, wk)
    v = before[...].astype(F32)
    s = sigmoid(v)
    return (three[1][...].astype(F32) + carried * (s * (1.0 + v * (1.0 - s)))).astype(BF)


def back_one(at, left, cot0, cot1, c2, c3, right, state, vw, wk, back, first, last):
    six = (left, cot0, cot1, c2, c3, right)
    for q in range(4):
        value = descend(six, q, state.at[q], vw, 1, wk)
        back[q] = value
        if q == 0:
            first[...] = value
        if q == 3:
            last[...] = value


def temporal_grads(at, cot0, cot1, c2, c3, acts2, back, acts1, blocks, flip):
    odd = at[0]
    views = (cot0, cot1, c2, c3)
    for layer, acts in ((0, acts1), (1, acts2)):
        for q in range(4):
            up = back.at[q] if layer == 0 else views[q]
            flip[:, pl.ds(q * PX, PX)] = up[...].T
        tails = jnp.zeros((C, THREE_TAILS), F32)
        for q in range(4):
            ends = side(*[acts[q + tap(k, odd), :, pl.ds(HEAD, TAIL)] for k in range(3)])
            tails = tails + dot(flip[:, pl.ds(q * PX, PX)], ends)
        values = []
        for k in range(3):
            total = jnp.zeros((C, HEAD), F32)
            for q in range(4):
                heads = acts[q + tap(k, odd), :, pl.ds(0, HEAD)]
                total = total + dot(flip[:, pl.ds(q * PX, PX)], heads)
            values.append(side(total, tails[:, k * TAIL : (k + 1) * TAIL]).astype(BF))
        for b in range(CLIPS):
            blocks[b, layer] = side(*[v[:, b * WIDTH : (b + 1) * WIDTH] for v in values])


def back_zero(at, left, back, right, s0, s1, s2, s3, vw, wk, own_sides, sides2, sides3, passing, kept, sent, flip):
    core = at[1]
    six = [left] + [back.at[q] for q in range(4)] + [right]
    column = lax.broadcasted_iota(jnp.int32, (1, PX), 1) % COLS
    for q, before in enumerate((s0, s1, s2, s3)):
        turned = descend(six, q, before, vw, 0, wk).T
        wide = turned.astype(F32)
        ahead = jnp.where(column == COLS - 1, 0.0, pltpu.roll(wide, PX - 1, 1))
        behind = jnp.where(column == 0, 0.0, pltpu.roll(wide, 1, 1))
        flip[q, pl.ds(0, C), :] = ahead.astype(BF)
        flip[q, pl.ds(C, C), :] = turned
        flip[q, pl.ds(2 * C, C), :] = behind.astype(BF)
    sides = (own_sides.at[0], own_sides.at[1], sides2, sides3)
    for half in range(2):
        for out, b in ((kept, 2 * half + core), (sent, 2 * half + 1 - core)):
            total = jnp.zeros((3 * C, 3 * WIDTH), F32)
            for q in range(4):
                total = total + dot(flip[q], sides[q][b])
            for j in range(3):
                out[half, j] = total[j * C : (j + 1) * C].astype(BF)
            for layer in range(2):
                out[half, 3 + layer] = passing[b, layer]


def pack(at, kept, got, out, wide, rows, vout, sems):
    halves, taps, channels, _ = kept.shape
    owners = out.shape[0] // halves
    count = channels // owners
    move = Mover(sems)
    for h in range(halves):
        for t in range(taps):
            rows[...] = kept[h, t].astype(F32) + got[h, t].astype(F32)
            for owner in range(owners):
                wide[owner, pl.ds(count * t, count), :] = rows[pl.ds(count * owner, count), :]
        for owner in range(owners):
            vout[owners * h + owner] = wide[owner].astype(BF)
        move.put(vout.at[pl.ds(owners * h, owners)], out.at[pl.ds(owners * h, owners)])
    move.finish()


def place(at, own, got, out, sems):
    odd = at[0]
    move = Mover(sems)
    here, there = pl.multiple_of(PX * odd, PX), pl.multiple_of(PX * (1 - odd), PX)
    for q, frame in enumerate((odd, 1 - odd)):
        move.put(own.at[q], out.at[frame, pl.ds(here, PX), :])
        move.put(nth(got, q), out.at[frame, pl.ds(there, PX), :])
    move.finish()


def after(value, *others):
    return lax.optimization_barrier((value, *others))[0]


def step(clips_in, cotangent, spatial_weight, temporal_weight):
    owners, clips = lax.axis_size("frame"), lax.axis_size("clip")
    odd = lax.axis_index("frame") % 2
    core = lax.axis_index("clip") % 2
    at = jnp.stack([odd, core]).astype(jnp.int32)
    swap = [(n, n ^ 1) for n in range(owners)]
    outer = [(n, n - 2 if n % 2 == 0 else n + 2) for n in range(owners)]
    outer = [(a, b) for a, b in outer if 0 <= b < owners]
    inner = [(n, n + 2 if n % 2 == 0 else n - 2) for n in range(owners)]
    inner = [(a, b) for a, b in inner if 0 <= b < owners]
    cores = [(n, n ^ 1) for n in range(clips)]

    def send(value, perm, axis="frame"):
        shape = value.shape
        if axis == "frame":
            value = value.reshape(-1, COLS, C)
        return lax.ppermute(value, axis, perm).reshape(shape)

    x = clips_in.reshape(2, FULL, C)
    cot = cotangent.reshape(2, FULL, C)
    ws = spatial_weight.reshape(9, C, C)
    flops = 2 * PX * C * C

    flat, two, four, six = (2 * PX, C), (2, PX, C), (4, PX, C), (6, PX, C)
    packed = [(9, C, C), (3, HEAD, THREE_TAILS), (3, THREE_TAILS, HEAD), (THREE_TAILS, THREE_TAILS)]
    taps = [(2, *KERNELS), (2, THREE_TAILS, C)]
    pad = (PX + 2 * COLS, C)

    tall_start = (TALL - 2 * COLS) * (1 - odd)
    x3 = send(lax.dynamic_slice(x, (odd, tall_start, 0), (1, TALL, C))[0], swap)
    s0, s1, own_sides, x2, c3, c2, cot0, cot1, w, wn, wk, wr, vt, vtk, vb, vbk = run(
        conv_own,
        [ONE, ONE, (2, *SIDES), TALL_ONE, ONE, ONE, ONE, ONE, *packed, *taps, *taps],
        (at, x, cot, ws, temporal_weight),
        [(2, *pad)],
        32,
        8 * flops,
        far=(1, 2, 3, 4),
    )
    wp = (w, wn, wk, wr)
    right = send(s0, outer)
    x2 = send(x2, swap)

    s3, sides3 = run(conv_other, [ONE, SIDES], (at, x3, *wp), [pad], 0, 4 * flops)
    left = send(s3, inner)
    c3 = send(after(c3, x2), swap)
    s2, sides2 = run(conv_other, [ONE, SIDES], (at, x2, *wp), [pad], 0, 4 * flops)
    c2 = send(after(c2, c3), swap)
    cot_right = send(after(cot0, right), outer)
    cot_left = send(c3, inner)

    acts1, state1, last, first = run(
        layer_one,
        [six, four, ONE, ONE],
        (at, left, s0, s1, s2, s3, right, vt, vtk),
        flops=8 * flops,
    )
    left1 = send(last, inner)
    right1 = send(first, outer)
    back1, first, last = run(
        back_one,
        [four, ONE, ONE],
        (at, cot_left, cot0, cot1, c2, c3, cot_right, state1, vb, vbk),
        flops=8 * flops,
    )
    back_left = send(last, inner)
    back_right = send(first, outer)
    acts2, own, sent = run(
        layer_two, [six, two, flat], (at, left1, state1, right1, vt, vtk), flops=8 * flops
    )
    returned = send(sent, swap)

    (temporal_blocks,) = run(
        temporal_grads,
        [(CLIPS, 2, C, 3 * WIDTH)],
        (at, cot0, cot1, c2, c3, acts2, back1, acts1),
        [(C, 4 * PX)],
        flops=16 * flops,
    )
    shares = (2, 5, C, 3 * WIDTH)
    kept, sent = run(
        back_zero,
        [shares] * 2,
        (at, back_left, back1, back_right, s0, s1, s2, s3, vb, vbk, own_sides, sides2, sides3, temporal_blocks),
        [(4, 3 * C, PX)],
        flops=32 * flops,
    )
    got = send(sent, cores, "clip")
    (out,) = run(place, [(2, FULL, C)], (at, own, returned), (), 4, 1000, far_outs=True)

    rows = C // owners
    block = (2 * owners, 5 * rows, 3 * WIDTH)
    (packs,) = run(
        pack,
        [block],
        (at, kept, got),
        [pltpu.VMEM((owners, 5 * rows, 3 * WIDTH), F32), pltpu.VMEM((C, 3 * WIDTH), F32), block],
        4,
        1000,
        far_outs=True,
    )
    groups = [[n + half * 2 + c for half in range(2) for n in range(0, owners * clips, clips)] for c in range(2)]
    parts = lax.all_to_all(packs, ("frame", "clip"), split_axis=0, concat_axis=0, axis_index_groups=groups, tiled=True)
    total = jnp.sum(parts.astype(F32), axis=0).reshape(5, rows, 3, WIDTH)
    grad_spatial = total[:3].transpose(1, 2, 0, 3)
    grad_temporal = total[3:].transpose(1, 0, 2, 3)
    return (out.reshape(clips_in.shape), grad_spatial, grad_temporal)


def solution(mesh):
    placed = (P("clip", "frame", None, None, None), P("clip", "frame", None, None, None), P(), P())
    return jax.shard_map(
        step,
        mesh=mesh,
        in_specs=placed,
        out_specs=(
            P("clip", "frame", None, None, None),
            P("frame", None, None, "clip"),
            P("frame", None, None, "clip"),
        ),
        check_vma=False,
    )
```

```python
import functools

import jax
import jax.numpy as jnp
from jax import lax
from jax.experimental import pallas as pl
from jax.experimental.pallas import tpu as pltpu
from jax.sharding import PartitionSpec as P


BF = jnp.bfloat16
F32 = jnp.float32
C = 320
COLS = 32
ROWS = 16
PX = ROWS * COLS
TALL = PX + COLS
FULL = 2 * PX
HEAD = 256
TAIL = C - HEAD
CLIPS = 4
VMEM_BYTES = 24 * 1024 * 1024
WIDTH = C // CLIPS
HBM = pl.BlockSpec(memory_space=pltpu.HBM)
VM = pl.BlockSpec(memory_space=pltpu.VMEM)
SM = pl.BlockSpec(memory_space=pltpu.SMEM)


ONE = (PX, C)
TALL_ONE = (TALL, C)
THREE_TAILS = 3 * TAIL
SIDES = (CLIPS, PX, 3 * WIDTH)
KERNELS = (3, C, C)


def dot(a, b):
    return jnp.dot(a, b, preferred_element_type=F32)


def side(*parts):
    return jnp.concatenate(parts, axis=1)


class Mover:
    def __init__(self, sems):
        self.sems, self.count, self.leaving = sems, 0, []

    def copy(self, src, dst):
        c = pltpu.make_async_copy(src, dst, self.sems.at[self.count])
        self.count += 1
        c.start()
        return c

    def fetch(self, src, dst):
        return Arrival(self.copy(src, dst), dst)

    def put(self, src, dst):
        self.leaving.append(self.copy(src, dst))

    def finish(self):
        for c in self.leaving:
            c.wait()


class Arrival:
    def __init__(self, copy, ref):
        self.copy, self.ref = copy, ref

    def get(self):
        if self.copy is not None:
            self.copy.wait()
            self.copy = None
        return self.ref


def nth(ref, n):
    return ref.at[pl.ds(n * PX, PX), :]


def run(kernel, outs, args, scratch=(), copies=0, flops=0, far=(), far_outs=False, limit=VMEM_BYTES):
    nbytes = sum(a.size * a.dtype.itemsize for a in args) + sum(
        functools.reduce(lambda m, n: m * n, s, 2) for s in outs
    )
    return pl.pallas_call(
        kernel,
        out_shape=[jax.ShapeDtypeStruct(s, BF) for s in outs],
        in_specs=[SM] + [HBM if n in far else VM for n in range(1, len(args))],
        out_specs=[HBM if far_outs else VM] * len(outs),
        scratch_shapes=[s if not isinstance(s, tuple) else pltpu.VMEM(s, BF) for s in scratch]
        + ([pltpu.SemaphoreType.DMA((copies,))] if copies else []),
        cost_estimate=pl.CostEstimate(flops=flops, bytes_accessed=nbytes, transcendentals=0),
        compiler_params=pltpu.CompilerParams(vmem_limit_bytes=limit),
    )(*args)


def column_of(rows):
    return lax.broadcasted_iota(jnp.int32, (rows, 1), 0) % COLS


def right_by_one(v):
    return jnp.where(column_of(v.shape[0]) == 0, 0.0, pltpu.roll(v, 1, 0))


def left_by_one(v):
    return jnp.where(column_of(v.shape[0]) == COLS - 1, 0.0, pltpu.roll(v, v.shape[0] - 1, 0))


def sigmoid(v):
    return 1.0 / (1.0 + jnp.exp(-v))


def padded(pad, odd):
    pad[pl.ds(0, COLS), :] = jnp.zeros((COLS, C), BF)
    pad[pl.ds(TALL, COLS), :] = jnp.zeros((COLS, C), BF)
    return pad.at[pl.ds(pl.multiple_of(COLS * (1 - odd), COLS), TALL), :]


def convolve(pad, w, wn, wk, wr, out, sides):
    tails = side(*[pad[pl.ds(COLS * i, PX), pl.ds(HEAD, TAIL)] for i in range(3)])

    def heads(i):
        return pad[pl.ds(COLS * i, PX), pl.ds(0, HEAD)]

    parts = []
    for j in range(3):
        acc = dot(heads(0), w[j, pl.ds(0, HEAD), pl.ds(0, HEAD)])
        acc = acc + dot(heads(1), w[3 + j, pl.ds(0, HEAD), pl.ds(0, HEAD)])
        acc = acc + dot(heads(2), w[6 + j, pl.ds(0, HEAD), pl.ds(0, HEAD)])
        parts.append(acc + dot(tails, wk[j]))
    centre = pad[pl.ds(COLS, PX), pl.ds(0, HEAD)].astype(F32)
    total = right_by_one(parts[0]) + parts[1] + left_by_one(parts[2])
    out[:, pl.ds(0, HEAD)] = (centre + total).astype(BF)
    acc = dot(heads(0), wn[0]) + dot(heads(1), wn[1]) + dot(heads(2), wn[2])
    acc = acc + dot(tails, wr[...])
    total = right_by_one(acc[:, :TAIL]) + acc[:, TAIL : 2 * TAIL] + left_by_one(acc[:, 2 * TAIL :])
    centre = pad[pl.ds(COLS, PX), pl.ds(HEAD, TAIL)].astype(F32)
    out[:, pl.ds(HEAD, TAIL)] = (centre + total).astype(BF)
    for b in range(CLIPS):
        columns = slice(b * WIDTH, (b + 1) * WIDTH)
        sides[b] = side(*[pad[pl.ds(COLS * i, PX), columns] for i in range(3)])


def conv_own(at, x, w, out0, out1, sides, x2, wn, wk, wr, pads):
    odd = at[0]
    for i in range(3):
        wn[i] = side(*[w[3 * i + j, pl.ds(0, HEAD), pl.ds(HEAD, TAIL)] for j in range(3)])
        for j in range(3):
            wk[j, pl.ds(TAIL * i, TAIL), :] = w[3 * i + j, pl.ds(HEAD, TAIL), pl.ds(0, HEAD)]
        wr[pl.ds(TAIL * i, TAIL), :] = side(
            *[w[3 * i + j, pl.ds(HEAD, TAIL), pl.ds(HEAD, TAIL)] for j in range(3)]
        )
    start = pl.multiple_of((TALL - 2 * COLS) * odd, COLS)
    for q, out in enumerate((out0, out1)):
        padded(pads.at[q], odd)[...] = x[odd + q * (1 - 2 * odd), pl.ds(start, TALL), :]
        convolve(pads.at[q], w, wn, wk, wr, out, sides.at[q])
    away = pl.multiple_of((TALL - 2 * COLS) * (1 - odd), COLS)
    x2[...] = x[1 - odd, pl.ds(away, TALL), :]


def prepare(at, cot, tw, c3, c2, cot0, cot1, vt, vtk, vb, vbk):
    odd = at[0]
    here, there = pl.multiple_of(PX * odd, PX), pl.multiple_of(PX * (1 - odd), PX)
    c3[...] = cot[odd, pl.ds(there, PX), :]
    c2[...] = cot[1 - odd, pl.ds(there, PX), :]
    cot0[...] = cot[odd, pl.ds(here, PX), :]
    cot1[...] = cot[1 - odd, pl.ds(here, PX), :]
    for l in range(2):
        for k in range(3):
            value = tw[l, tap(k, odd)]
            turned = value.T
            vt[l, k] = value
            vb[l, k] = turned
            vtk[l, pl.ds(TAIL * k, TAIL), :] = value[HEAD:, :]
            vbk[l, pl.ds(TAIL * k, TAIL), :] = turned[HEAD:, :]


def conv_other(at, x, w, wn, wk, wr, out, sides, pad):
    padded(pad, at[0])[...] = x[...]
    convolve(pad, w, wn, wk, wr, out, sides)


def tap(k, odd):
    return k + odd * (2 - 2 * k)


def three_taps(three, vw, layer, wk):
    tails = side(*[ref[:, pl.ds(HEAD, TAIL)] for ref in three])
    totals = []
    for columns in (pl.ds(0, HEAD), pl.ds(HEAD, TAIL)):
        total = dot(three[0][:, pl.ds(0, HEAD)], vw[layer, 0, pl.ds(0, HEAD), columns])
        total = total + dot(three[1][:, pl.ds(0, HEAD)], vw[layer, 1, pl.ds(0, HEAD), columns])
        total = total + dot(three[2][:, pl.ds(0, HEAD)], vw[layer, 2, pl.ds(0, HEAD), columns])
        totals.append(total + dot(tails, wk[layer, :, columns]))
    return side(*totals)


def temporal(states, vw, layer, wk, acts):
    done = 0
    for q in range(4):
        while done < q + 3:
            v = states[done][...].astype(F32)
            acts[done] = (v * sigmoid(v)).astype(BF)
            done += 1
        term = three_taps([acts.at[q + k] for k in range(3)], vw, layer, wk)
        yield (states[q + 1][...].astype(F32) + term).astype(BF)


def layer_one(at, left, s0, s1, s2, s3, right, vw, wk, acts, state, last, first):
    states = (left, s0, s1, s2, s3, right)
    for q, value in enumerate(temporal(states, vw, 0, wk, acts)):
        state[q] = value
        if q == 0:
            first[...] = value
        if q == 3:
            last[...] = value


def layer_two(at, left, state, right, vw, wk, acts, own, sent):
    states = (left, state.at[0], state.at[1], state.at[2], state.at[3], right)
    for q, value in enumerate(temporal(states, vw, 1, wk, acts)):
        if q < 2:
            own[q] = value
        else:
            sent[pl.ds((3 - q) * PX, PX), :] = value


def descend(six, q, before, vw, layer, wk):
    three = [six[q + 2 - k] for k in range(3)]
    carried = three_taps(three, vw, layer, wk)
    v = before[...].astype(F32)
    s = sigmoid(v)
    return (three[1][...].astype(F32) + carried * (s * (1.0 + v * (1.0 - s)))).astype(BF)


def back_one(at, left, cot0, cot1, c2, c3, right, state, vw, wk, back, first, last):
    six = (left, cot0, cot1, c2, c3, right)
    for q in range(4):
        value = descend(six, q, state.at[q], vw, 1, wk)
        back[q] = value
        if q == 0:
            first[...] = value
        if q == 3:
            last[...] = value


def temporal_grads(at, cot0, cot1, c2, c3, acts2, back, acts1, blocks, flip):
    odd = at[0]
    views = (cot0, cot1, c2, c3)
    for layer, acts in ((0, acts1), (1, acts2)):
        for q in range(4):
            up = back.at[q] if layer == 0 else views[q]
            flip[:, pl.ds(q * PX, PX)] = up[...].T
        tails = jnp.zeros((C, THREE_TAILS), F32)
        for q in range(4):
            ends = side(*[acts[q + tap(k, odd), :, pl.ds(HEAD, TAIL)] for k in range(3)])
            tails = tails + dot(flip[:, pl.ds(q * PX, PX)], ends)
        values = []
        for k in range(3):
            total = jnp.zeros((C, HEAD), F32)
            for q in range(4):
                heads = acts[q + tap(k, odd), :, pl.ds(0, HEAD)]
                total = total + dot(flip[:, pl.ds(q * PX, PX)], heads)
            values.append(side(total, tails[:, k * TAIL : (k + 1) * TAIL]).astype(BF))
        for b in range(CLIPS):
            blocks[b, layer] = side(*[v[:, b * WIDTH : (b + 1) * WIDTH] for v in values])


def back_zero(at, left, back, right, s0, s1, s2, s3, vw, wk, own_sides, sides2, sides3, passing, kept, sent, flip):
    core = at[1]
    six = [left] + [back.at[q] for q in range(4)] + [right]
    column = lax.broadcasted_iota(jnp.int32, (1, PX), 1) % COLS
    for q, before in enumerate((s0, s1, s2, s3)):
        turned = descend(six, q, before, vw, 0, wk).T
        wide = turned.astype(F32)
        ahead = jnp.where(column == COLS - 1, 0.0, pltpu.roll(wide, PX - 1, 1))
        behind = jnp.where(column == 0, 0.0, pltpu.roll(wide, 1, 1))
        flip[q, pl.ds(0, C), :] = ahead.astype(BF)
        flip[q, pl.ds(C, C), :] = turned
        flip[q, pl.ds(2 * C, C), :] = behind.astype(BF)
    sides = (own_sides.at[0], own_sides.at[1], sides2, sides3)
    for half in range(2):
        for out, b in ((kept, 2 * half + core), (sent, 2 * half + 1 - core)):
            total = jnp.zeros((3 * C, 3 * WIDTH), F32)
            for q in range(4):
                total = total + dot(flip[q], sides[q][b])
            for j in range(3):
                out[half, j] = total[j * C : (j + 1) * C].astype(BF)
            for layer in range(2):
                out[half, 3 + layer] = passing[b, layer]


def pack(at, kept, got, out, wide, rows, vout, sems):
    halves, taps, channels, _ = kept.shape
    owners = out.shape[0] // halves
    count = channels // owners
    move = Mover(sems)
    for h in range(halves):
        for t in range(taps):
            rows[...] = kept[h, t].astype(F32) + got[h, t].astype(F32)
            for owner in range(owners):
                wide[owner, pl.ds(count * t, count), :] = rows[pl.ds(count * owner, count), :]
        for owner in range(owners):
            vout[owners * h + owner] = wide[owner].astype(BF)
        move.put(vout.at[pl.ds(owners * h, owners)], out.at[pl.ds(owners * h, owners)])
    move.finish()


def place(at, own, got, out, sems):
    odd = at[0]
    move = Mover(sems)
    here, there = pl.multiple_of(PX * odd, PX), pl.multiple_of(PX * (1 - odd), PX)
    for q, frame in enumerate((odd, 1 - odd)):
        move.put(own.at[q], out.at[frame, pl.ds(here, PX), :])
        move.put(nth(got, q), out.at[frame, pl.ds(there, PX), :])
    move.finish()


def after(value, *others):
    return lax.optimization_barrier((value, *others))[0]


def step(clips_in, cotangent, spatial_weight, temporal_weight):
    owners, clips = lax.axis_size("frame"), lax.axis_size("clip")
    odd = lax.axis_index("frame") % 2
    core = lax.axis_index("clip") % 2
    at = jnp.stack([odd, core]).astype(jnp.int32)
    swap = [(n, n ^ 1) for n in range(owners)]
    outer = [(n, n - 2 if n % 2 == 0 else n + 2) for n in range(owners)]
    outer = [(a, b) for a, b in outer if 0 <= b < owners]
    inner = [(n, n + 2 if n % 2 == 0 else n - 2) for n in range(owners)]
    inner = [(a, b) for a, b in inner if 0 <= b < owners]
    cores = [(n, n ^ 1) for n in range(clips)]

    def send(value, perm, axis="frame"):
        shape = value.shape
        if axis == "frame":
            value = value.reshape(-1, COLS, C)
        return lax.ppermute(value, axis, perm).reshape(shape)

    x = clips_in.reshape(2, FULL, C)
    cot = cotangent.reshape(2, FULL, C)
    ws = spatial_weight.reshape(9, C, C)
    flops = 2 * PX * C * C

    flat, two, four, six = (2 * PX, C), (2, PX, C), (4, PX, C), (6, PX, C)
    packed = [(3, HEAD, THREE_TAILS), (3, THREE_TAILS, HEAD), (THREE_TAILS, THREE_TAILS)]
    taps = [(2, *KERNELS), (2, THREE_TAILS, C)]
    pad = (PX + 2 * COLS, C)

    tall_start = (TALL - 2 * COLS) * (1 - odd)
    x3 = send(lax.dynamic_slice(x, (odd, tall_start, 0), (1, TALL, C))[0], swap)
    s0, s1, own_sides, x2, wn, wk, wr = run(
        conv_own,
        [ONE, ONE, (2, *SIDES), TALL_ONE, *packed],
        (at, x, ws),
        [(2, *pad)],
        flops=8 * flops,
    )
    wp = (ws, wn, wk, wr)
    right = send(s0, outer)
    x2 = send(x2, swap)
    c3, c2, cot0, cot1, vt, vtk, vb, vbk = run(
        prepare, [ONE] * 4 + taps * 2, (at, after(cot, s0), after(temporal_weight, s0)), flops=flops
    )

    s3, sides3 = run(conv_other, [ONE, SIDES], (at, x3, *wp), [pad], 0, 4 * flops)
    left = send(s3, inner)
    c3 = send(after(c3, x2), swap)
    s2, sides2 = run(conv_other, [ONE, SIDES], (at, x2, *wp), [pad], 0, 4 * flops)
    c2 = send(after(c2, c3), swap)
    cot_right = send(after(cot0, right), outer)
    cot_left = send(c3, inner)

    acts1, state1, last, first = run(
        layer_one,
        [six, four, ONE, ONE],
        (at, left, s0, s1, s2, s3, right, vt, vtk),
        flops=8 * flops,
    )
    left1 = send(last, inner)
    right1 = send(first, outer)
    back1, first, last = run(
        back_one,
        [four, ONE, ONE],
        (at, cot_left, cot0, cot1, c2, c3, cot_right, state1, vb, vbk),
        flops=8 * flops,
    )
    back_left = send(last, inner)
    back_right = send(first, outer)
    acts2, own, sent = run(
        layer_two, [six, two, flat], (at, left1, state1, right1, vt, vtk), flops=8 * flops
    )
    returned = send(sent, swap)

    (temporal_blocks,) = run(
        temporal_grads,
        [(CLIPS, 2, C, 3 * WIDTH)],
        (at, cot0, cot1, c2, c3, acts2, back1, acts1),
        [(C, 4 * PX)],
        flops=16 * flops,
    )
    shares = (2, 5, C, 3 * WIDTH)
    kept, sent = run(
        back_zero,
        [shares] * 2,
        (at, back_left, back1, back_right, s0, s1, s2, s3, vb, vbk, own_sides, sides2, sides3, temporal_blocks),
        [(4, 3 * C, PX)],
        flops=32 * flops,
    )
    got = send(sent, cores, "clip")
    (out,) = run(place, [(2, FULL, C)], (at, own, returned), (), 4, 1000, far_outs=True)

    rows = C // owners
    block = (2 * owners, 5 * rows, 3 * WIDTH)
    (packs,) = run(
        pack,
        [block],
        (at, kept, got),
        [pltpu.VMEM((owners, 5 * rows, 3 * WIDTH), F32), pltpu.VMEM((C, 3 * WIDTH), F32), block],
        4,
        1000,
        far_outs=True,
    )
    groups = [[n + half * 2 + c for half in range(2) for n in range(0, owners * clips, clips)] for c in range(2)]
    parts = lax.all_to_all(
        packs, ("frame", "clip"), split_axis=0, concat_axis=0, axis_index_groups=groups, tiled=True
    )
    total = jnp.sum(parts.astype(F32), axis=0).reshape(5, rows, 3, WIDTH)
    grad_spatial = total[:3].transpose(1, 2, 0, 3)
    grad_temporal = total[3:].transpose(1, 0, 2, 3)
    return (out.reshape(clips_in.shape), grad_spatial, grad_temporal)


def solution(mesh):
    placed = (P("clip", "frame", None, None, None), P("clip", "frame", None, None, None), P(), P())
    return jax.shard_map(
        step,
        mesh=mesh,
        in_specs=placed,
        out_specs=(
            P("clip", "frame", None, None, None),
            P("frame", None, None, "clip"),
            P("frame", None, None, "clip"),
        ),
        check_vma=False,
    )
```

```python
import functools

import jax
import jax.numpy as jnp
from jax import lax
from jax.experimental import pallas as pl
from jax.experimental.pallas import tpu as pltpu
from jax.sharding import PartitionSpec as P


BF = jnp.bfloat16
F32 = jnp.float32
C = 320
COLS = 32
ROWS = 16
PX = ROWS * COLS
TALL = PX + COLS
FULL = 2 * PX
HEAD = 256
TAIL = C - HEAD
CLIPS = 4
VMEM_BYTES = 24 * 1024 * 1024
WIDTH = C // CLIPS
HBM = pl.BlockSpec(memory_space=pltpu.HBM)
VM = pl.BlockSpec(memory_space=pltpu.VMEM)
SM = pl.BlockSpec(memory_space=pltpu.SMEM)


ONE = (PX, C)
TALL_ONE = (TALL, C)
THREE_TAILS = 3 * TAIL
SIDES = (CLIPS, PX, 3 * WIDTH)
KERNELS = (3, C, C)


def dot(a, b):
    return jnp.dot(a, b, preferred_element_type=F32)


def side(*parts):
    return jnp.concatenate(parts, axis=1)


class Mover:
    def __init__(self, sems):
        self.sems, self.count, self.leaving = sems, 0, []

    def copy(self, src, dst):
        c = pltpu.make_async_copy(src, dst, self.sems.at[self.count])
        self.count += 1
        c.start()
        return c

    def fetch(self, src, dst):
        return Arrival(self.copy(src, dst), dst)

    def put(self, src, dst):
        self.leaving.append(self.copy(src, dst))

    def finish(self):
        for c in self.leaving:
            c.wait()


class Arrival:
    def __init__(self, copy, ref):
        self.copy, self.ref = copy, ref

    def get(self):
        if self.copy is not None:
            self.copy.wait()
            self.copy = None
        return self.ref


def nth(ref, n):
    return ref.at[pl.ds(n * PX, PX), :]


def run(kernel, outs, args, scratch=(), copies=0, flops=0, far=(), far_outs=False, out_kind=None):
    nbytes = sum(a.size * a.dtype.itemsize for a in args) + sum(
        functools.reduce(lambda m, n: m * n, s, 2) for s in outs
    )
    kind = BF if out_kind is None else out_kind
    return pl.pallas_call(
        kernel,
        out_shape=[jax.ShapeDtypeStruct(s, kind) for s in outs],
        in_specs=[SM] + [HBM if n in far else VM for n in range(1, len(args))],
        out_specs=[HBM if far_outs else VM] * len(outs),
        scratch_shapes=[s if not isinstance(s, tuple) else pltpu.VMEM(s, BF) for s in scratch]
        + ([pltpu.SemaphoreType.DMA((copies,))] if copies else []),
        cost_estimate=pl.CostEstimate(flops=flops, bytes_accessed=nbytes, transcendentals=0),
        compiler_params=pltpu.CompilerParams(vmem_limit_bytes=VMEM_BYTES),
    )(*args)


def column_of(rows):
    return lax.broadcasted_iota(jnp.int32, (rows, 1), 0) % COLS


def right_by_one(v):
    return jnp.where(column_of(v.shape[0]) == 0, 0.0, pltpu.roll(v, 1, 0))


def left_by_one(v):
    return jnp.where(column_of(v.shape[0]) == COLS - 1, 0.0, pltpu.roll(v, v.shape[0] - 1, 0))


def sigmoid(v):
    return 1.0 / (1.0 + jnp.exp(-v))


def padded(pad, odd):
    pad[pl.ds(0, COLS), :] = jnp.zeros((COLS, C), BF)
    pad[pl.ds(TALL, COLS), :] = jnp.zeros((COLS, C), BF)
    return pad.at[pl.ds(pl.multiple_of(COLS * (1 - odd), COLS), TALL), :]


def convolve(pad, w, wn, wk, wr, out, sides):
    tails = side(*[pad[pl.ds(COLS * i, PX), pl.ds(HEAD, TAIL)] for i in range(3)])

    def heads(i):
        return pad[pl.ds(COLS * i, PX), pl.ds(0, HEAD)]

    parts = []
    for j in range(3):
        acc = dot(heads(0), w[j, pl.ds(0, HEAD), pl.ds(0, HEAD)])
        acc = acc + dot(heads(1), w[3 + j, pl.ds(0, HEAD), pl.ds(0, HEAD)])
        acc = acc + dot(heads(2), w[6 + j, pl.ds(0, HEAD), pl.ds(0, HEAD)])
        parts.append(acc + dot(tails, wk[j]))
    centre = pad[pl.ds(COLS, PX), pl.ds(0, HEAD)].astype(F32)
    total = right_by_one(parts[0]) + parts[1] + left_by_one(parts[2])
    out[:, pl.ds(0, HEAD)] = (centre + total).astype(BF)
    acc = dot(heads(0), wn[0]) + dot(heads(1), wn[1]) + dot(heads(2), wn[2])
    acc = acc + dot(tails, wr[...])
    total = right_by_one(acc[:, :TAIL]) + acc[:, TAIL : 2 * TAIL] + left_by_one(acc[:, 2 * TAIL :])
    centre = pad[pl.ds(COLS, PX), pl.ds(HEAD, TAIL)].astype(F32)
    out[:, pl.ds(HEAD, TAIL)] = (centre + total).astype(BF)
    for b in range(CLIPS):
        columns = slice(b * WIDTH, (b + 1) * WIDTH)
        sides[b] = side(*[pad[pl.ds(COLS * i, PX), columns] for i in range(3)])


def conv_own(at, x, w, out0, out1, sides, x2, wn, wk, wr, pads):
    odd = at[0]
    for i in range(3):
        wn[i] = side(*[w[3 * i + j, pl.ds(0, HEAD), pl.ds(HEAD, TAIL)] for j in range(3)])
        for j in range(3):
            wk[j, pl.ds(TAIL * i, TAIL), :] = w[3 * i + j, pl.ds(HEAD, TAIL), pl.ds(0, HEAD)]
        wr[pl.ds(TAIL * i, TAIL), :] = side(
            *[w[3 * i + j, pl.ds(HEAD, TAIL), pl.ds(HEAD, TAIL)] for j in range(3)]
        )
    start = pl.multiple_of((TALL - 2 * COLS) * odd, COLS)
    for q, out in enumerate((out0, out1)):
        padded(pads.at[q], odd)[...] = x[odd + q * (1 - 2 * odd), pl.ds(start, TALL), :]
        convolve(pads.at[q], w, wn, wk, wr, out, sides.at[q])
    away = pl.multiple_of((TALL - 2 * COLS) * (1 - odd), COLS)
    x2[...] = x[1 - odd, pl.ds(away, TALL), :]


def prepare(at, cot, tw, c3, c2, cot0, cot1, vt, vtk, vb, vbk):
    odd = at[0]
    here, there = pl.multiple_of(PX * odd, PX), pl.multiple_of(PX * (1 - odd), PX)
    c3[...] = cot[odd, pl.ds(there, PX), :]
    c2[...] = cot[1 - odd, pl.ds(there, PX), :]
    cot0[...] = cot[odd, pl.ds(here, PX), :]
    cot1[...] = cot[1 - odd, pl.ds(here, PX), :]
    for l in range(2):
        for k in range(3):
            value = tw[l, tap(k, odd)]
            turned = value.T
            vt[l, k] = value
            vb[l, k] = turned
            vtk[l, pl.ds(TAIL * k, TAIL), :] = value[HEAD:, :]
            vbk[l, pl.ds(TAIL * k, TAIL), :] = turned[HEAD:, :]


def conv_other(at, x, w, wn, wk, wr, out, sides, pad):
    padded(pad, at[0])[...] = x[...]
    convolve(pad, w, wn, wk, wr, out, sides)


def tap(k, odd):
    return k + odd * (2 - 2 * k)


def three_taps(three, vw, layer, wk):
    tails = side(*[ref[:, pl.ds(HEAD, TAIL)] for ref in three])
    totals = []
    for columns in (pl.ds(0, HEAD), pl.ds(HEAD, TAIL)):
        total = dot(three[0][:, pl.ds(0, HEAD)], vw[layer, 0, pl.ds(0, HEAD), columns])
        total = total + dot(three[1][:, pl.ds(0, HEAD)], vw[layer, 1, pl.ds(0, HEAD), columns])
        total = total + dot(three[2][:, pl.ds(0, HEAD)], vw[layer, 2, pl.ds(0, HEAD), columns])
        totals.append(total + dot(tails, wk[layer, :, columns]))
    return side(*totals)


def temporal(states, vw, layer, wk, acts):
    done = 0
    for q in range(4):
        while done < q + 3:
            v = states[done][...].astype(F32)
            acts[done] = (v * sigmoid(v)).astype(BF)
            done += 1
        term = three_taps([acts.at[q + k] for k in range(3)], vw, layer, wk)
        yield (states[q + 1][...].astype(F32) + term).astype(BF)


def layer_one(at, left, s0, s1, s2, s3, right, vw, wk, acts, state, last, first):
    states = (left, s0, s1, s2, s3, right)
    for q, value in enumerate(temporal(states, vw, 0, wk, acts)):
        state[q] = value
        if q == 0:
            first[...] = value
        if q == 3:
            last[...] = value


def layer_two(at, left, state, right, vw, wk, acts, own, sent):
    states = (left, state.at[0], state.at[1], state.at[2], state.at[3], right)
    for q, value in enumerate(temporal(states, vw, 1, wk, acts)):
        if q < 2:
            own[q] = value
        else:
            sent[pl.ds((3 - q) * PX, PX), :] = value


def descend(six, q, before, vw, layer, wk):
    three = [six[q + 2 - k] for k in range(3)]
    carried = three_taps(three, vw, layer, wk)
    v = before[...].astype(F32)
    s = sigmoid(v)
    return (three[1][...].astype(F32) + carried * (s * (1.0 + v * (1.0 - s)))).astype(BF)


def back_one(at, left, cot0, cot1, c2, c3, right, state, vw, wk, back, first, last):
    six = (left, cot0, cot1, c2, c3, right)
    for q in range(4):
        value = descend(six, q, state.at[q], vw, 1, wk)
        back[q] = value
        if q == 0:
            first[...] = value
        if q == 3:
            last[...] = value


def temporal_grads(at, cot0, cot1, c2, c3, acts2, back, acts1, blocks, flip):
    odd = at[0]
    views = (cot0, cot1, c2, c3)
    for layer, acts in ((0, acts1), (1, acts2)):
        for q in range(4):
            up = back.at[q] if layer == 0 else views[q]
            flip[:, pl.ds(q * PX, PX)] = up[...].T
        tails = jnp.zeros((C, THREE_TAILS), F32)
        for q in range(4):
            ends = side(*[acts[q + tap(k, odd), :, pl.ds(HEAD, TAIL)] for k in range(3)])
            tails = tails + dot(flip[:, pl.ds(q * PX, PX)], ends)
        values = []
        for k in range(3):
            total = jnp.zeros((C, HEAD), F32)
            for q in range(4):
                heads = acts[q + tap(k, odd), :, pl.ds(0, HEAD)]
                total = total + dot(flip[:, pl.ds(q * PX, PX)], heads)
            values.append(side(total, tails[:, k * TAIL : (k + 1) * TAIL]).astype(BF))
        for b in range(CLIPS):
            blocks[b, layer] = side(*[v[:, b * WIDTH : (b + 1) * WIDTH] for v in values])


def back_zero(at, left, back, right, s0, s1, s2, s3, vw, wk, own_sides, sides2, sides3, passing, kept, sent, flip):
    core = at[1]
    six = [left] + [back.at[q] for q in range(4)] + [right]
    column = lax.broadcasted_iota(jnp.int32, (1, PX), 1) % COLS
    for q, before in enumerate((s0, s1, s2, s3)):
        turned = descend(six, q, before, vw, 0, wk).T
        wide = turned.astype(F32)
        ahead = jnp.where(column == COLS - 1, 0.0, pltpu.roll(wide, PX - 1, 1))
        behind = jnp.where(column == 0, 0.0, pltpu.roll(wide, 1, 1))
        flip[q, pl.ds(0, C), :] = ahead.astype(BF)
        flip[q, pl.ds(C, C), :] = turned
        flip[q, pl.ds(2 * C, C), :] = behind.astype(BF)
    sides = (own_sides.at[0], own_sides.at[1], sides2, sides3)
    for half in range(2):
        for out, b in ((kept, 2 * half + core), (sent, 2 * half + 1 - core)):
            total = jnp.zeros((3 * C, 3 * WIDTH), F32)
            for q in range(4):
                total = total + dot(flip[q], sides[q][b])
            for j in range(3):
                out[half, j] = total[j * C : (j + 1) * C].astype(BF)
            for layer in range(2):
                out[half, 3 + layer] = passing[b, layer]


def pack(at, kept, got, out, wide, rows):
    halves, taps, channels, _ = kept.shape
    owners = out.shape[0]
    count = channels // owners
    for h in range(halves):
        for t in range(taps):
            rows[...] = kept[h, t].astype(F32) + got[h, t].astype(F32)
            for owner in range(owners):
                block = pl.ds(count * (taps * h + t), count)
                wide[owner, block, :] = rows[pl.ds(count * owner, count), :]
    for owner in range(owners):
        out[owner] = wide[owner].astype(BF)


def gather_parts(at, parts, mine, theirs):
    total = parts[0].astype(F32)
    for n in range(1, parts.shape[0]):
        total = total + parts[n].astype(F32)
    count = mine.shape[0]
    upper = at[2] == 1
    mine[...] = jnp.where(upper, total[count:], total[:count])
    theirs[...] = jnp.where(upper, total[:count], total[count:])


def place(at, own, got, out, sems):
    odd = at[0]
    move = Mover(sems)
    here, there = pl.multiple_of(PX * odd, PX), pl.multiple_of(PX * (1 - odd), PX)
    for q, frame in enumerate((odd, 1 - odd)):
        move.put(own.at[q], out.at[frame, pl.ds(here, PX), :])
        move.put(nth(got, q), out.at[frame, pl.ds(there, PX), :])
    move.finish()


def after(value, *others):
    return lax.optimization_barrier((value, *others))[0]


def step(clips_in, cotangent, spatial_weight, temporal_weight):
    owners, clips = lax.axis_size("frame"), lax.axis_size("clip")
    odd = lax.axis_index("frame") % 2
    core = lax.axis_index("clip") % 2
    at = jnp.stack([odd, core, lax.axis_index("clip") // 2]).astype(jnp.int32)
    swap = [(n, n ^ 1) for n in range(owners)]
    outer = [(n, n - 2 if n % 2 == 0 else n + 2) for n in range(owners)]
    outer = [(a, b) for a, b in outer if 0 <= b < owners]
    inner = [(n, n + 2 if n % 2 == 0 else n - 2) for n in range(owners)]
    inner = [(a, b) for a, b in inner if 0 <= b < owners]
    cores = [(n, n ^ 1) for n in range(clips)]

    def send(value, perm, axis="frame"):
        shape = value.shape
        if axis == "frame":
            value = value.reshape(-1, COLS, C)
        return lax.ppermute(value, axis, perm).reshape(shape)

    x = clips_in.reshape(2, FULL, C)
    cot = cotangent.reshape(2, FULL, C)
    ws = spatial_weight.reshape(9, C, C)
    flops = 2 * PX * C * C

    flat, two, four, six = (2 * PX, C), (2, PX, C), (4, PX, C), (6, PX, C)
    packed = [(3, HEAD, THREE_TAILS), (3, THREE_TAILS, HEAD), (THREE_TAILS, THREE_TAILS)]
    taps = [(2, *KERNELS), (2, THREE_TAILS, C)]
    pad = (PX + 2 * COLS, C)

    tall_start = (TALL - 2 * COLS) * (1 - odd)
    x3 = send(lax.dynamic_slice(x, (odd, tall_start, 0), (1, TALL, C))[0], swap)
    s0, s1, own_sides, x2, wn, wk, wr = run(
        conv_own,
        [ONE, ONE, (2, *SIDES), TALL_ONE, *packed],
        (at, x, ws),
        [(2, *pad)],
        flops=8 * flops,
    )
    wp = (ws, wn, wk, wr)
    right = send(s0, outer)
    x2 = send(x2, swap)
    c3, c2, cot0, cot1, vt, vtk, vb, vbk = run(
        prepare, [ONE] * 4 + taps * 2, (at, after(cot, s0), after(temporal_weight, s0)), flops=flops
    )

    s3, sides3 = run(conv_other, [ONE, SIDES], (at, x3, *wp), [pad], 0, 4 * flops)
    left = send(s3, inner)
    c3 = send(after(c3, x2), swap)
    s2, sides2 = run(conv_other, [ONE, SIDES], (at, x2, *wp), [pad], 0, 4 * flops)
    c2 = send(after(c2, c3), swap)
    cot_right = send(after(cot0, right), outer)
    cot_left = send(c3, inner)

    acts1, state1, last, first = run(
        layer_one,
        [six, four, ONE, ONE],
        (at, left, s0, s1, s2, s3, right, vt, vtk),
        flops=8 * flops,
    )
    left1 = send(last, inner)
    right1 = send(first, outer)
    back1, first, last = run(
        back_one,
        [four, ONE, ONE],
        (at, cot_left, cot0, cot1, c2, c3, cot_right, state1, vb, vbk),
        flops=8 * flops,
    )
    back_left = send(last, inner)
    back_right = send(first, outer)
    acts2, own, sent = run(
        layer_two, [six, two, flat], (at, left1, state1, right1, vt, vtk), flops=8 * flops
    )
    returned = send(sent, swap)

    (temporal_blocks,) = run(
        temporal_grads,
        [(CLIPS, 2, C, 3 * WIDTH)],
        (at, cot0, cot1, c2, c3, acts2, back1, acts1),
        [(C, 4 * PX)],
        flops=16 * flops,
    )
    shares = (2, 5, C, 3 * WIDTH)
    kept, sent = run(
        back_zero,
        [shares] * 2,
        (at, back_left, back1, back_right, s0, s1, s2, s3, vb, vbk, own_sides, sides2, sides3, temporal_blocks),
        [(4, 3 * C, PX)],
        flops=32 * flops,
    )
    got = send(sent, cores, "clip")
    (out,) = run(place, [(2, FULL, C)], (at, own, returned), (), 4, 1000, far_outs=True)

    rows = C // owners
    block = (owners, 10 * rows, 3 * WIDTH)
    (packs,) = run(
        pack, [block], (at, kept, got), [pltpu.VMEM(block, F32), pltpu.VMEM((C, 3 * WIDTH), F32)], flops=1000
    )
    parts = lax.all_to_all(packs, "frame", split_axis=0, concat_axis=0, tiled=True)
    mine, theirs = run(gather_parts, [(5 * rows, 3 * WIDTH)] * 2, (at, parts), flops=1000, out_kind=F32)
    halves = [(n, n ^ 2) for n in range(clips)]
    total = (mine + send(theirs, halves, "clip")).reshape(5, rows, 3, WIDTH)
    grad_spatial = total[:3].transpose(1, 2, 0, 3)
    grad_temporal = total[3:].transpose(1, 0, 2, 3)
    return (out.reshape(clips_in.shape), grad_spatial, grad_temporal)


def solution(mesh):
    placed = (P("clip", "frame", None, None, None), P("clip", "frame", None, None, None), P(), P())
    return jax.shard_map(
        step,
        mesh=mesh,
        in_specs=placed,
        out_specs=(
            P("clip", "frame", None, None, None),
            P("frame", None, None, "clip"),
            P("frame", None, None, "clip"),
        ),
        check_vma=False,
    )
```

```python
import functools

import jax
import jax.numpy as jnp
from jax import lax
from jax.experimental import pallas as pl
from jax.experimental.pallas import tpu as pltpu
from jax.sharding import PartitionSpec as P


BF = jnp.bfloat16
F32 = jnp.float32
C = 320
COLS = 32
ROWS = 16
PX = ROWS * COLS
TALL = PX + COLS
FULL = 2 * PX
HEAD = 256
TAIL = C - HEAD
CLIPS = 4
LANES = 128
VMEM_BYTES = 24 * 1024 * 1024
WIDTH = C // CLIPS
HBM = pl.BlockSpec(memory_space=pltpu.HBM)
VM = pl.BlockSpec(memory_space=pltpu.VMEM)
SM = pl.BlockSpec(memory_space=pltpu.SMEM)


ONE = (PX, C)
THREE_TAILS = 3 * TAIL
SIDES = (CLIPS, PX, 3 * WIDTH)
KERNELS = (3, C, C)


def dot(a, b):
    return jnp.dot(a, b, preferred_element_type=F32)


def side(*parts):
    return jnp.concatenate(parts, axis=1)


class Mover:
    def __init__(self, sems):
        self.sems, self.count, self.leaving = sems, 0, []

    def copy(self, src, dst):
        c = pltpu.make_async_copy(src, dst, self.sems.at[self.count])
        self.count += 1
        c.start()
        return c

    def fetch(self, src, dst):
        return Arrival(self.copy(src, dst), dst)

    def put(self, src, dst):
        self.leaving.append(self.copy(src, dst))

    def finish(self):
        for c in self.leaving:
            c.wait()


class Arrival:
    def __init__(self, copy, ref):
        self.copy, self.ref = copy, ref

    def get(self):
        if self.copy is not None:
            self.copy.wait()
            self.copy = None
        return self.ref


def nth(ref, n):
    return ref.at[pl.ds(n * PX, PX), :]


def run(kernel, outs, args, scratch=(), copies=0, flops=0, far=(), far_outs=False):
    nbytes = sum(a.size * a.dtype.itemsize for a in args) + sum(
        functools.reduce(lambda m, n: m * n, s, 2) for s in outs
    )
    return pl.pallas_call(
        kernel,
        out_shape=[jax.ShapeDtypeStruct(s, BF) for s in outs],
        in_specs=[SM] + [HBM if n in far else VM for n in range(1, len(args))],
        out_specs=[HBM if far_outs else VM] * len(outs),
        scratch_shapes=[s if not isinstance(s, tuple) else pltpu.VMEM(s, BF) for s in scratch]
        + ([pltpu.SemaphoreType.DMA((copies,))] if copies else []),
        cost_estimate=pl.CostEstimate(flops=flops, bytes_accessed=nbytes, transcendentals=0),
        compiler_params=pltpu.CompilerParams(vmem_limit_bytes=VMEM_BYTES),
    )(*args)


def column_of(rows):
    return lax.broadcasted_iota(jnp.int32, (rows, 1), 0) % COLS


def right_by_one(v):
    return jnp.where(column_of(v.shape[0]) == 0, 0.0, pltpu.roll(v, 1, 0))


def left_by_one(v):
    return jnp.where(column_of(v.shape[0]) == COLS - 1, 0.0, pltpu.roll(v, v.shape[0] - 1, 0))


def sigmoid(v):
    return 1.0 / (1.0 + jnp.exp(-v))


def padded(pad, odd):
    pad[pl.ds(0, COLS), :] = jnp.zeros((COLS, C), BF)
    pad[pl.ds(TALL, COLS), :] = jnp.zeros((COLS, C), BF)
    return pad.at[pl.ds(pl.multiple_of(COLS * (1 - odd), COLS), TALL), :]


def fold(rows, dst):
    count = rows.shape[0]
    for n in range(2):
        dst[pl.ds(n * count, count), :] = rows[:, n * LANES : (n + 1) * LANES]
    half = count // 2
    dst[pl.ds(2 * count, half), :] = side(rows[:half, HEAD:], rows[half:, HEAD:])


def unfold(src, dst):
    count = dst.shape[0]
    for n in range(2):
        dst[:, pl.ds(n * LANES, LANES)] = src[pl.ds(n * count, count), :]
    half = count // 2
    for n in range(2):
        dst[pl.ds(n * half, half), pl.ds(HEAD, TAIL)] = src[pl.ds(2 * count, half), pl.ds(n * TAIL, TAIL)]


def convolve(pad, w, wn, wk, wr, out, sides):
    tails = side(*[pad[pl.ds(COLS * i, PX), pl.ds(HEAD, TAIL)] for i in range(3)])

    def heads(i):
        return pad[pl.ds(COLS * i, PX), pl.ds(0, HEAD)]

    parts = []
    for j in range(3):
        acc = dot(heads(0), w[j, pl.ds(0, HEAD), pl.ds(0, HEAD)])
        acc = acc + dot(heads(1), w[3 + j, pl.ds(0, HEAD), pl.ds(0, HEAD)])
        acc = acc + dot(heads(2), w[6 + j, pl.ds(0, HEAD), pl.ds(0, HEAD)])
        parts.append(acc + dot(tails, wk[j]))
    centre = pad[pl.ds(COLS, PX), pl.ds(0, HEAD)].astype(F32)
    total = right_by_one(parts[0]) + parts[1] + left_by_one(parts[2])
    out[:, pl.ds(0, HEAD)] = (centre + total).astype(BF)
    acc = dot(heads(0), wn[0]) + dot(heads(1), wn[1]) + dot(heads(2), wn[2])
    acc = acc + dot(tails, wr[...])
    total = right_by_one(acc[:, :TAIL]) + acc[:, TAIL : 2 * TAIL] + left_by_one(acc[:, 2 * TAIL :])
    centre = pad[pl.ds(COLS, PX), pl.ds(HEAD, TAIL)].astype(F32)
    out[:, pl.ds(HEAD, TAIL)] = (centre + total).astype(BF)
    for b in range(CLIPS):
        columns = slice(b * WIDTH, (b + 1) * WIDTH)
        sides[b] = side(*[pad[pl.ds(COLS * i, PX), columns] for i in range(3)])


def conv_own(at, x, w, out0, out1, sides, x2, wn, wk, wr, pads):
    odd = at[0]
    for i in range(3):
        wn[i] = side(*[w[3 * i + j, pl.ds(0, HEAD), pl.ds(HEAD, TAIL)] for j in range(3)])
        for j in range(3):
            wk[j, pl.ds(TAIL * i, TAIL), :] = w[3 * i + j, pl.ds(HEAD, TAIL), pl.ds(0, HEAD)]
        wr[pl.ds(TAIL * i, TAIL), :] = side(
            *[w[3 * i + j, pl.ds(HEAD, TAIL), pl.ds(HEAD, TAIL)] for j in range(3)]
        )
    start = pl.multiple_of((TALL - 2 * COLS) * odd, COLS)
    for q, out in enumerate((out0, out1)):
        padded(pads.at[q], odd)[...] = x[odd + q * (1 - 2 * odd), pl.ds(start, TALL), :]
        convolve(pads.at[q], w, wn, wk, wr, out, sides.at[q])
    away = pl.multiple_of((TALL - 2 * COLS) * (1 - odd), COLS)
    fold(x[1 - odd, pl.ds(away, TALL), :], x2)


def prepare(at, cot, tw, c3, c2, cot0, cot1, vt, vtk, vb, vbk):
    odd = at[0]
    here, there = pl.multiple_of(PX * odd, PX), pl.multiple_of(PX * (1 - odd), PX)
    fold(cot[odd, pl.ds(there, PX), :], c3)
    fold(cot[1 - odd, pl.ds(there, PX), :], c2)
    cot0[...] = cot[odd, pl.ds(here, PX), :]
    cot1[...] = cot[1 - odd, pl.ds(here, PX), :]
    for l in range(2):
        for k in range(3):
            value = tw[l, tap(k, odd)]
            turned = value.T
            vt[l, k] = value
            vb[l, k] = turned
            vtk[l, pl.ds(TAIL * k, TAIL), :] = value[HEAD:, :]
            vbk[l, pl.ds(TAIL * k, TAIL), :] = turned[HEAD:, :]


def conv_other(at, x, w, wn, wk, wr, out, sides, pad):
    padded(pad, at[0])[...] = x[...]
    convolve(pad, w, wn, wk, wr, out, sides)


def conv_folded(at, x, w, wn, wk, wr, out, sides, pad):
    unfold(x, padded(pad, at[0]))
    convolve(pad, w, wn, wk, wr, out, sides)


def tap(k, odd):
    return k + odd * (2 - 2 * k)


def three_taps(three, vw, layer, wk):
    tails = side(*[ref[:, pl.ds(HEAD, TAIL)] for ref in three])
    totals = []
    for columns in (pl.ds(0, HEAD), pl.ds(HEAD, TAIL)):
        total = dot(three[0][:, pl.ds(0, HEAD)], vw[layer, 0, pl.ds(0, HEAD), columns])
        total = total + dot(three[1][:, pl.ds(0, HEAD)], vw[layer, 1, pl.ds(0, HEAD), columns])
        total = total + dot(three[2][:, pl.ds(0, HEAD)], vw[layer, 2, pl.ds(0, HEAD), columns])
        totals.append(total + dot(tails, wk[layer, :, columns]))
    return side(*totals)


def temporal(states, vw, layer, wk, acts):
    done = 0
    for q in range(4):
        while done < q + 3:
            v = states[done][...].astype(F32)
            acts[done] = (v * sigmoid(v)).astype(BF)
            done += 1
        term = three_taps([acts.at[q + k] for k in range(3)], vw, layer, wk)
        yield (states[q + 1][...].astype(F32) + term).astype(BF)


def layer_one(at, left, s0, s1, s2, s3, right, vw, wk, acts, state, last, first):
    states = (left, s0, s1, s2, s3, right)
    for q, value in enumerate(temporal(states, vw, 0, wk, acts)):
        state[q] = value
        if q == 0:
            first[...] = value
        if q == 3:
            last[...] = value


def layer_two(at, left, state, right, vw, wk, acts, own, sent):
    states = (left, state.at[0], state.at[1], state.at[2], state.at[3], right)
    for q, value in enumerate(temporal(states, vw, 1, wk, acts)):
        if q < 2:
            own[q] = value
        else:
            sent[pl.ds((3 - q) * PX, PX), :] = value


def descend(six, q, before, vw, layer, wk):
    three = [six[q + 2 - k] for k in range(3)]
    carried = three_taps(three, vw, layer, wk)
    v = before[...].astype(F32)
    s = sigmoid(v)
    return (three[1][...].astype(F32) + carried * (s * (1.0 + v * (1.0 - s)))).astype(BF)


def back_one(at, folded, cot0, cot1, folded2, folded3, right, state, vw, wk, back, first, last, c2, c3, left):
    unfold(folded, left)
    unfold(folded2, c2)
    unfold(folded3, c3)
    six = (left, cot0, cot1, c2, c3, right)
    for q in range(4):
        value = descend(six, q, state.at[q], vw, 1, wk)
        back[q] = value
        if q == 0:
            first[...] = value
        if q == 3:
            last[...] = value


def temporal_grads(at, cot0, cot1, c2, c3, acts2, back, acts1, blocks, flip):
    odd = at[0]
    views = (cot0, cot1, c2, c3)
    for layer, acts in ((0, acts1), (1, acts2)):
        for q in range(4):
            up = back.at[q] if layer == 0 else views[q]
            flip[:, pl.ds(q * PX, PX)] = up[...].T
        tails = jnp.zeros((C, THREE_TAILS), F32)
        for q in range(4):
            ends = side(*[acts[q + tap(k, odd), :, pl.ds(HEAD, TAIL)] for k in range(3)])
            tails = tails + dot(flip[:, pl.ds(q * PX, PX)], ends)
        values = []
        for k in range(3):
            total = jnp.zeros((C, HEAD), F32)
            for q in range(4):
                heads = acts[q + tap(k, odd), :, pl.ds(0, HEAD)]
                total = total + dot(flip[:, pl.ds(q * PX, PX)], heads)
            values.append(side(total, tails[:, k * TAIL : (k + 1) * TAIL]).astype(BF))
        for b in range(CLIPS):
            blocks[b, layer] = side(*[v[:, b * WIDTH : (b + 1) * WIDTH] for v in values])


def back_zero(at, left, back, right, s0, s1, s2, s3, vw, wk, own_sides, sides2, sides3, passing, kept, sent, flip):
    core = at[1]
    six = [left] + [back.at[q] for q in range(4)] + [right]
    column = lax.broadcasted_iota(jnp.int32, (1, PX), 1) % COLS
    for q, before in enumerate((s0, s1, s2, s3)):
        turned = descend(six, q, before, vw, 0, wk).T
        wide = turned.astype(F32)
        ahead = jnp.where(column == COLS - 1, 0.0, pltpu.roll(wide, PX - 1, 1))
        behind = jnp.where(column == 0, 0.0, pltpu.roll(wide, 1, 1))
        flip[q, pl.ds(0, C), :] = ahead.astype(BF)
        flip[q, pl.ds(C, C), :] = turned
        flip[q, pl.ds(2 * C, C), :] = behind.astype(BF)
    sides = (own_sides.at[0], own_sides.at[1], sides2, sides3)
    for half in range(2):
        for out, b in ((kept, 2 * half + core), (sent, 2 * half + 1 - core)):
            total = jnp.zeros((3 * C, 3 * WIDTH), F32)
            for q in range(4):
                total = total + dot(flip[q], sides[q][b])
            for j in range(3):
                out[half, j] = total[j * C : (j + 1) * C].astype(BF)
            for layer in range(2):
                out[half, 3 + layer] = passing[b, layer]


def pack(at, kept, got, out, wide, rows, vout, sems):
    halves, taps, channels, _ = kept.shape
    owners = out.shape[0] // halves
    count = channels // owners
    move = Mover(sems)
    for h in range(halves):
        for t in range(taps):
            rows[...] = kept[h, t].astype(F32) + got[h, t].astype(F32)
            for owner in range(owners):
                wide[owner, pl.ds(count * t, count), :] = rows[pl.ds(count * owner, count), :]
        for owner in range(owners):
            vout[owners * h + owner] = wide[owner].astype(BF)
        move.put(vout.at[pl.ds(owners * h, owners)], out.at[pl.ds(owners * h, owners)])
    move.finish()


def place(at, own, got, out, sems):
    odd = at[0]
    move = Mover(sems)
    here, there = pl.multiple_of(PX * odd, PX), pl.multiple_of(PX * (1 - odd), PX)
    for q, frame in enumerate((odd, 1 - odd)):
        move.put(own.at[q], out.at[frame, pl.ds(here, PX), :])
        move.put(nth(got, q), out.at[frame, pl.ds(there, PX), :])
    move.finish()


def after(value, *others):
    return lax.optimization_barrier((value, *others))[0]


def step(clips_in, cotangent, spatial_weight, temporal_weight):
    owners, clips = lax.axis_size("frame"), lax.axis_size("clip")
    odd = lax.axis_index("frame") % 2
    core = lax.axis_index("clip") % 2
    at = jnp.stack([odd, core]).astype(jnp.int32)
    swap = [(n, n ^ 1) for n in range(owners)]
    outer = [(n, n - 2 if n % 2 == 0 else n + 2) for n in range(owners)]
    outer = [(a, b) for a, b in outer if 0 <= b < owners]
    inner = [(n, n + 2 if n % 2 == 0 else n - 2) for n in range(owners)]
    inner = [(a, b) for a, b in inner if 0 <= b < owners]
    cores = [(n, n ^ 1) for n in range(clips)]

    def send(value, perm, axis="frame"):
        shape = value.shape
        if axis == "frame" and shape[-1] == C:
            value = value.reshape(-1, COLS, C)
        return lax.ppermute(value, axis, perm).reshape(shape)

    x = clips_in.reshape(2, FULL, C)
    cot = cotangent.reshape(2, FULL, C)
    ws = spatial_weight.reshape(9, C, C)
    flops = 2 * PX * C * C

    flat, two, four, six = (2 * PX, C), (2, PX, C), (4, PX, C), (6, PX, C)
    packed = [(3, HEAD, THREE_TAILS), (3, THREE_TAILS, HEAD), (THREE_TAILS, THREE_TAILS)]
    taps = [(2, *KERNELS), (2, THREE_TAILS, C)]
    pad = (PX + 2 * COLS, C)

    tall_start = (TALL - 2 * COLS) * (1 - odd)
    x3 = send(lax.dynamic_slice(x, (odd, tall_start, 0), (1, TALL, C))[0], swap)
    s0, s1, own_sides, x2, wn, wk, wr = run(
        conv_own,
        [ONE, ONE, (2, *SIDES), (TALL * C // LANES, LANES), *packed],
        (at, x, ws),
        [(2, *pad)],
        flops=8 * flops,
    )
    wp = (ws, wn, wk, wr)
    right = send(s0, outer)
    x2 = send(x2, swap)
    c3, c2, cot0, cot1, vt, vtk, vb, vbk = run(
        prepare, [(PX * C // LANES, LANES)] * 2 + [ONE] * 2 + taps * 2, (at, after(cot, s0), after(temporal_weight, s0)), flops=flops
    )

    s3, sides3 = run(conv_other, [ONE, SIDES], (at, x3, *wp), [pad], 0, 4 * flops)
    left = send(s3, inner)
    c3 = send(after(c3, x2), swap)
    s2, sides2 = run(conv_folded, [ONE, SIDES], (at, x2, *wp), [pad], 0, 4 * flops)
    c2 = send(after(c2, c3), swap)
    cot_right = send(after(cot0, right), outer)
    cot_left = send(c3, inner)

    acts1, state1, last, first = run(
        layer_one,
        [six, four, ONE, ONE],
        (at, left, s0, s1, s2, s3, right, vt, vtk),
        flops=8 * flops,
    )
    left1 = send(last, inner)
    right1 = send(first, outer)
    back1, first, last, u2, u3 = run(
        back_one,
        [four, ONE, ONE, ONE, ONE],
        (at, cot_left, cot0, cot1, c2, c3, cot_right, state1, vb, vbk),
        [ONE],
        flops=8 * flops,
    )
    back_left = send(last, inner)
    back_right = send(first, outer)
    acts2, own, sent = run(
        layer_two, [six, two, flat], (at, left1, state1, right1, vt, vtk), flops=8 * flops
    )
    returned = send(sent, swap)

    (temporal_blocks,) = run(
        temporal_grads,
        [(CLIPS, 2, C, 3 * WIDTH)],
        (at, cot0, cot1, u2, u3, acts2, back1, acts1),
        [(C, 4 * PX)],
        flops=16 * flops,
    )
    shares = (2, 5, C, 3 * WIDTH)
    kept, sent = run(
        back_zero,
        [shares] * 2,
        (at, back_left, back1, back_right, s0, s1, s2, s3, vb, vbk, own_sides, sides2, sides3, temporal_blocks),
        [(4, 3 * C, PX)],
        flops=32 * flops,
    )
    got = send(sent, cores, "clip")
    (out,) = run(place, [(2, FULL, C)], (at, own, returned), (), 4, 1000, far_outs=True)

    rows = C // owners
    block = (2 * owners, 5 * rows, 3 * WIDTH)
    (packs,) = run(
        pack,
        [block],
        (at, kept, got),
        [pltpu.VMEM((owners, 5 * rows, 3 * WIDTH), F32), pltpu.VMEM((C, 3 * WIDTH), F32), block],
        4,
        1000,
        far_outs=True,
    )
    groups = [[n + half * 2 + c for half in range(2) for n in range(0, owners * clips, clips)] for c in range(2)]
    parts = lax.all_to_all(packs, ("frame", "clip"), split_axis=0, concat_axis=0, axis_index_groups=groups, tiled=True)
    total = jnp.sum(parts.astype(F32), axis=0).reshape(5, rows, 3, WIDTH)
    grad_spatial = total[:3].transpose(1, 2, 0, 3)
    grad_temporal = total[3:].transpose(1, 0, 2, 3)
    return (out.reshape(clips_in.shape), grad_spatial, grad_temporal)


def solution(mesh):
    placed = (P("clip", "frame", None, None, None), P("clip", "frame", None, None, None), P(), P())
    return jax.shard_map(
        step,
        mesh=mesh,
        in_specs=placed,
        out_specs=(
            P("clip", "frame", None, None, None),
            P("frame", None, None, "clip"),
            P("frame", None, None, "clip"),
        ),
        check_vma=False,
    )
```

```python
import functools

import jax
import jax.numpy as jnp
from jax import lax
from jax.experimental import pallas as pl
from jax.experimental.pallas import tpu as pltpu
from jax.sharding import PartitionSpec as P


BF = jnp.bfloat16
F32 = jnp.float32
C = 320
COLS = 32
ROWS = 16
PX = ROWS * COLS
TALL = PX + COLS
FULL = 2 * PX
HEAD = 256
TAIL = C - HEAD
CLIPS = 4
LANES = 128
VMEM_BYTES = 24 * 1024 * 1024
WIDTH = C // CLIPS
HBM = pl.BlockSpec(memory_space=pltpu.HBM)
VM = pl.BlockSpec(memory_space=pltpu.VMEM)
SM = pl.BlockSpec(memory_space=pltpu.SMEM)


ONE = (PX, C)
THREE_TAILS = 3 * TAIL
FOLDED = PX * C // LANES
SIDES = (CLIPS, PX, 3 * WIDTH)
KERNELS = (3, C, C)


def dot(a, b):
    return jnp.dot(a, b, preferred_element_type=F32)


def side(*parts):
    return jnp.concatenate(parts, axis=1)


class Mover:
    def __init__(self, sems):
        self.sems, self.count, self.leaving = sems, 0, []

    def copy(self, src, dst):
        c = pltpu.make_async_copy(src, dst, self.sems.at[self.count])
        self.count += 1
        c.start()
        return c

    def fetch(self, src, dst):
        return Arrival(self.copy(src, dst), dst)

    def put(self, src, dst):
        self.leaving.append(self.copy(src, dst))

    def finish(self):
        for c in self.leaving:
            c.wait()


class Arrival:
    def __init__(self, copy, ref):
        self.copy, self.ref = copy, ref

    def get(self):
        if self.copy is not None:
            self.copy.wait()
            self.copy = None
        return self.ref


def run(kernel, outs, args, scratch=(), copies=0, flops=0, far=(), far_outs=False):
    nbytes = sum(a.size * a.dtype.itemsize for a in args) + sum(
        functools.reduce(lambda m, n: m * n, s, 2) for s in outs
    )
    return pl.pallas_call(
        kernel,
        out_shape=[jax.ShapeDtypeStruct(s, BF) for s in outs],
        in_specs=[SM] + [HBM if n in far else VM for n in range(1, len(args))],
        out_specs=[HBM if far_outs else VM] * len(outs),
        scratch_shapes=[s if not isinstance(s, tuple) else pltpu.VMEM(s, BF) for s in scratch]
        + ([pltpu.SemaphoreType.DMA((copies,))] if copies else []),
        cost_estimate=pl.CostEstimate(flops=flops, bytes_accessed=nbytes, transcendentals=0),
        compiler_params=pltpu.CompilerParams(vmem_limit_bytes=VMEM_BYTES),
    )(*args)


def column_of(rows):
    return lax.broadcasted_iota(jnp.int32, (rows, 1), 0) % COLS


def right_by_one(v):
    return jnp.where(column_of(v.shape[0]) == 0, 0.0, pltpu.roll(v, 1, 0))


def left_by_one(v):
    return jnp.where(column_of(v.shape[0]) == COLS - 1, 0.0, pltpu.roll(v, v.shape[0] - 1, 0))


def sigmoid(v):
    return 1.0 / (1.0 + jnp.exp(-v))


def padded(pad, odd):
    pad[pl.ds(0, COLS), :] = jnp.zeros((COLS, C), BF)
    pad[pl.ds(TALL, COLS), :] = jnp.zeros((COLS, C), BF)
    return pad.at[pl.ds(pl.multiple_of(COLS * (1 - odd), COLS), TALL), :]


def part(ref, n):
    return ref.at[pl.ds(n * FOLDED, FOLDED), :]


def fold(rows, dst):
    count = rows.shape[0]
    for n in range(2):
        dst[pl.ds(n * count, count), :] = rows[:, n * LANES : (n + 1) * LANES]
    half = count // 2
    dst[pl.ds(2 * count, half), :] = side(rows[:half, HEAD:], rows[half:, HEAD:])


def unfold(src, dst):
    count = dst.shape[0]
    for n in range(2):
        dst[:, pl.ds(n * LANES, LANES)] = src[pl.ds(n * count, count), :]
    half = count // 2
    for n in range(2):
        dst[pl.ds(n * half, half), pl.ds(HEAD, TAIL)] = src[pl.ds(2 * count, half), pl.ds(n * TAIL, TAIL)]


def convolve(pad, w, wn, wk, wr, out, sides):
    tails = side(*[pad[pl.ds(COLS * i, PX), pl.ds(HEAD, TAIL)] for i in range(3)])

    def heads(i):
        return pad[pl.ds(COLS * i, PX), pl.ds(0, HEAD)]

    parts = []
    for j in range(3):
        acc = dot(heads(0), w[j, pl.ds(0, HEAD), pl.ds(0, HEAD)])
        acc = acc + dot(heads(1), w[3 + j, pl.ds(0, HEAD), pl.ds(0, HEAD)])
        acc = acc + dot(heads(2), w[6 + j, pl.ds(0, HEAD), pl.ds(0, HEAD)])
        parts.append(acc + dot(tails, wk[j]))
    centre = pad[pl.ds(COLS, PX), pl.ds(0, HEAD)].astype(F32)
    total = right_by_one(parts[0]) + parts[1] + left_by_one(parts[2])
    out[:, pl.ds(0, HEAD)] = (centre + total).astype(BF)
    acc = dot(heads(0), wn[0]) + dot(heads(1), wn[1]) + dot(heads(2), wn[2])
    acc = acc + dot(tails, wr[...])
    total = right_by_one(acc[:, :TAIL]) + acc[:, TAIL : 2 * TAIL] + left_by_one(acc[:, 2 * TAIL :])
    centre = pad[pl.ds(COLS, PX), pl.ds(HEAD, TAIL)].astype(F32)
    out[:, pl.ds(HEAD, TAIL)] = (centre + total).astype(BF)
    for b in range(CLIPS):
        columns = slice(b * WIDTH, (b + 1) * WIDTH)
        sides[b] = side(*[pad[pl.ds(COLS * i, PX), columns] for i in range(3)])


def conv_own(at, x, w, out0, out1, sides, x2, wn, wk, wr, pads):
    odd = at[0]
    for i in range(3):
        wn[i] = side(*[w[3 * i + j, pl.ds(0, HEAD), pl.ds(HEAD, TAIL)] for j in range(3)])
        for j in range(3):
            wk[j, pl.ds(TAIL * i, TAIL), :] = w[3 * i + j, pl.ds(HEAD, TAIL), pl.ds(0, HEAD)]
        wr[pl.ds(TAIL * i, TAIL), :] = side(
            *[w[3 * i + j, pl.ds(HEAD, TAIL), pl.ds(HEAD, TAIL)] for j in range(3)]
        )
    start = pl.multiple_of((TALL - 2 * COLS) * odd, COLS)
    for q, out in enumerate((out0, out1)):
        padded(pads.at[q], odd)[...] = x[odd + q * (1 - 2 * odd), pl.ds(start, TALL), :]
        convolve(pads.at[q], w, wn, wk, wr, out, sides.at[q])
    away = pl.multiple_of((TALL - 2 * COLS) * (1 - odd), COLS)
    fold(x[1 - odd, pl.ds(away, TALL), :], x2)


def prepare(at, cot, tw, s0, c3, c2, pair, cot0, cot1, vt, vtk, vb, vbk):
    odd = at[0]
    here, there = pl.multiple_of(PX * odd, PX), pl.multiple_of(PX * (1 - odd), PX)
    fold(cot[odd, pl.ds(there, PX), :], c3)
    fold(cot[1 - odd, pl.ds(there, PX), :], c2)
    fold(s0[...], part(pair, 0))
    fold(cot[odd, pl.ds(here, PX), :], part(pair, 1))
    cot0[...] = cot[odd, pl.ds(here, PX), :]
    cot1[...] = cot[1 - odd, pl.ds(here, PX), :]
    for l in range(2):
        for k in range(3):
            value = tw[l, tap(k, odd)]
            turned = value.T
            vt[l, k] = value
            vb[l, k] = turned
            vtk[l, pl.ds(TAIL * k, TAIL), :] = value[HEAD:, :]
            vbk[l, pl.ds(TAIL * k, TAIL), :] = turned[HEAD:, :]


def conv_other(at, x, w, wn, wk, wr, out, sides, pad):
    padded(pad, at[0])[...] = x[...]
    convolve(pad, w, wn, wk, wr, out, sides)


def conv_folded(at, x, w, wn, wk, wr, out, sides, pad):
    unfold(x, padded(pad, at[0]))
    convolve(pad, w, wn, wk, wr, out, sides)


def tap(k, odd):
    return k + odd * (2 - 2 * k)


def three_taps(three, vw, layer, wk):
    tails = side(*[ref[:, pl.ds(HEAD, TAIL)] for ref in three])
    totals = []
    for columns in (pl.ds(0, HEAD), pl.ds(HEAD, TAIL)):
        total = dot(three[0][:, pl.ds(0, HEAD)], vw[layer, 0, pl.ds(0, HEAD), columns])
        total = total + dot(three[1][:, pl.ds(0, HEAD)], vw[layer, 1, pl.ds(0, HEAD), columns])
        total = total + dot(three[2][:, pl.ds(0, HEAD)], vw[layer, 2, pl.ds(0, HEAD), columns])
        totals.append(total + dot(tails, wk[layer, :, columns]))
    return side(*totals)


def temporal(states, vw, layer, wk, acts):
    done = 0
    for q in range(4):
        while done < q + 3:
            v = states[done][...].astype(F32)
            acts[done] = (v * sigmoid(v)).astype(BF)
            done += 1
        term = three_taps([acts.at[q + k] for k in range(3)], vw, layer, wk)
        yield (states[q + 1][...].astype(F32) + term).astype(BF)


def layer_one(at, left, s0, s1, s2, s3, pair, vw, wk, acts, state, last, first, right):
    unfold(part(pair, 0), right)
    states = (left, s0, s1, s2, s3, right)
    for q, value in enumerate(temporal(states, vw, 0, wk, acts)):
        state[q] = value
        if q == 0:
            first[...] = value
        if q == 3:
            last[...] = value


def layer_two(at, left, state, right, vw, wk, acts, own, sent):
    states = (left, state.at[0], state.at[1], state.at[2], state.at[3], right)
    for q, value in enumerate(temporal(states, vw, 1, wk, acts)):
        if q < 2:
            own[q] = value
        else:
            fold(value, part(sent, 3 - q))


def descend(six, q, before, vw, layer, wk):
    three = [six[q + 2 - k] for k in range(3)]
    carried = three_taps(three, vw, layer, wk)
    v = before[...].astype(F32)
    s = sigmoid(v)
    return (three[1][...].astype(F32) + carried * (s * (1.0 + v * (1.0 - s)))).astype(BF)


def back_one(at, folded, cot0, cot1, folded2, folded3, pair, state, vw, wk, back, first, last, c2, c3, left, right):
    unfold(part(pair, 1), right)
    unfold(folded, left)
    unfold(folded2, c2)
    unfold(folded3, c3)
    six = (left, cot0, cot1, c2, c3, right)
    for q in range(4):
        value = descend(six, q, state.at[q], vw, 1, wk)
        back[q] = value
        if q == 0:
            first[...] = value
        if q == 3:
            last[...] = value


def temporal_grads(at, cot0, cot1, c2, c3, acts2, back, acts1, blocks, flip):
    odd = at[0]
    views = (cot0, cot1, c2, c3)
    for layer, acts in ((0, acts1), (1, acts2)):
        for q in range(4):
            up = back.at[q] if layer == 0 else views[q]
            flip[:, pl.ds(q * PX, PX)] = up[...].T
        tails = jnp.zeros((C, THREE_TAILS), F32)
        for q in range(4):
            ends = side(*[acts[q + tap(k, odd), :, pl.ds(HEAD, TAIL)] for k in range(3)])
            tails = tails + dot(flip[:, pl.ds(q * PX, PX)], ends)
        values = []
        for k in range(3):
            total = jnp.zeros((C, HEAD), F32)
            for q in range(4):
                heads = acts[q + tap(k, odd), :, pl.ds(0, HEAD)]
                total = total + dot(flip[:, pl.ds(q * PX, PX)], heads)
            values.append(side(total, tails[:, k * TAIL : (k + 1) * TAIL]).astype(BF))
        for b in range(CLIPS):
            blocks[b, layer] = side(*[v[:, b * WIDTH : (b + 1) * WIDTH] for v in values])


def back_zero(at, left, back, right, s0, s1, s2, s3, vw, wk, own_sides, sides2, sides3, passing, kept, sent, flip):
    core = at[1]
    six = [left] + [back.at[q] for q in range(4)] + [right]
    column = lax.broadcasted_iota(jnp.int32, (1, PX), 1) % COLS
    for q, before in enumerate((s0, s1, s2, s3)):
        turned = descend(six, q, before, vw, 0, wk).T
        wide = turned.astype(F32)
        ahead = jnp.where(column == COLS - 1, 0.0, pltpu.roll(wide, PX - 1, 1))
        behind = jnp.where(column == 0, 0.0, pltpu.roll(wide, 1, 1))
        flip[q, pl.ds(0, C), :] = ahead.astype(BF)
        flip[q, pl.ds(C, C), :] = turned
        flip[q, pl.ds(2 * C, C), :] = behind.astype(BF)
    sides = (own_sides.at[0], own_sides.at[1], sides2, sides3)
    for half in range(2):
        for out, b in ((kept, 2 * half + core), (sent, 2 * half + 1 - core)):
            total = jnp.zeros((3 * C, 3 * WIDTH), F32)
            for q in range(4):
                total = total + dot(flip[q], sides[q][b])
            for j in range(3):
                out[half, j] = total[j * C : (j + 1) * C].astype(BF)
            for layer in range(2):
                out[half, 3 + layer] = passing[b, layer]


def pack(at, kept, got, out, wide, rows, vout, sems):
    halves, taps, channels, _ = kept.shape
    owners = out.shape[0] // halves
    count = channels // owners
    move = Mover(sems)
    for h in range(halves):
        for t in range(taps):
            rows[...] = kept[h, t].astype(F32) + got[h, t].astype(F32)
            for owner in range(owners):
                wide[owner, pl.ds(count * t, count), :] = rows[pl.ds(count * owner, count), :]
        for owner in range(owners):
            vout[owners * h + owner] = wide[owner].astype(BF)
        move.put(vout.at[pl.ds(owners * h, owners)], out.at[pl.ds(owners * h, owners)])
    move.finish()


def place(at, own, got, out, vgot, sems):
    odd = at[0]
    move = Mover(sems)
    here, there = pl.multiple_of(PX * odd, PX), pl.multiple_of(PX * (1 - odd), PX)
    for q, frame in enumerate((odd, 1 - odd)):
        move.put(own.at[q], out.at[frame, pl.ds(here, PX), :])
        unfold(part(got, q), vgot.at[q])
        move.put(vgot.at[q], out.at[frame, pl.ds(there, PX), :])
    move.finish()


def after(value, *others):
    return lax.optimization_barrier((value, *others))[0]


def step(clips_in, cotangent, spatial_weight, temporal_weight):
    owners, clips = lax.axis_size("frame"), lax.axis_size("clip")
    odd = lax.axis_index("frame") % 2
    core = lax.axis_index("clip") % 2
    at = jnp.stack([odd, core]).astype(jnp.int32)
    swap = [(n, n ^ 1) for n in range(owners)]
    outer = [(n, n - 2 if n % 2 == 0 else n + 2) for n in range(owners)]
    outer = [(a, b) for a, b in outer if 0 <= b < owners]
    inner = [(n, n + 2 if n % 2 == 0 else n - 2) for n in range(owners)]
    inner = [(a, b) for a, b in inner if 0 <= b < owners]
    cores = [(n, n ^ 1) for n in range(clips)]

    def send(value, perm, axis="frame"):
        shape = value.shape
        if axis == "frame" and shape[-1] == C:
            value = value.reshape(-1, COLS, C)
        return lax.ppermute(value, axis, perm).reshape(shape)

    x = clips_in.reshape(2, FULL, C)
    cot = cotangent.reshape(2, FULL, C)
    ws = spatial_weight.reshape(9, C, C)
    flops = 2 * PX * C * C

    two, four, six = (2, PX, C), (4, PX, C), (6, PX, C)
    packed = [(3, HEAD, THREE_TAILS), (3, THREE_TAILS, HEAD), (THREE_TAILS, THREE_TAILS)]
    taps = [(2, *KERNELS), (2, THREE_TAILS, C)]
    pad = (PX + 2 * COLS, C)

    tall_start = (TALL - 2 * COLS) * (1 - odd)
    x3 = send(lax.dynamic_slice(x, (odd, tall_start, 0), (1, TALL, C))[0], swap)
    s0, s1, own_sides, x2, wn, wk, wr = run(
        conv_own,
        [ONE, ONE, (2, *SIDES), (TALL * C // LANES, LANES), *packed],
        (at, x, ws),
        [(2, *pad)],
        flops=8 * flops,
    )
    wp = (ws, wn, wk, wr)
    x2 = send(x2, swap)
    c3, c2, pair, cot0, cot1, vt, vtk, vb, vbk = run(
        prepare,
        [(FOLDED, LANES), (FOLDED, LANES), (2 * FOLDED, LANES), ONE, ONE, *taps, *taps],
        (at, after(cot, s0), after(temporal_weight, s0), s0),
        flops=flops,
    )
    right = send(pair, outer)

    s3, sides3 = run(conv_other, [ONE, SIDES], (at, x3, *wp), [pad], 0, 4 * flops)
    left = send(s3, inner)
    c3 = send(after(c3, x2), swap)
    s2, sides2 = run(conv_folded, [ONE, SIDES], (at, x2, *wp), [pad], 0, 4 * flops)
    c2 = send(after(c2, c3), swap)
    cot_left = send(c3, inner)

    acts1, state1, last, first = run(
        layer_one,
        [six, four, ONE, ONE],
        (at, left, s0, s1, s2, s3, right, vt, vtk),
        [ONE],
        flops=8 * flops,
    )
    left1 = send(last, inner)
    right1 = send(first, outer)
    back1, first, last, u2, u3 = run(
        back_one,
        [four, ONE, ONE, ONE, ONE],
        (at, cot_left, cot0, cot1, c2, c3, right, state1, vb, vbk),
        [ONE, ONE],
        flops=8 * flops,
    )
    back_left = send(last, inner)
    back_right = send(first, outer)
    acts2, own, sent = run(
        layer_two, [six, two, (2 * FOLDED, LANES)], (at, left1, state1, right1, vt, vtk), flops=8 * flops
    )
    returned = send(sent, swap)

    (temporal_blocks,) = run(
        temporal_grads,
        [(CLIPS, 2, C, 3 * WIDTH)],
        (at, cot0, cot1, u2, u3, acts2, back1, acts1),
        [(C, 4 * PX)],
        flops=16 * flops,
    )
    shares = (2, 5, C, 3 * WIDTH)
    kept, sent = run(
        back_zero,
        [shares] * 2,
        (at, back_left, back1, back_right, s0, s1, s2, s3, vb, vbk, own_sides, sides2, sides3, temporal_blocks),
        [(4, 3 * C, PX)],
        flops=32 * flops,
    )
    got = send(sent, cores, "clip")
    (out,) = run(place, [(2, FULL, C)], (at, own, returned), [two], 4, 1000, far_outs=True)

    rows = C // owners
    block = (2 * owners, 5 * rows, 3 * WIDTH)
    (packs,) = run(
        pack,
        [block],
        (at, kept, got),
        [pltpu.VMEM((owners, 5 * rows, 3 * WIDTH), F32), pltpu.VMEM((C, 3 * WIDTH), F32), block],
        4,
        1000,
        far_outs=True,
    )
    groups = [[n + half * 2 + c for half in range(2) for n in range(0, owners * clips, clips)] for c in range(2)]
    parts = lax.all_to_all(packs, ("frame", "clip"), split_axis=0, concat_axis=0, axis_index_groups=groups, tiled=True)
    total = jnp.sum(parts.astype(F32), axis=0).reshape(5, rows, 3, WIDTH)
    grad_spatial = total[:3].transpose(1, 2, 0, 3)
    grad_temporal = total[3:].transpose(1, 0, 2, 3)
    return (out.reshape(clips_in.shape), grad_spatial, grad_temporal)


def solution(mesh):
    placed = (P("clip", "frame", None, None, None), P("clip", "frame", None, None, None), P(), P())
    return jax.shard_map(
        step,
        mesh=mesh,
        in_specs=placed,
        out_specs=(
            P("clip", "frame", None, None, None),
            P("frame", None, None, "clip"),
            P("frame", None, None, "clip"),
        ),
        check_vma=False,
    )
```

```python
import functools

import jax
import jax.numpy as jnp
from jax import lax
from jax.experimental import pallas as pl
from jax.experimental.pallas import tpu as pltpu
from jax.sharding import PartitionSpec as P


BF = jnp.bfloat16
F32 = jnp.float32
C = 320
COLS = 32
ROWS = 16
PX = ROWS * COLS
TALL = PX + COLS
FULL = 2 * PX
HEAD = 256
TAIL = C - HEAD
CLIPS = 4
LANES = 128
VMEM_BYTES = 24 * 1024 * 1024
WIDTH = C // CLIPS
HBM = pl.BlockSpec(memory_space=pltpu.HBM)
VM = pl.BlockSpec(memory_space=pltpu.VMEM)
SM = pl.BlockSpec(memory_space=pltpu.SMEM)


ONE = (PX, C)
THREE_TAILS = 3 * TAIL
FOLDED = PX * C // LANES
SIDES = (CLIPS, PX, 3 * WIDTH)
KERNELS = (3, C, C)


def dot(a, b):
    return jnp.dot(a, b, preferred_element_type=F32)


def side(*parts):
    return jnp.concatenate(parts, axis=1)


class Mover:
    def __init__(self, sems):
        self.sems, self.count, self.leaving = sems, 0, []

    def copy(self, src, dst):
        c = pltpu.make_async_copy(src, dst, self.sems.at[self.count])
        self.count += 1
        c.start()
        return c

    def fetch(self, src, dst):
        return Arrival(self.copy(src, dst), dst)

    def put(self, src, dst):
        self.leaving.append(self.copy(src, dst))

    def finish(self):
        for c in self.leaving:
            c.wait()


class Arrival:
    def __init__(self, copy, ref):
        self.copy, self.ref = copy, ref

    def get(self):
        if self.copy is not None:
            self.copy.wait()
            self.copy = None
        return self.ref


def run(kernel, outs, args, scratch=(), copies=0, flops=0, far=(), far_outs=False):
    nbytes = sum(a.size * a.dtype.itemsize for a in args) + sum(
        functools.reduce(lambda m, n: m * n, s, 2) for s in outs
    )
    return pl.pallas_call(
        kernel,
        out_shape=[jax.ShapeDtypeStruct(s, BF) for s in outs],
        in_specs=[SM] + [HBM if n in far else VM for n in range(1, len(args))],
        out_specs=[HBM if far_outs else VM] * len(outs),
        scratch_shapes=[s if not isinstance(s, tuple) else pltpu.VMEM(s, BF) for s in scratch]
        + ([pltpu.SemaphoreType.DMA((copies,))] if copies else []),
        cost_estimate=pl.CostEstimate(flops=flops, bytes_accessed=nbytes, transcendentals=0),
        compiler_params=pltpu.CompilerParams(vmem_limit_bytes=VMEM_BYTES),
    )(*args)


def column_of(rows):
    return lax.broadcasted_iota(jnp.int32, (rows, 1), 0) % COLS


def right_by_one(v):
    return jnp.where(column_of(v.shape[0]) == 0, 0.0, pltpu.roll(v, 1, 0))


def left_by_one(v):
    return jnp.where(column_of(v.shape[0]) == COLS - 1, 0.0, pltpu.roll(v, v.shape[0] - 1, 0))


def sigmoid(v):
    return 1.0 / (1.0 + jnp.exp(-v))


def padded(pad, odd):
    pad[pl.ds(0, COLS), :] = jnp.zeros((COLS, C), BF)
    pad[pl.ds(TALL, COLS), :] = jnp.zeros((COLS, C), BF)
    return pad.at[pl.ds(pl.multiple_of(COLS * (1 - odd), COLS), TALL), :]


def part(ref, n):
    return ref.at[pl.ds(n * FOLDED, FOLDED), :]


def fold(rows, dst):
    count = rows.shape[0]
    for n in range(2):
        dst[pl.ds(n * count, count), :] = rows[:, n * LANES : (n + 1) * LANES]
    half = count // 2
    dst[pl.ds(2 * count, half), :] = side(rows[:half, HEAD:], rows[half:, HEAD:])


def unfold(src, dst):
    count = dst.shape[0]
    for n in range(2):
        dst[:, pl.ds(n * LANES, LANES)] = src[pl.ds(n * count, count), :]
    half = count // 2
    for n in range(2):
        dst[pl.ds(n * half, half), pl.ds(HEAD, TAIL)] = src[pl.ds(2 * count, half), pl.ds(n * TAIL, TAIL)]


def convolve(pad, w, wn, wk, wr, out, sides):
    tails = side(*[pad[pl.ds(COLS * i, PX), pl.ds(HEAD, TAIL)] for i in range(3)])

    def heads(i):
        return pad[pl.ds(COLS * i, PX), pl.ds(0, HEAD)]

    parts = []
    for j in range(3):
        acc = dot(heads(0), w[j, pl.ds(0, HEAD), pl.ds(0, HEAD)])
        acc = acc + dot(heads(1), w[3 + j, pl.ds(0, HEAD), pl.ds(0, HEAD)])
        acc = acc + dot(heads(2), w[6 + j, pl.ds(0, HEAD), pl.ds(0, HEAD)])
        parts.append(acc + dot(tails, wk[j]))
    centre = pad[pl.ds(COLS, PX), pl.ds(0, HEAD)].astype(F32)
    total = right_by_one(parts[0]) + parts[1] + left_by_one(parts[2])
    out[:, pl.ds(0, HEAD)] = (centre + total).astype(BF)
    acc = dot(heads(0), wn[0]) + dot(heads(1), wn[1]) + dot(heads(2), wn[2])
    acc = acc + dot(tails, wr[...])
    total = right_by_one(acc[:, :TAIL]) + acc[:, TAIL : 2 * TAIL] + left_by_one(acc[:, 2 * TAIL :])
    centre = pad[pl.ds(COLS, PX), pl.ds(HEAD, TAIL)].astype(F32)
    out[:, pl.ds(HEAD, TAIL)] = (centre + total).astype(BF)
    for b in range(CLIPS):
        columns = slice(b * WIDTH, (b + 1) * WIDTH)
        sides[b] = side(*[pad[pl.ds(COLS * i, PX), columns] for i in range(3)])


def conv_own(at, x, w, out0, out1, sides, x2, wn, wk, wr, pads):
    odd = at[0]
    for i in range(3):
        wn[i] = side(*[w[3 * i + j, pl.ds(0, HEAD), pl.ds(HEAD, TAIL)] for j in range(3)])
        for j in range(3):
            wk[j, pl.ds(TAIL * i, TAIL), :] = w[3 * i + j, pl.ds(HEAD, TAIL), pl.ds(0, HEAD)]
        wr[pl.ds(TAIL * i, TAIL), :] = side(
            *[w[3 * i + j, pl.ds(HEAD, TAIL), pl.ds(HEAD, TAIL)] for j in range(3)]
        )
    start = pl.multiple_of((TALL - 2 * COLS) * odd, COLS)
    for q, out in enumerate((out0, out1)):
        padded(pads.at[q], odd)[...] = x[odd + q * (1 - 2 * odd), pl.ds(start, TALL), :]
        convolve(pads.at[q], w, wn, wk, wr, out, sides.at[q])
    away = pl.multiple_of((TALL - 2 * COLS) * (1 - odd), COLS)
    fold(x[1 - odd, pl.ds(away, TALL), :], x2)


def prepare(at, cot, tw, c3, c2, cot0, cot1, vt, vtk, vb, vbk):
    odd = at[0]
    here, there = pl.multiple_of(PX * odd, PX), pl.multiple_of(PX * (1 - odd), PX)
    fold(cot[odd, pl.ds(there, PX), :], c3)
    fold(cot[1 - odd, pl.ds(there, PX), :], c2)
    cot0[...] = cot[odd, pl.ds(here, PX), :]
    cot1[...] = cot[1 - odd, pl.ds(here, PX), :]
    for l in range(2):
        for k in range(3):
            value = tw[l, tap(k, odd)]
            turned = value.T
            vt[l, k] = value
            vb[l, k] = turned
            vtk[l, pl.ds(TAIL * k, TAIL), :] = value[HEAD:, :]
            vbk[l, pl.ds(TAIL * k, TAIL), :] = turned[HEAD:, :]


def conv_other(at, x, w, wn, wk, wr, out, sides, pad):
    padded(pad, at[0])[...] = x[...]
    convolve(pad, w, wn, wk, wr, out, sides)


def conv_folded(at, x, w, wn, wk, wr, out, sides, pad):
    unfold(x, padded(pad, at[0]))
    convolve(pad, w, wn, wk, wr, out, sides)


def tap(k, odd):
    return k + odd * (2 - 2 * k)


def three_taps(three, vw, layer, wk):
    tails = side(*[ref[:, pl.ds(HEAD, TAIL)] for ref in three])
    totals = []
    for columns in (pl.ds(0, HEAD), pl.ds(HEAD, TAIL)):
        total = dot(three[0][:, pl.ds(0, HEAD)], vw[layer, 0, pl.ds(0, HEAD), columns])
        total = total + dot(three[1][:, pl.ds(0, HEAD)], vw[layer, 1, pl.ds(0, HEAD), columns])
        total = total + dot(three[2][:, pl.ds(0, HEAD)], vw[layer, 2, pl.ds(0, HEAD), columns])
        totals.append(total + dot(tails, wk[layer, :, columns]))
    return side(*totals)


def temporal(states, vw, layer, wk, acts):
    done = 0
    for q in range(4):
        while done < q + 3:
            v = states[done][...].astype(F32)
            acts[done] = (v * sigmoid(v)).astype(BF)
            done += 1
        term = three_taps([acts.at[q + k] for k in range(3)], vw, layer, wk)
        yield (states[q + 1][...].astype(F32) + term).astype(BF)


def layer_one(at, left, s0, s1, s2, s3, right, vw, wk, acts, state, last, first):
    states = (left, s0, s1, s2, s3, right)
    for q, value in enumerate(temporal(states, vw, 0, wk, acts)):
        state[q] = value
        if q == 0:
            first[...] = value
        if q == 3:
            last[...] = value


def layer_two(at, left, state, right, vw, wk, acts, own, sent):
    states = (left, state.at[0], state.at[1], state.at[2], state.at[3], right)
    for q, value in enumerate(temporal(states, vw, 1, wk, acts)):
        if q < 2:
            own[q] = value
        else:
            fold(value, part(sent, 3 - q))


def descend(six, q, before, vw, layer, wk):
    three = [six[q + 2 - k] for k in range(3)]
    carried = three_taps(three, vw, layer, wk)
    v = before[...].astype(F32)
    s = sigmoid(v)
    return (three[1][...].astype(F32) + carried * (s * (1.0 + v * (1.0 - s)))).astype(BF)


def back_one(at, folded, cot0, cot1, folded2, folded3, right, state, vw, wk, back, first, last, c2, c3, left):
    unfold(folded, left)
    unfold(folded2, c2)
    unfold(folded3, c3)
    six = (left, cot0, cot1, c2, c3, right)
    for q in range(4):
        value = descend(six, q, state.at[q], vw, 1, wk)
        back[q] = value
        if q == 0:
            first[...] = value
        if q == 3:
            last[...] = value


def temporal_grads(at, cot0, cot1, c2, c3, acts2, back, acts1, blocks, flip):
    odd = at[0]
    views = (cot0, cot1, c2, c3)
    for layer, acts in ((0, acts1), (1, acts2)):
        for q in range(4):
            up = back.at[q] if layer == 0 else views[q]
            flip[:, pl.ds(q * PX, PX)] = up[...].T
        tails = jnp.zeros((C, THREE_TAILS), F32)
        for q in range(4):
            ends = side(*[acts[q + tap(k, odd), :, pl.ds(HEAD, TAIL)] for k in range(3)])
            tails = tails + dot(flip[:, pl.ds(q * PX, PX)], ends)
        values = []
        for k in range(3):
            total = jnp.zeros((C, HEAD), F32)
            for q in range(4):
                heads = acts[q + tap(k, odd), :, pl.ds(0, HEAD)]
                total = total + dot(flip[:, pl.ds(q * PX, PX)], heads)
            values.append(side(total, tails[:, k * TAIL : (k + 1) * TAIL]).astype(BF))
        for b in range(CLIPS):
            blocks[b, layer] = side(*[v[:, b * WIDTH : (b + 1) * WIDTH] for v in values])


def back_zero(at, left, back, right, s0, s1, s2, s3, vw, wk, own_sides, sides2, sides3, passing, kept, sent, flip):
    core = at[1]
    six = [left] + [back.at[q] for q in range(4)] + [right]
    column = lax.broadcasted_iota(jnp.int32, (1, PX), 1) % COLS
    for q, before in enumerate((s0, s1, s2, s3)):
        turned = descend(six, q, before, vw, 0, wk).T
        wide = turned.astype(F32)
        ahead = jnp.where(column == COLS - 1, 0.0, pltpu.roll(wide, PX - 1, 1))
        behind = jnp.where(column == 0, 0.0, pltpu.roll(wide, 1, 1))
        flip[q, pl.ds(0, C), :] = ahead.astype(BF)
        flip[q, pl.ds(C, C), :] = turned
        flip[q, pl.ds(2 * C, C), :] = behind.astype(BF)
    sides = (own_sides.at[0], own_sides.at[1], sides2, sides3)
    for half in range(2):
        for out, b in ((kept, 2 * half + core), (sent, 2 * half + 1 - core)):
            total = jnp.zeros((3 * C, 3 * WIDTH), F32)
            for q in range(4):
                total = total + dot(flip[q], sides[q][b])
            for j in range(3):
                out[half, j] = total[j * C : (j + 1) * C].astype(BF)
            for layer in range(2):
                out[half, 3 + layer] = passing[b, layer]


def pack(at, kept, got, out, wide, rows, vout, sems):
    halves, taps, channels, _ = kept.shape
    owners = out.shape[0] // halves
    count = channels // owners
    move = Mover(sems)
    for h in range(halves):
        for t in range(taps):
            rows[...] = kept[h, t].astype(F32) + got[h, t].astype(F32)
            for owner in range(owners):
                wide[owner, pl.ds(count * t, count), :] = rows[pl.ds(count * owner, count), :]
        for owner in range(owners):
            vout[owners * h + owner] = wide[owner].astype(BF)
        move.put(vout.at[pl.ds(owners * h, owners)], out.at[pl.ds(owners * h, owners)])
    move.finish()


def place(at, own, got, out, vgot, sems):
    odd = at[0]
    move = Mover(sems)
    here, there = pl.multiple_of(PX * odd, PX), pl.multiple_of(PX * (1 - odd), PX)
    for q, frame in enumerate((odd, 1 - odd)):
        move.put(own.at[q], out.at[frame, pl.ds(here, PX), :])
        unfold(part(got, q), vgot.at[q])
        move.put(vgot.at[q], out.at[frame, pl.ds(there, PX), :])
    move.finish()


def after(value, *others):
    return lax.optimization_barrier((value, *others))[0]


def step(clips_in, cotangent, spatial_weight, temporal_weight):
    owners, clips = lax.axis_size("frame"), lax.axis_size("clip")
    odd = lax.axis_index("frame") % 2
    core = lax.axis_index("clip") % 2
    at = jnp.stack([odd, core]).astype(jnp.int32)
    swap = [(n, n ^ 1) for n in range(owners)]
    outer = [(n, n - 2 if n % 2 == 0 else n + 2) for n in range(owners)]
    outer = [(a, b) for a, b in outer if 0 <= b < owners]
    inner = [(n, n + 2 if n % 2 == 0 else n - 2) for n in range(owners)]
    inner = [(a, b) for a, b in inner if 0 <= b < owners]
    cores = [(n, n ^ 1) for n in range(clips)]

    def send(value, perm, axis="frame"):
        shape = value.shape
        if axis == "frame" and shape[-1] == C:
            value = value.reshape(-1, COLS, C)
        return lax.ppermute(value, axis, perm).reshape(shape)

    x = clips_in.reshape(2, FULL, C)
    cot = cotangent.reshape(2, FULL, C)
    ws = spatial_weight.reshape(9, C, C)
    flops = 2 * PX * C * C

    two, four, six = (2, PX, C), (4, PX, C), (6, PX, C)
    packed = [(3, HEAD, THREE_TAILS), (3, THREE_TAILS, HEAD), (THREE_TAILS, THREE_TAILS)]
    taps = [(2, *KERNELS), (2, THREE_TAILS, C)]
    pad = (PX + 2 * COLS, C)

    tall_start = (TALL - 2 * COLS) * (1 - odd)
    x3 = send(lax.dynamic_slice(x, (odd, tall_start, 0), (1, TALL, C))[0], swap)
    s0, s1, own_sides, x2, wn, wk, wr = run(
        conv_own,
        [ONE, ONE, (2, *SIDES), (TALL * C // LANES, LANES), *packed],
        (at, x, ws),
        [(2, *pad)],
        flops=8 * flops,
    )
    wp = (ws, wn, wk, wr)
    right = send(s0, outer)
    x2 = send(x2, swap)
    c3, c2, cot0, cot1, vt, vtk, vb, vbk = run(
        prepare, [(PX * C // LANES, LANES)] * 2 + [ONE] * 2 + taps * 2, (at, after(cot, s0), after(temporal_weight, s0)), flops=flops
    )

    s3, sides3 = run(conv_other, [ONE, SIDES], (at, x3, *wp), [pad], 0, 4 * flops)
    left = send(s3, inner)
    c3 = send(after(c3, x2), swap)
    s2, sides2 = run(conv_folded, [ONE, SIDES], (at, x2, *wp), [pad], 0, 4 * flops)
    c2 = send(after(c2, c3), swap)
    cot_right = send(after(cot0, s3), outer)
    cot_left = send(c3, inner)

    acts1, state1, last, first = run(
        layer_one,
        [six, four, ONE, ONE],
        (at, left, s0, s1, s2, s3, right, vt, vtk),
        flops=8 * flops,
    )
    left1 = send(last, inner)
    right1 = send(first, outer)
    back1, first, last, u2, u3 = run(
        back_one,
        [four, ONE, ONE, ONE, ONE],
        (at, cot_left, cot0, cot1, c2, c3, cot_right, state1, vb, vbk),
        [ONE],
        flops=8 * flops,
    )
    back_left = send(last, inner)
    back_right = send(first, outer)
    acts2, own, sent = run(
        layer_two, [six, two, (2 * FOLDED, LANES)], (at, left1, state1, right1, vt, vtk), flops=8 * flops
    )
    returned = send(sent, swap)

    (temporal_blocks,) = run(
        temporal_grads,
        [(CLIPS, 2, C, 3 * WIDTH)],
        (at, cot0, cot1, u2, u3, acts2, back1, acts1),
        [(C, 4 * PX)],
        flops=16 * flops,
    )
    shares = (2, 5, C, 3 * WIDTH)
    kept, sent = run(
        back_zero,
        [shares] * 2,
        (at, back_left, back1, back_right, s0, s1, s2, s3, vb, vbk, own_sides, sides2, sides3, temporal_blocks),
        [(4, 3 * C, PX)],
        flops=32 * flops,
    )
    got = send(sent, cores, "clip")
    (out,) = run(place, [(2, FULL, C)], (at, own, returned), [two], 4, 1000, far_outs=True)

    rows = C // owners
    block = (2 * owners, 5 * rows, 3 * WIDTH)
    (packs,) = run(
        pack,
        [block],
        (at, kept, got),
        [pltpu.VMEM((owners, 5 * rows, 3 * WIDTH), F32), pltpu.VMEM((C, 3 * WIDTH), F32), block],
        4,
        1000,
        far_outs=True,
    )
    groups = [[n + half * 2 + c for half in range(2) for n in range(0, owners * clips, clips)] for c in range(2)]
    parts = lax.all_to_all(packs, ("frame", "clip"), split_axis=0, concat_axis=0, axis_index_groups=groups, tiled=True)
    total = jnp.sum(parts.astype(F32), axis=0).reshape(5, rows, 3, WIDTH)
    grad_spatial = total[:3].transpose(1, 2, 0, 3)
    grad_temporal = total[3:].transpose(1, 0, 2, 3)
    return (out.reshape(clips_in.shape), grad_spatial, grad_temporal)


def solution(mesh):
    placed = (P("clip", "frame", None, None, None), P("clip", "frame", None, None, None), P(), P())
    return jax.shard_map(
        step,
        mesh=mesh,
        in_specs=placed,
        out_specs=(
            P("clip", "frame", None, None, None),
            P("frame", None, None, "clip"),
            P("frame", None, None, "clip"),
        ),
        check_vma=False,
    )
```

```python
import functools

import jax
import jax.numpy as jnp
from jax import lax
from jax.experimental import pallas as pl
from jax.experimental.pallas import tpu as pltpu
from jax.sharding import PartitionSpec as P


BF = jnp.bfloat16
F32 = jnp.float32
C = 320
COLS = 32
ROWS = 16
PX = ROWS * COLS
TALL = PX + COLS
FULL = 2 * PX
HEAD = 256
TAIL = C - HEAD
CLIPS = 4
LANES = 128
VMEM_BYTES = 24 * 1024 * 1024
WIDTH = C // CLIPS
HBM = pl.BlockSpec(memory_space=pltpu.HBM)
VM = pl.BlockSpec(memory_space=pltpu.VMEM)
SM = pl.BlockSpec(memory_space=pltpu.SMEM)


ONE = (PX, C)
THREE_TAILS = 3 * TAIL
FOLDED = PX * C // LANES
SIDES = (CLIPS, PX, 3 * WIDTH)
KERNELS = (3, C, C)


def dot(a, b):
    return jnp.dot(a, b, preferred_element_type=F32)


def side(*parts):
    return jnp.concatenate(parts, axis=1)


class Mover:
    def __init__(self, sems):
        self.sems, self.count, self.leaving = sems, 0, []

    def copy(self, src, dst):
        c = pltpu.make_async_copy(src, dst, self.sems.at[self.count])
        self.count += 1
        c.start()
        return c

    def fetch(self, src, dst):
        return Arrival(self.copy(src, dst), dst)

    def put(self, src, dst):
        self.leaving.append(self.copy(src, dst))

    def finish(self):
        for c in self.leaving:
            c.wait()


class Arrival:
    def __init__(self, copy, ref):
        self.copy, self.ref = copy, ref

    def get(self):
        if self.copy is not None:
            self.copy.wait()
            self.copy = None
        return self.ref


def run(kernel, outs, args, scratch=(), copies=0, flops=0, far=(), far_outs=False, kind=BF):
    nbytes = sum(a.size * a.dtype.itemsize for a in args) + sum(
        functools.reduce(lambda m, n: m * n, s, 2) for s in outs
    )
    return pl.pallas_call(
        kernel,
        out_shape=[jax.ShapeDtypeStruct(s, kind) for s in outs],
        in_specs=[SM] + [HBM if n in far else VM for n in range(1, len(args))],
        out_specs=[HBM if far_outs else VM] * len(outs),
        scratch_shapes=[s if not isinstance(s, tuple) else pltpu.VMEM(s, BF) for s in scratch]
        + ([pltpu.SemaphoreType.DMA((copies,))] if copies else []),
        cost_estimate=pl.CostEstimate(flops=flops, bytes_accessed=nbytes, transcendentals=0),
        compiler_params=pltpu.CompilerParams(vmem_limit_bytes=VMEM_BYTES),
    )(*args)


def column_of(rows):
    return lax.broadcasted_iota(jnp.int32, (rows, 1), 0) % COLS


def right_by_one(v):
    return jnp.where(column_of(v.shape[0]) == 0, 0.0, pltpu.roll(v, 1, 0))


def left_by_one(v):
    return jnp.where(column_of(v.shape[0]) == COLS - 1, 0.0, pltpu.roll(v, v.shape[0] - 1, 0))


def sigmoid(v):
    return 1.0 / (1.0 + jnp.exp(-v))


def padded(pad, odd):
    pad[pl.ds(0, COLS), :] = jnp.zeros((COLS, C), BF)
    pad[pl.ds(TALL, COLS), :] = jnp.zeros((COLS, C), BF)
    return pad.at[pl.ds(pl.multiple_of(COLS * (1 - odd), COLS), TALL), :]


def part(ref, n):
    return ref.at[pl.ds(n * FOLDED, FOLDED), :]


def fold(rows, dst):
    count = rows.shape[0]
    for n in range(2):
        dst[pl.ds(n * count, count), :] = rows[:, n * LANES : (n + 1) * LANES]
    half = count // 2
    dst[pl.ds(2 * count, half), :] = side(rows[:half, HEAD:], rows[half:, HEAD:])


def unfold(src, dst):
    count = dst.shape[0]
    for n in range(2):
        dst[:, pl.ds(n * LANES, LANES)] = src[pl.ds(n * count, count), :]
    half = count // 2
    for n in range(2):
        dst[pl.ds(n * half, half), pl.ds(HEAD, TAIL)] = src[pl.ds(2 * count, half), pl.ds(n * TAIL, TAIL)]


def convolve(pad, w, wn, wk, wr, out, sides):
    tails = side(*[pad[pl.ds(COLS * i, PX), pl.ds(HEAD, TAIL)] for i in range(3)])

    def heads(i):
        return pad[pl.ds(COLS * i, PX), pl.ds(0, HEAD)]

    parts = []
    for j in range(3):
        acc = dot(heads(0), w[j, pl.ds(0, HEAD), pl.ds(0, HEAD)])
        acc = acc + dot(heads(1), w[3 + j, pl.ds(0, HEAD), pl.ds(0, HEAD)])
        acc = acc + dot(heads(2), w[6 + j, pl.ds(0, HEAD), pl.ds(0, HEAD)])
        parts.append(acc + dot(tails, wk[j]))
    centre = pad[pl.ds(COLS, PX), pl.ds(0, HEAD)].astype(F32)
    total = right_by_one(parts[0]) + parts[1] + left_by_one(parts[2])
    out[:, pl.ds(0, HEAD)] = (centre + total).astype(BF)
    acc = dot(heads(0), wn[0]) + dot(heads(1), wn[1]) + dot(heads(2), wn[2])
    acc = acc + dot(tails, wr[...])
    total = right_by_one(acc[:, :TAIL]) + acc[:, TAIL : 2 * TAIL] + left_by_one(acc[:, 2 * TAIL :])
    centre = pad[pl.ds(COLS, PX), pl.ds(HEAD, TAIL)].astype(F32)
    out[:, pl.ds(HEAD, TAIL)] = (centre + total).astype(BF)
    for b in range(CLIPS):
        columns = slice(b * WIDTH, (b + 1) * WIDTH)
        sides[b] = side(*[pad[pl.ds(COLS * i, PX), columns] for i in range(3)])


def conv_own(at, x, w, out0, out1, sides, x2, wn, wk, wr, pads):
    odd = at[0]
    for i in range(3):
        wn[i] = side(*[w[3 * i + j, pl.ds(0, HEAD), pl.ds(HEAD, TAIL)] for j in range(3)])
        for j in range(3):
            wk[j, pl.ds(TAIL * i, TAIL), :] = w[3 * i + j, pl.ds(HEAD, TAIL), pl.ds(0, HEAD)]
        wr[pl.ds(TAIL * i, TAIL), :] = side(
            *[w[3 * i + j, pl.ds(HEAD, TAIL), pl.ds(HEAD, TAIL)] for j in range(3)]
        )
    start = pl.multiple_of((TALL - 2 * COLS) * odd, COLS)
    for q, out in enumerate((out0, out1)):
        padded(pads.at[q], odd)[...] = x[odd + q * (1 - 2 * odd), pl.ds(start, TALL), :]
        convolve(pads.at[q], w, wn, wk, wr, out, sides.at[q])
    away = pl.multiple_of((TALL - 2 * COLS) * (1 - odd), COLS)
    fold(x[1 - odd, pl.ds(away, TALL), :], x2)


def prepare(at, cot, tw, c3, c2, cot0, cot1, vt, vtk, vb, vbk):
    odd = at[0]
    here, there = pl.multiple_of(PX * odd, PX), pl.multiple_of(PX * (1 - odd), PX)
    fold(cot[odd, pl.ds(there, PX), :], c3)
    fold(cot[1 - odd, pl.ds(there, PX), :], c2)
    cot0[...] = cot[odd, pl.ds(here, PX), :]
    cot1[...] = cot[1 - odd, pl.ds(here, PX), :]
    for l in range(2):
        for k in range(3):
            value = tw[l, tap(k, odd)]
            turned = value.T
            vt[l, k] = value
            vb[l, k] = turned
            vtk[l, pl.ds(TAIL * k, TAIL), :] = value[HEAD:, :]
            vbk[l, pl.ds(TAIL * k, TAIL), :] = turned[HEAD:, :]


def conv_other(at, x, w, wn, wk, wr, out, sides, pad):
    padded(pad, at[0])[...] = x[...]
    convolve(pad, w, wn, wk, wr, out, sides)


def conv_folded(at, x, w, wn, wk, wr, out, sides, pad):
    unfold(x, padded(pad, at[0]))
    convolve(pad, w, wn, wk, wr, out, sides)


def tap(k, odd):
    return k + odd * (2 - 2 * k)


def three_taps(three, vw, layer, wk):
    tails = side(*[ref[:, pl.ds(HEAD, TAIL)] for ref in three])
    totals = []
    for columns in (pl.ds(0, HEAD), pl.ds(HEAD, TAIL)):
        total = dot(three[0][:, pl.ds(0, HEAD)], vw[layer, 0, pl.ds(0, HEAD), columns])
        total = total + dot(three[1][:, pl.ds(0, HEAD)], vw[layer, 1, pl.ds(0, HEAD), columns])
        total = total + dot(three[2][:, pl.ds(0, HEAD)], vw[layer, 2, pl.ds(0, HEAD), columns])
        totals.append(total + dot(tails, wk[layer, :, columns]))
    return side(*totals)


def temporal(states, vw, layer, wk, acts):
    done = 0
    for q in range(4):
        while done < q + 3:
            v = states[done][...].astype(F32)
            acts[done] = (v * sigmoid(v)).astype(BF)
            done += 1
        term = three_taps([acts.at[q + k] for k in range(3)], vw, layer, wk)
        yield (states[q + 1][...].astype(F32) + term).astype(BF)


def layer_one(at, left, s0, s1, s2, s3, right, vw, wk, acts, state, last, first):
    states = (left, s0, s1, s2, s3, right)
    for q, value in enumerate(temporal(states, vw, 0, wk, acts)):
        state[q] = value
        if q == 0:
            first[...] = value
        if q == 3:
            last[...] = value


def layer_two(at, left, state, right, vw, wk, acts, own, sent):
    states = (left, state.at[0], state.at[1], state.at[2], state.at[3], right)
    for q, value in enumerate(temporal(states, vw, 1, wk, acts)):
        if q < 2:
            own[q] = value
        else:
            fold(value, part(sent, 3 - q))


def descend(six, q, before, vw, layer, wk):
    three = [six[q + 2 - k] for k in range(3)]
    carried = three_taps(three, vw, layer, wk)
    v = before[...].astype(F32)
    s = sigmoid(v)
    return (three[1][...].astype(F32) + carried * (s * (1.0 + v * (1.0 - s)))).astype(BF)


def back_one(at, folded, cot0, cot1, folded2, folded3, right, state, vw, wk, back, first, last, c2, c3, left):
    unfold(folded, left)
    unfold(folded2, c2)
    unfold(folded3, c3)
    six = (left, cot0, cot1, c2, c3, right)
    for q in range(4):
        value = descend(six, q, state.at[q], vw, 1, wk)
        back[q] = value
        if q == 0:
            first[...] = value
        if q == 3:
            last[...] = value


def temporal_grads(at, cot0, cot1, c2, c3, acts2, back, acts1, blocks, flip):
    odd = at[0]
    views = (cot0, cot1, c2, c3)
    for layer, acts in ((0, acts1), (1, acts2)):
        for q in range(4):
            up = back.at[q] if layer == 0 else views[q]
            flip[:, pl.ds(q * PX, PX)] = up[...].T
        tails = jnp.zeros((C, THREE_TAILS), F32)
        for q in range(4):
            ends = side(*[acts[q + tap(k, odd), :, pl.ds(HEAD, TAIL)] for k in range(3)])
            tails = tails + dot(flip[:, pl.ds(q * PX, PX)], ends)
        values = []
        for k in range(3):
            total = jnp.zeros((C, HEAD), F32)
            for q in range(4):
                heads = acts[q + tap(k, odd), :, pl.ds(0, HEAD)]
                total = total + dot(flip[:, pl.ds(q * PX, PX)], heads)
            values.append(side(total, tails[:, k * TAIL : (k + 1) * TAIL]).astype(BF))
        for b in range(CLIPS):
            blocks[b, layer] = side(*[v[:, b * WIDTH : (b + 1) * WIDTH] for v in values])


def back_zero(at, left, back, right, s0, s1, s2, s3, vw, wk, own_sides, sides2, sides3, passing, kept, sent, flip):
    core = at[1]
    six = [left] + [back.at[q] for q in range(4)] + [right]
    column = lax.broadcasted_iota(jnp.int32, (1, PX), 1) % COLS
    for q, before in enumerate((s0, s1, s2, s3)):
        turned = descend(six, q, before, vw, 0, wk).T
        wide = turned.astype(F32)
        ahead = jnp.where(column == COLS - 1, 0.0, pltpu.roll(wide, PX - 1, 1))
        behind = jnp.where(column == 0, 0.0, pltpu.roll(wide, 1, 1))
        flip[q, pl.ds(0, C), :] = ahead.astype(BF)
        flip[q, pl.ds(C, C), :] = turned
        flip[q, pl.ds(2 * C, C), :] = behind.astype(BF)
    sides = (own_sides.at[0], own_sides.at[1], sides2, sides3)
    for half in range(2):
        for out, b in ((kept, 2 * half + core), (sent, 2 * half + 1 - core)):
            total = jnp.zeros((3 * C, 3 * WIDTH), F32)
            for q in range(4):
                total = total + dot(flip[q], sides[q][b])
            for j in range(3):
                out[half, j] = total[j * C : (j + 1) * C].astype(BF)
            for layer in range(2):
                out[half, 3 + layer] = passing[b, layer]


def pack(at, kept, got, out, wide, rows):
    halves, taps, channels, width = kept.shape
    owners = out.shape[0] // halves
    count = channels // owners
    rows[:, pl.ds(width, 2 * LANES - width)] = jnp.zeros((channels, 2 * LANES - width), F32)
    for h in range(halves):
        for t in range(taps):
            rows[:, pl.ds(0, width)] = kept[h, t].astype(F32) + got[h, t].astype(F32)
            for owner in range(owners):
                for n in range(2):
                    block = pl.ds(count * (2 * t + n), count)
                    wide[owner, block, :] = rows[pl.ds(count * owner, count), pl.ds(n * LANES, LANES)]
        for owner in range(owners):
            out[owners * h + owner] = wide[owner].astype(BF)


def finish(at, parts, spatial, temporal):
    total = parts[0].astype(F32)
    for n in range(1, parts.shape[0]):
        total = total + parts[n].astype(F32)
    count = spatial.shape[0]
    for t in range(5):
        low = total[2 * t * count : (2 * t + 1) * count]
        high = total[(2 * t + 1) * count : (2 * t + 2) * count]
        row = side(low, high[:, : 3 * WIDTH - LANES])
        for i in range(3):
            piece = row[:, i * WIDTH : (i + 1) * WIDTH]
            for r in range(count):
                if t < 3:
                    spatial[r, i, pl.ds(t, 1), :] = piece[r : r + 1]
                else:
                    temporal[r, i, pl.ds(t - 3, 1), :] = piece[r : r + 1]


def place(at, own, got, out, vgot, sems):
    odd = at[0]
    move = Mover(sems)
    here, there = pl.multiple_of(PX * odd, PX), pl.multiple_of(PX * (1 - odd), PX)
    for q, frame in enumerate((odd, 1 - odd)):
        move.put(own.at[q], out.at[frame, pl.ds(here, PX), :])
        unfold(part(got, q), vgot.at[q])
        move.put(vgot.at[q], out.at[frame, pl.ds(there, PX), :])
    move.finish()


def after(value, *others):
    return lax.optimization_barrier((value, *others))[0]


def step(clips_in, cotangent, spatial_weight, temporal_weight):
    owners, clips = lax.axis_size("frame"), lax.axis_size("clip")
    odd = lax.axis_index("frame") % 2
    core = lax.axis_index("clip") % 2
    at = jnp.stack([odd, core]).astype(jnp.int32)
    swap = [(n, n ^ 1) for n in range(owners)]
    outer = [(n, n - 2 if n % 2 == 0 else n + 2) for n in range(owners)]
    outer = [(a, b) for a, b in outer if 0 <= b < owners]
    inner = [(n, n + 2 if n % 2 == 0 else n - 2) for n in range(owners)]
    inner = [(a, b) for a, b in inner if 0 <= b < owners]
    cores = [(n, n ^ 1) for n in range(clips)]

    def send(value, perm, axis="frame"):
        shape = value.shape
        if axis == "frame" and shape[-1] == C:
            value = value.reshape(-1, COLS, C)
        return lax.ppermute(value, axis, perm).reshape(shape)

    x = clips_in.reshape(2, FULL, C)
    cot = cotangent.reshape(2, FULL, C)
    ws = spatial_weight.reshape(9, C, C)
    flops = 2 * PX * C * C

    two, four, six = (2, PX, C), (4, PX, C), (6, PX, C)
    packed = [(3, HEAD, THREE_TAILS), (3, THREE_TAILS, HEAD), (THREE_TAILS, THREE_TAILS)]
    taps = [(2, *KERNELS), (2, THREE_TAILS, C)]
    pad = (PX + 2 * COLS, C)

    tall_start = (TALL - 2 * COLS) * (1 - odd)
    x3 = send(lax.dynamic_slice(x, (odd, tall_start, 0), (1, TALL, C))[0], swap)
    s0, s1, own_sides, x2, wn, wk, wr = run(
        conv_own,
        [ONE, ONE, (2, *SIDES), (TALL * C // LANES, LANES), *packed],
        (at, x, ws),
        [(2, *pad)],
        flops=8 * flops,
    )
    wp = (ws, wn, wk, wr)
    right = send(s0, outer)
    x2 = send(x2, swap)
    s3, sides3 = run(conv_other, [ONE, SIDES], (at, x3, *wp), [pad], 0, 4 * flops)
    left = send(s3, inner)
    c3, c2, cot0, cot1, vt, vtk, vb, vbk = run(
        prepare, [(PX * C // LANES, LANES)] * 2 + [ONE] * 2 + taps * 2, (at, after(cot, s3), after(temporal_weight, s3)), flops=flops
    )
    c3 = send(after(c3, x2), swap)
    s2, sides2 = run(conv_folded, [ONE, SIDES], (at, x2, *wp), [pad], 0, 4 * flops)
    c2 = send(after(c2, c3), swap)
    cot_right = send(after(cot0, s3), outer)
    cot_left = send(c3, inner)

    acts1, state1, last, first = run(
        layer_one,
        [six, four, ONE, ONE],
        (at, left, s0, s1, s2, s3, right, vt, vtk),
        flops=8 * flops,
    )
    left1 = send(last, inner)
    right1 = send(first, outer)
    back1, first, last, u2, u3 = run(
        back_one,
        [four, ONE, ONE, ONE, ONE],
        (at, cot_left, cot0, cot1, c2, c3, cot_right, state1, vb, vbk),
        [ONE],
        flops=8 * flops,
    )
    back_left = send(last, inner)
    back_right = send(first, outer)
    acts2, own, sent = run(
        layer_two, [six, two, (2 * FOLDED, LANES)], (at, left1, state1, right1, vt, vtk), flops=8 * flops
    )
    returned = send(sent, swap)

    (temporal_blocks,) = run(
        temporal_grads,
        [(CLIPS, 2, C, 3 * WIDTH)],
        (at, cot0, cot1, u2, u3, acts2, back1, acts1),
        [(C, 4 * PX)],
        flops=16 * flops,
    )
    shares = (2, 5, C, 3 * WIDTH)
    kept, sent = run(
        back_zero,
        [shares] * 2,
        (at, back_left, back1, back_right, s0, s1, s2, s3, vb, vbk, own_sides, sides2, sides3, temporal_blocks),
        [(4, 3 * C, PX)],
        flops=32 * flops,
    )
    got = send(sent, cores, "clip")
    (out,) = run(place, [(2, FULL, C)], (at, own, returned), [two], 4, 1000, far_outs=True)

    rows = C // owners
    block = (2 * owners, 10 * rows, LANES)
    (packs,) = run(
        pack,
        [block],
        (at, kept, got),
        [pltpu.VMEM((owners, 10 * rows, LANES), F32), pltpu.VMEM((C, 2 * LANES), F32)],
        flops=1000,
    )
    groups = [[n + half * 2 + c for half in range(2) for n in range(0, owners * clips, clips)] for c in range(2)]
    parts = lax.all_to_all(packs, ("frame", "clip"), split_axis=0, concat_axis=0, axis_index_groups=groups, tiled=True)
    grad_spatial, grad_temporal = run(
        finish, [(rows, 3, 3, WIDTH), (rows, 3, 2, WIDTH)], (at, parts), flops=1000, kind=F32
    )
    grad_temporal = grad_temporal.transpose(0, 2, 1, 3)
    return (out.reshape(clips_in.shape), grad_spatial, grad_temporal)


def solution(mesh):
    placed = (P("clip", "frame", None, None, None), P("clip", "frame", None, None, None), P(), P())
    return jax.shard_map(
        step,
        mesh=mesh,
        in_specs=placed,
        out_specs=(
            P("clip", "frame", None, None, None),
            P("frame", None, None, "clip"),
            P("frame", None, None, "clip"),
        ),
        check_vma=False,
    )
```

```python
import functools

import jax
import jax.numpy as jnp
from jax import lax
from jax.experimental import pallas as pl
from jax.experimental.pallas import tpu as pltpu
from jax.sharding import PartitionSpec as P


BF = jnp.bfloat16
F32 = jnp.float32
C = 320
COLS = 32
ROWS = 16
PX = ROWS * COLS
TALL = PX + COLS
FULL = 2 * PX
HEAD = 256
TAIL = C - HEAD
CLIPS = 4
LANES = 128
VMEM_BYTES = 24 * 1024 * 1024
WIDTH = C // CLIPS
HBM = pl.BlockSpec(memory_space=pltpu.HBM)
VM = pl.BlockSpec(memory_space=pltpu.VMEM)
SM = pl.BlockSpec(memory_space=pltpu.SMEM)


ONE = (PX, C)
THREE_TAILS = 3 * TAIL
FOLDED = PX * C // LANES
SIDES = (CLIPS, PX, 3 * WIDTH)
KERNELS = (3, C, C)


def dot(a, b):
    return jnp.dot(a, b, preferred_element_type=F32)


def side(*parts):
    return jnp.concatenate(parts, axis=1)


class Mover:
    def __init__(self, sems):
        self.sems, self.count, self.leaving = sems, 0, []

    def copy(self, src, dst):
        c = pltpu.make_async_copy(src, dst, self.sems.at[self.count])
        self.count += 1
        c.start()
        return c

    def fetch(self, src, dst):
        return Arrival(self.copy(src, dst), dst)

    def put(self, src, dst):
        self.leaving.append(self.copy(src, dst))

    def finish(self):
        for c in self.leaving:
            c.wait()


class Arrival:
    def __init__(self, copy, ref):
        self.copy, self.ref = copy, ref

    def get(self):
        if self.copy is not None:
            self.copy.wait()
            self.copy = None
        return self.ref


def run(kernel, outs, args, scratch=(), copies=0, flops=0, far=(), far_outs=False, kind=BF):
    nbytes = sum(a.size * a.dtype.itemsize for a in args) + sum(
        functools.reduce(lambda m, n: m * n, s, 2) for s in outs
    )
    return pl.pallas_call(
        kernel,
        out_shape=[jax.ShapeDtypeStruct(s, kind) for s in outs],
        in_specs=[SM] + [HBM if n in far else VM for n in range(1, len(args))],
        out_specs=[HBM if far_outs else VM] * len(outs),
        scratch_shapes=[s if not isinstance(s, tuple) else pltpu.VMEM(s, BF) for s in scratch]
        + ([pltpu.SemaphoreType.DMA((copies,))] if copies else []),
        cost_estimate=pl.CostEstimate(flops=flops, bytes_accessed=nbytes, transcendentals=0),
        compiler_params=pltpu.CompilerParams(vmem_limit_bytes=VMEM_BYTES),
    )(*args)


def column_of(rows):
    return lax.broadcasted_iota(jnp.int32, (rows, 1), 0) % COLS


def right_by_one(v):
    return jnp.where(column_of(v.shape[0]) == 0, 0.0, pltpu.roll(v, 1, 0))


def left_by_one(v):
    return jnp.where(column_of(v.shape[0]) == COLS - 1, 0.0, pltpu.roll(v, v.shape[0] - 1, 0))


def sigmoid(v):
    return 1.0 / (1.0 + jnp.exp(-v))


def padded(pad, odd):
    pad[pl.ds(0, COLS), :] = jnp.zeros((COLS, C), BF)
    pad[pl.ds(TALL, COLS), :] = jnp.zeros((COLS, C), BF)
    return pad.at[pl.ds(pl.multiple_of(COLS * (1 - odd), COLS), TALL), :]


def part(ref, n):
    return ref.at[pl.ds(n * FOLDED, FOLDED), :]


def fold(rows, dst):
    count = rows.shape[0]
    for n in range(2):
        dst[pl.ds(n * count, count), :] = rows[:, n * LANES : (n + 1) * LANES]
    half = count // 2
    dst[pl.ds(2 * count, half), :] = side(rows[:half, HEAD:], rows[half:, HEAD:])


def unfold(src, dst):
    count = dst.shape[0]
    for n in range(2):
        dst[:, pl.ds(n * LANES, LANES)] = src[pl.ds(n * count, count), :]
    half = count // 2
    for n in range(2):
        dst[pl.ds(n * half, half), pl.ds(HEAD, TAIL)] = src[pl.ds(2 * count, half), pl.ds(n * TAIL, TAIL)]


def convolve(pad, w, wn, wk, wr, out, sides):
    tails = side(*[pad[pl.ds(COLS * i, PX), pl.ds(HEAD, TAIL)] for i in range(3)])

    def heads(i):
        return pad[pl.ds(COLS * i, PX), pl.ds(0, HEAD)]

    parts = []
    for j in range(3):
        acc = dot(heads(0), w[j, pl.ds(0, HEAD), pl.ds(0, HEAD)])
        acc = acc + dot(heads(1), w[3 + j, pl.ds(0, HEAD), pl.ds(0, HEAD)])
        acc = acc + dot(heads(2), w[6 + j, pl.ds(0, HEAD), pl.ds(0, HEAD)])
        parts.append(acc + dot(tails, wk[j]))
    centre = pad[pl.ds(COLS, PX), pl.ds(0, HEAD)].astype(F32)
    total = right_by_one(parts[0]) + parts[1] + left_by_one(parts[2])
    out[:, pl.ds(0, HEAD)] = (centre + total).astype(BF)
    acc = dot(heads(0), wn[0]) + dot(heads(1), wn[1]) + dot(heads(2), wn[2])
    acc = acc + dot(tails, wr[...])
    total = right_by_one(acc[:, :TAIL]) + acc[:, TAIL : 2 * TAIL] + left_by_one(acc[:, 2 * TAIL :])
    centre = pad[pl.ds(COLS, PX), pl.ds(HEAD, TAIL)].astype(F32)
    out[:, pl.ds(HEAD, TAIL)] = (centre + total).astype(BF)
    for b in range(CLIPS):
        columns = slice(b * WIDTH, (b + 1) * WIDTH)
        sides[b] = side(*[pad[pl.ds(COLS * i, PX), columns] for i in range(3)])


def conv_own(at, x, w, out0, out1, sides, x2, wn, wk, wr, pads):
    odd = at[0]
    for i in range(3):
        wn[i] = side(*[w[3 * i + j, pl.ds(0, HEAD), pl.ds(HEAD, TAIL)] for j in range(3)])
        for j in range(3):
            wk[j, pl.ds(TAIL * i, TAIL), :] = w[3 * i + j, pl.ds(HEAD, TAIL), pl.ds(0, HEAD)]
        wr[pl.ds(TAIL * i, TAIL), :] = side(
            *[w[3 * i + j, pl.ds(HEAD, TAIL), pl.ds(HEAD, TAIL)] for j in range(3)]
        )
    start = pl.multiple_of((TALL - 2 * COLS) * odd, COLS)
    for q, out in enumerate((out0, out1)):
        padded(pads.at[q], odd)[...] = x[odd + q * (1 - 2 * odd), pl.ds(start, TALL), :]
        convolve(pads.at[q], w, wn, wk, wr, out, sides.at[q])
    away = pl.multiple_of((TALL - 2 * COLS) * (1 - odd), COLS)
    fold(x[1 - odd, pl.ds(away, TALL), :], x2)


def prepare(at, cot, tw, c3, c2, cot0, cot1, vt, vtk, vb, vbk):
    odd = at[0]
    here, there = pl.multiple_of(PX * odd, PX), pl.multiple_of(PX * (1 - odd), PX)
    fold(cot[odd, pl.ds(there, PX), :], c3)
    fold(cot[1 - odd, pl.ds(there, PX), :], c2)
    cot0[...] = cot[odd, pl.ds(here, PX), :]
    cot1[...] = cot[1 - odd, pl.ds(here, PX), :]
    for l in range(2):
        for k in range(3):
            value = tw[l, tap(k, odd)]
            turned = value.T
            vt[l, k] = value
            vb[l, k] = turned
            vtk[l, pl.ds(TAIL * k, TAIL), :] = value[HEAD:, :]
            vbk[l, pl.ds(TAIL * k, TAIL), :] = turned[HEAD:, :]


def conv_other(at, x, w, wn, wk, wr, out, sides, pad):
    padded(pad, at[0])[...] = x[...]
    convolve(pad, w, wn, wk, wr, out, sides)


def conv_folded(at, x, w, wn, wk, wr, out, sides, pad):
    unfold(x, padded(pad, at[0]))
    convolve(pad, w, wn, wk, wr, out, sides)


def tap(k, odd):
    return k + odd * (2 - 2 * k)


def three_taps(three, vw, layer, wk):
    tails = side(*[ref[:, pl.ds(HEAD, TAIL)] for ref in three])
    totals = []
    for columns in (pl.ds(0, HEAD), pl.ds(HEAD, TAIL)):
        total = dot(three[0][:, pl.ds(0, HEAD)], vw[layer, 0, pl.ds(0, HEAD), columns])
        total = total + dot(three[1][:, pl.ds(0, HEAD)], vw[layer, 1, pl.ds(0, HEAD), columns])
        total = total + dot(three[2][:, pl.ds(0, HEAD)], vw[layer, 2, pl.ds(0, HEAD), columns])
        totals.append(total + dot(tails, wk[layer, :, columns]))
    return side(*totals)


def temporal(states, vw, layer, wk, acts):
    done = 0
    for q in range(4):
        while done < q + 3:
            v = states[done][...].astype(F32)
            acts[done] = (v * (0.5 + 0.5 * jnp.tanh(0.5 * v))).astype(BF)
            done += 1
        term = three_taps([acts.at[q + k] for k in range(3)], vw, layer, wk)
        yield (states[q + 1][...].astype(F32) + term).astype(BF)


def layer_one(at, left, s0, s1, s2, s3, right, vw, wk, acts, state, last, first):
    states = (left, s0, s1, s2, s3, right)
    for q, value in enumerate(temporal(states, vw, 0, wk, acts)):
        state[q] = value
        if q == 0:
            first[...] = value
        if q == 3:
            last[...] = value


def layer_two(at, left, state, right, vw, wk, acts, own, sent):
    states = (left, state.at[0], state.at[1], state.at[2], state.at[3], right)
    for q, value in enumerate(temporal(states, vw, 1, wk, acts)):
        if q < 2:
            own[q] = value
        else:
            fold(value, part(sent, 3 - q))


def descend(six, q, before, vw, layer, wk):
    three = [six[q + 2 - k] for k in range(3)]
    carried = three_taps(three, vw, layer, wk)
    v = before[...].astype(F32)
    s = sigmoid(v)
    return (three[1][...].astype(F32) + carried * (s * (1.0 + v * (1.0 - s)))).astype(BF)


def back_one(at, folded, cot0, cot1, folded2, folded3, right, state, vw, wk, back, first, last, c2, c3, left):
    unfold(folded, left)
    unfold(folded2, c2)
    unfold(folded3, c3)
    six = (left, cot0, cot1, c2, c3, right)
    for q in range(4):
        value = descend(six, q, state.at[q], vw, 1, wk)
        back[q] = value
        if q == 0:
            first[...] = value
        if q == 3:
            last[...] = value


def temporal_grads(at, cot0, cot1, c2, c3, acts2, back, acts1, blocks, flip):
    odd = at[0]
    views = (cot0, cot1, c2, c3)
    for layer, acts in ((0, acts1), (1, acts2)):
        for q in range(4):
            up = back.at[q] if layer == 0 else views[q]
            flip[:, pl.ds(q * PX, PX)] = up[...].T
        tails = jnp.zeros((C, THREE_TAILS), F32)
        for q in range(4):
            ends = side(*[acts[q + tap(k, odd), :, pl.ds(HEAD, TAIL)] for k in range(3)])
            tails = tails + dot(flip[:, pl.ds(q * PX, PX)], ends)
        values = []
        for k in range(3):
            total = jnp.zeros((C, HEAD), F32)
            for q in range(4):
                heads = acts[q + tap(k, odd), :, pl.ds(0, HEAD)]
                total = total + dot(flip[:, pl.ds(q * PX, PX)], heads)
            values.append(side(total, tails[:, k * TAIL : (k + 1) * TAIL]).astype(BF))
        for b in range(CLIPS):
            blocks[b, layer] = side(*[v[:, b * WIDTH : (b + 1) * WIDTH] for v in values])


def back_zero(at, left, back, right, s0, s1, s2, s3, vw, wk, own_sides, sides2, sides3, passing, sent, flip):
    core = at[1]
    six = [left] + [back.at[q] for q in range(4)] + [right]
    column = lax.broadcasted_iota(jnp.int32, (1, PX), 1) % COLS
    for q, before in enumerate((s0, s1, s2, s3)):
        turned = descend(six, q, before, vw, 0, wk).T
        wide = turned.astype(F32)
        ahead = jnp.where(column == COLS - 1, 0.0, pltpu.roll(wide, PX - 1, 1))
        behind = jnp.where(column == 0, 0.0, pltpu.roll(wide, 1, 1))
        flip[q, pl.ds(0, C), :] = ahead.astype(BF)
        flip[q, pl.ds(C, C), :] = turned
        flip[q, pl.ds(2 * C, C), :] = behind.astype(BF)
    spatial_blocks(flip, (own_sides.at[0], own_sides.at[1], sides2, sides3), passing, sent, 1 - core)


def keep_blocks(at, flip, own_sides, sides2, sides3, passing, kept):
    spatial_blocks(flip, (own_sides.at[0], own_sides.at[1], sides2, sides3), passing, kept, at[1])


def spatial_blocks(flip, sides, passing, out, core):
    for half in range(2):
        b = 2 * half + core
        total = jnp.zeros((3 * C, 3 * WIDTH), F32)
        for q in range(4):
            total = total + dot(flip[q], sides[q][b])
        for j in range(3):
            out[half, j] = total[j * C : (j + 1) * C].astype(BF)
        for layer in range(2):
            out[half, 3 + layer] = passing[b, layer]


def pack(at, kept, got, out, wide, rows):
    halves, taps, channels, width = kept.shape
    owners = out.shape[0] // halves
    count = channels // owners
    rows[:, pl.ds(width, 2 * LANES - width)] = jnp.zeros((channels, 2 * LANES - width), F32)
    for h in range(halves):
        for t in range(taps):
            rows[:, pl.ds(0, width)] = kept[h, t].astype(F32) + got[h, t].astype(F32)
            for owner in range(owners):
                for n in range(2):
                    block = pl.ds(count * (2 * t + n), count)
                    wide[owner, block, :] = rows[pl.ds(count * owner, count), pl.ds(n * LANES, LANES)]
        for owner in range(owners):
            out[owners * h + owner] = wide[owner].astype(BF)


def finish(at, parts, spatial, temporal):
    total = parts[0].astype(F32)
    for n in range(1, parts.shape[0]):
        total = total + parts[n].astype(F32)
    count = spatial.shape[0]
    for t in range(5):
        low = total[2 * t * count : (2 * t + 1) * count]
        high = total[(2 * t + 1) * count : (2 * t + 2) * count]
        row = side(low, high[:, : 3 * WIDTH - LANES])
        for i in range(3):
            piece = row[:, i * WIDTH : (i + 1) * WIDTH]
            for r in range(count):
                if t < 3:
                    spatial[r, i, pl.ds(t, 1), :] = piece[r : r + 1]
                else:
                    temporal[r, i, pl.ds(t - 3, 1), :] = piece[r : r + 1]


def place(at, own, got, out, vgot, sems):
    odd = at[0]
    move = Mover(sems)
    here, there = pl.multiple_of(PX * odd, PX), pl.multiple_of(PX * (1 - odd), PX)
    for q, frame in enumerate((odd, 1 - odd)):
        move.put(own.at[q], out.at[frame, pl.ds(here, PX), :])
        unfold(part(got, q), vgot.at[q])
        move.put(vgot.at[q], out.at[frame, pl.ds(there, PX), :])
    move.finish()


def after(value, *others):
    return lax.optimization_barrier((value, *others))[0]


def step(clips_in, cotangent, spatial_weight, temporal_weight):
    owners, clips = lax.axis_size("frame"), lax.axis_size("clip")
    odd = lax.axis_index("frame") % 2
    core = lax.axis_index("clip") % 2
    at = jnp.stack([odd, core]).astype(jnp.int32)
    swap = [(n, n ^ 1) for n in range(owners)]
    outer = [(n, n - 2 if n % 2 == 0 else n + 2) for n in range(owners)]
    outer = [(a, b) for a, b in outer if 0 <= b < owners]
    inner = [(n, n + 2 if n % 2 == 0 else n - 2) for n in range(owners)]
    inner = [(a, b) for a, b in inner if 0 <= b < owners]
    cores = [(n, n ^ 1) for n in range(clips)]

    def send(value, perm, axis="frame"):
        shape = value.shape
        if axis == "frame" and shape[-1] == C:
            value = value.reshape(-1, COLS, C)
        return lax.ppermute(value, axis, perm).reshape(shape)

    x = clips_in.reshape(2, FULL, C)
    cot = cotangent.reshape(2, FULL, C)
    ws = spatial_weight.reshape(9, C, C)
    flops = 2 * PX * C * C

    two, four, six = (2, PX, C), (4, PX, C), (6, PX, C)
    packed = [(3, HEAD, THREE_TAILS), (3, THREE_TAILS, HEAD), (THREE_TAILS, THREE_TAILS)]
    taps = [(2, *KERNELS), (2, THREE_TAILS, C)]
    pad = (PX + 2 * COLS, C)

    tall_start = (TALL - 2 * COLS) * (1 - odd)
    x3 = send(lax.dynamic_slice(x, (odd, tall_start, 0), (1, TALL, C))[0], swap)
    s0, s1, own_sides, x2, wn, wk, wr = run(
        conv_own,
        [ONE, ONE, (2, *SIDES), (TALL * C // LANES, LANES), *packed],
        (at, x, ws),
        [(2, *pad)],
        flops=8 * flops,
    )
    wp = (ws, wn, wk, wr)
    right = send(s0, outer)
    x2 = send(x2, swap)
    s3, sides3 = run(conv_other, [ONE, SIDES], (at, x3, *wp), [pad], 0, 4 * flops)
    left = send(s3, inner)
    c3, c2, cot0, cot1, vt, vtk, vb, vbk = run(
        prepare, [(PX * C // LANES, LANES)] * 2 + [ONE] * 2 + taps * 2, (at, after(cot, s3), after(temporal_weight, s3)), flops=flops
    )
    c3 = send(after(c3, x2), swap)
    s2, sides2 = run(conv_folded, [ONE, SIDES], (at, x2, *wp), [pad], 0, 4 * flops)
    c2 = send(after(c2, c3), swap)
    cot_right = send(after(cot0, s3), outer)
    cot_left = send(c3, inner)

    acts1, state1, last, first = run(
        layer_one,
        [six, four, ONE, ONE],
        (at, left, s0, s1, s2, s3, right, vt, vtk),
        flops=8 * flops,
    )
    left1 = send(last, inner)
    right1 = send(first, outer)
    back1, first, last, u2, u3 = run(
        back_one,
        [four, ONE, ONE, ONE, ONE],
        (at, cot_left, cot0, cot1, c2, c3, cot_right, state1, vb, vbk),
        [ONE],
        flops=8 * flops,
    )
    back_left = send(last, inner)
    back_right = send(first, outer)
    acts2, own, sent = run(
        layer_two, [six, two, (2 * FOLDED, LANES)], (at, left1, state1, right1, vt, vtk), flops=8 * flops
    )
    returned = send(sent, swap)

    (temporal_blocks,) = run(
        temporal_grads,
        [(CLIPS, 2, C, 3 * WIDTH)],
        (at, cot0, cot1, u2, u3, acts2, back1, acts1),
        [(C, 4 * PX)],
        flops=16 * flops,
    )
    shares = (2, 5, C, 3 * WIDTH)
    sent, flip = run(
        back_zero,
        [shares, (4, 3 * C, PX)],
        (at, back_left, back1, back_right, s0, s1, s2, s3, vb, vbk, own_sides, sides2, sides3, temporal_blocks),
        flops=20 * flops,
    )
    (kept,) = run(
        keep_blocks, [shares], (at, flip, own_sides, sides2, sides3, temporal_blocks), flops=12 * flops
    )
    got = send(sent, cores, "clip")
    (out,) = run(place, [(2, FULL, C)], (at, own, returned), [two], 4, 1000, far_outs=True)

    rows = C // owners
    block = (2 * owners, 10 * rows, LANES)
    (packs,) = run(
        pack,
        [block],
        (at, kept, got),
        [pltpu.VMEM((owners, 10 * rows, LANES), F32), pltpu.VMEM((C, 2 * LANES), F32)],
        flops=1000,
    )
    groups = [[n + half * 2 + c for half in range(2) for n in range(0, owners * clips, clips)] for c in range(2)]
    parts = lax.all_to_all(packs, ("frame", "clip"), split_axis=0, concat_axis=0, axis_index_groups=groups, tiled=True)
    grad_spatial, grad_temporal = run(
        finish, [(rows, 3, 3, WIDTH), (rows, 3, 2, WIDTH)], (at, parts), flops=1000, kind=F32
    )
    grad_temporal = grad_temporal.transpose(0, 2, 1, 3)
    return (out.reshape(clips_in.shape), grad_spatial, grad_temporal)


def solution(mesh):
    placed = (P("clip", "frame", None, None, None), P("clip", "frame", None, None, None), P(), P())
    return jax.shard_map(
        step,
        mesh=mesh,
        in_specs=placed,
        out_specs=(
            P("clip", "frame", None, None, None),
            P("frame", None, None, "clip"),
            P("frame", None, None, "clip"),
        ),
        check_vma=False,
    )
```
